128 devices in a mesh: belt: 16 (over x, z_lo, core), lon: 8 (over z_hi, y).
Axes of the slice: x: 4, y: 4, z: 4 (z_hi: 2, z_lo: 2; z = z_hi * 2 + z_lo), core: 2. Of those that a mesh axis runs over, the one named last changes fastest.
Arguments:
- grid_fields: bfloat16 [32, 2048, 4096], P(None, 'belt', 'lon'), may hold values from -6 to 6
- field_order: int32 [32], replicated, may hold values from 0 to 31, each once
- wave_order: int32 [1024], replicated, may hold values from 0 to 1023, as said below
Outputs:
- spectral: float32 [1024, 2, 32, 2, 512], P(('belt', 'lon'))
The draws below stay inside these ranges and needn't reach their ends.
Inputs may be any that keep to these rules, and one draw needn't show every extreme that they name: wave_order is a permutation of the wavenumbers; each aligned block of 8 entries holds 4 wavenumbers m followed, in the same order, by their partners 1024 - 1 - m. field_order is a permutation.
All inputs are finite; a program needn't handle non-finite values.
Results may differ from the reference program's by a relative error of at most 0.0023.
Values may be sent and summed in bfloat16 or wider, within the bound.
A program may use at most 128 MiB of HBM per device.

```python
import math
import jax
import jax.numpy as jnp
from jax import lax

NLAT = 2048
NLON = 4096
NT = 1024
FL = 32
PAIRS_DEV = 4
SLOTS_DEV = 8


def draw_wave_order(key, part):
    pairs = jax.random.permutation(key, NT // 2).astype(jnp.int32).reshape(-1, PAIRS_DEV)
    return jnp.concatenate([pairs, NT - 1 - pairs], axis=1).reshape(-1)


def levels(own_key, extent, split, low, largest):
    gain = 1.0
    for axis_at, parts in split:
        draws = jax.random.uniform(jax.random.fold_in(jax.random.fold_in(own_key, 6), axis_at), (parts,), jnp.float32, low / len(split), largest / len(split))
        gain = gain * jnp.repeat(jnp.exp(draws), extent[axis_at] // parts).reshape((-1,) + (1,) * (len(extent) - 1 - axis_at))
    return gain


def bell_draw(own_key, dims, width, reach, split=(), kind=jnp.bfloat16):
    level = levels(own_key, dims, split, -0.22, 0.18) if split else 1.0
    values = jax.random.normal(own_key, dims, jnp.float32) * width * level
    return jnp.minimum(jnp.maximum(values, -reach), reach).astype(kind)


def setup_inputs(seed: int = 0) -> dict:
    seeds = jax.random.split(jax.random.key(seed), 4)
    return {
        "grid_fields": bell_draw(seeds[0], (FL, NLAT, NLON), 1.0, 6.0, ((1, 16), (2, 8))),
        "field_order": jax.random.permutation(seeds[1], FL).astype(jnp.int32),
        "wave_order": draw_wave_order(jax.random.fold_in(seeds[3], 71), 0),
    }


def angle_table(wavenumbers, lon_count):
    lon_index = jnp.arange(lon_count, dtype=jnp.int32)
    phase_step = lon_index[:, None] * wavenumbers[None, :] % lon_count
    angles = phase_step.astype(jnp.float32) * (2.0 * math.pi / lon_count)
    return (jnp.cos(angles).astype(jnp.bfloat16), jnp.sin(angles).astype(jnp.bfloat16))

def latitude_geometry(lat_count):
    lat_index = jnp.arange(lat_count // 2).astype(jnp.float32)
    colatitude = math.pi * (lat_index + 0.75) / (lat_count + 0.5)
    sine_lat = jnp.sin(colatitude)
    weight = math.pi / (lat_count + 0.5) * sine_lat * math.sqrt(lat_count / 2.0)
    return (jnp.cos(colatitude), sine_lat, weight)

def initial_state(wave_value, sine_lat, mode_count):
    term_index = jnp.arange(1, mode_count + 1).astype(jnp.float32)
    log_terms = jnp.log1p(0.5 / term_index)
    start_sum = lax.optimization_barrier(jnp.sum(jnp.where(term_index[None, :] <= wave_value, log_terms[None, :], 0.0), axis=1, keepdims=True))
    log_scale = -0.5 * math.log(2.0) + 0.5 * start_sum + wave_value * jnp.log(sine_lat)[None, :]
    return (jnp.zeros_like(log_scale), jnp.ones_like(log_scale), log_scale)

def advance(previous, current, log_scale, wave_value, degree, cosine):
    factor = jnp.sqrt((4.0 * degree * degree - 1.0) / (degree * degree - wave_value * wave_value))
    before = degree - 1.0
    factor_prev = jnp.sqrt(jnp.maximum(4.0 * before * before - 1.0, 1.0) / jnp.maximum(before * before - wave_value * wave_value, 1.0))
    following = factor * (cosine[None, :] * current - previous / factor_prev)
    row_total = jnp.abs(following) + jnp.abs(current)
    return (current / row_total, following / row_total, log_scale + jnp.log(row_total))

def emit_row(current, log_scale, wave_value, row_value, weight, mode_count):
    return jnp.where(wave_value + row_value < mode_count, jnp.exp(log_scale) * current, 0.0) * weight[None, :]

def legendre_rows(wavenumbers):
    wave_value = wavenumbers.astype(jnp.float32)[:, None]
    cosine, sine_lat, weight = latitude_geometry(NLAT)
    initial = initial_state(wave_value, sine_lat, NT)

    def scan_step(carried, pair_index):
        previous, current, log_scale = carried
        row_value = (2 * pair_index).astype(jnp.float32)
        even_row = emit_row(current, log_scale, wave_value, row_value, weight, NT)
        previous, current, log_scale = advance(previous, current, log_scale, wave_value, wave_value + row_value + 1.0, cosine)
        odd_row = emit_row(current, log_scale, wave_value, row_value + 1.0, weight, NT)
        previous, current, log_scale = advance(previous, current, log_scale, wave_value, wave_value + row_value + 2.0, cosine)
        return ((previous, current, log_scale), jnp.stack((even_row, odd_row), axis=0))
    final_state, row_values = lax.scan(scan_step, initial, jnp.arange(NT // 2, dtype=jnp.int32))
    return row_values

def project(legendre, samples):
    half_count = samples.shape[3] // 2
    north_half = samples[:, :, :, :half_count]
    south_half = jnp.flip(samples[:, :, :, half_count:], axis=3)
    even_sum = north_half + south_half
    odd_diff = north_half - south_half
    even_part = jnp.einsum('ksj,scfj->scfk', legendre[:, 0], even_sum, precision=lax.Precision.HIGHEST)
    odd_part = jnp.einsum('ksj,scfj->scfk', legendre[:, 1], odd_diff, precision=lax.Precision.HIGHEST)
    return jnp.stack((even_part, odd_part), axis=3)

def reference(grid_fields, field_order, wave_order):
    ordered = jnp.take(grid_fields, field_order, axis=0)
    mode_index = jnp.arange(NT, dtype=jnp.int32)
    cos_table, sin_table = angle_table(mode_index, NLON)
    cos_wide = cos_table.astype(jnp.float32)
    sin_wide = sin_table.astype(jnp.float32)
    dft_scale = 1.0 / math.sqrt(NLON)

    def one_field(lat_rows):
        widened = lat_rows.astype(jnp.float32)
        real_part = jnp.dot(widened, cos_wide, precision=lax.Precision.HIGHEST) * dft_scale
        imag_part = jnp.dot(widened, sin_wide, precision=lax.Precision.HIGHEST) * -dft_scale
        return (real_part, imag_part)
    real_all, imag_all = lax.map(one_field, ordered)
    groups = wave_order.reshape(-1, SLOTS_DEV)

    def one_group(wavenumbers):
        legendre = legendre_rows(wavenumbers)
        samples = jnp.stack((jnp.take(real_all, wavenumbers, axis=2), jnp.take(imag_all, wavenumbers, axis=2)), axis=0)
        samples = jnp.transpose(samples, (3, 0, 1, 2))
        return project(legendre, samples)
    spectral = lax.map(one_group, groups)
    return spectral.reshape(NT, 2, FL, 2, NT // 2)
```

```python
import functools
import math

import jax
import jax.numpy as jnp
from jax import lax
from jax.experimental import pallas as pl
from jax.experimental.pallas import tpu as pltpu
from jax.sharding import PartitionSpec as P

LANES = 128
LINK_DTYPE = jnp.bfloat16
NT_DIMS = (((1,), (1,)), ((), ()))


def split(value):
    high = value.astype(jnp.bfloat16)
    return high, (value - high.astype(jnp.float32)).astype(jnp.bfloat16)


def angle_factors(wavenumbers, lon_count):
    coarse = jnp.arange(lon_count // LANES, dtype=jnp.int32) * LANES
    fine = jnp.arange(LANES, dtype=jnp.int32)
    steps = jnp.concatenate((coarse, fine))
    phase = wavenumbers[:, None] * steps[None, :] % lon_count
    angles = phase.astype(jnp.float32) * (2.0 * math.pi / lon_count)
    return jnp.cos(angles), jnp.sin(angles)


def dft_table(wave_order, lon_count, slot_count):
    cosine, sine = angle_factors(wave_order, lon_count)
    coarse_count = lon_count // LANES
    pad = -coarse_count % LANES
    if pad:
        fill = ((0, 0), (0, pad))
        cosine = jnp.concatenate(
            (jnp.pad(cosine[:, :coarse_count], fill), cosine[:, coarse_count:]), axis=1
        )
        sine = jnp.concatenate(
            (jnp.pad(sine[:, :coarse_count], fill), sine[:, coarse_count:]), axis=1
        )
    owners = wave_order.shape[0] // slot_count
    width = cosine.shape[1]
    cosine = cosine.reshape(owners, slot_count, width)
    sine = sine.reshape(owners, slot_count, width)
    step = 8

    def body(cos_ref, sin_ref, out_ref):
        @pl.loop(0, step)
        def _(owner):
            cos_all = cos_ref[owner]
            sin_all = sin_ref[owner]
            cos_fine = cos_all[:, width - LANES :]
            sin_fine = sin_all[:, width - LANES :]
            row = pl.multiple_of(owner * 16, 16)
            for a in range(coarse_count):
                ca = cos_all[:, a : a + 1]
                sa = sin_all[:, a : a + 1]
                cosine_rows = ca * cos_fine - sa * sin_fine
                sine_rows = sa * cos_fine + ca * sin_fine
                out_ref[pl.ds(row, 16), a * LANES : (a + 1) * LANES] = jnp.concatenate(
                    (cosine_rows, -sine_rows), axis=0
                ).astype(jnp.bfloat16)

    return pl.pallas_call(
        body,
        name="dft_table",
        grid=(owners // step,),
        in_specs=[pl.BlockSpec((step, slot_count, width), lambda i: (i, 0, 0))] * 2,
        out_specs=pl.BlockSpec((step * 16, lon_count), lambda i: (i, 0)),
        out_shape=jax.ShapeDtypeStruct((owners * 16, lon_count), jnp.bfloat16),
        cost_estimate=pl.CostEstimate(
            flops=owners * 16 * lon_count * 4, bytes_accessed=owners * 32 * lon_count, transcendentals=0
        ),
    )(cosine, sine)


def dft(table, samples, scale):
    parts, rows, length = samples.shape
    table_rows = table.shape[0]
    step = 512

    def body(table_ref, samples_ref, out_ref):
        total = None
        for part in range(parts):
            term = lax.dot_general(
                table_ref[:, part * length : (part + 1) * length],
                samples_ref[part],
                NT_DIMS,
                preferred_element_type=jnp.float32,
            )
            total = term if total is None else total + term
        out_ref[...] = (total * scale).astype(out_ref.dtype)

    return pl.pallas_call(
        body,
        name="dft",
        grid=(table_rows // step,),
        in_specs=[
            pl.BlockSpec((step, parts * length), lambda i: (i, 0)),
            pl.BlockSpec((parts, rows, length), lambda i: (0, 0, 0)),
        ],
        out_specs=pl.BlockSpec((step, rows), lambda i: (i, 0)),
        out_shape=jax.ShapeDtypeStruct((table_rows, rows), LINK_DTYPE),
        compiler_params=pltpu.CompilerParams(vmem_limit_bytes=48 << 20),
        cost_estimate=pl.CostEstimate(
            flops=2 * table_rows * rows * parts * length,
            bytes_accessed=2 * table_rows * parts * length,
            transcendentals=0,
        ),
    )(table, samples)


def latitude_geometry(lat_count):
    lat_index = jnp.arange(lat_count // 2).astype(jnp.float32)
    colatitude = math.pi * (lat_index + 0.75) / (lat_count + 0.5)
    sine_lat = jnp.sin(colatitude)
    weight = math.pi / (lat_count + 0.5) * sine_lat * math.sqrt(lat_count / 2.0)
    return (jnp.cos(colatitude), sine_lat, weight)


def legendre(wavenumbers, mode_count, lat_count):
    slots = wavenumbers.shape[0]
    half = lat_count // 2
    chunks = half // LANES
    wave_value = wavenumbers.astype(jnp.float32)[:, None]
    cosine, sine_lat, weight = latitude_geometry(lat_count)
    term_index = jnp.arange(1, mode_count + 1).astype(jnp.float32)
    log_terms = jnp.log1p(0.5 / term_index)
    start_sum = jnp.sum(
        jnp.where(term_index[None, :] <= wave_value, log_terms[None, :], 0.0), axis=1, keepdims=True
    )
    log_start = -0.5 * math.log(2.0) + 0.5 * start_sum + wave_value * jnp.log(sine_lat)[None, :]
    geometry = jnp.stack((cosine, weight))[:, None, :] * jnp.ones((2, slots, 1), jnp.float32)
    wave_lanes = jnp.broadcast_to(wave_value, (slots, LANES))
    block = 32
    renorm = 16

    def body(wave_ref, log_ref, geo_ref, out_ref, prev_ref, cur_ref, scale_ref, inv_ref, rows_ref):
        step = pl.program_id(0)

        @pl.when(step == 0)
        def _():
            prev_ref[...] = jnp.zeros_like(prev_ref)
            cur_ref[...] = jnp.ones_like(cur_ref)
            scale_ref[...] = log_ref[...]
            inv_ref[...] = jnp.zeros_like(inv_ref)

        wave = wave_ref[...]
        first = (step * block).astype(jnp.float32)
        lanes = [slice(a * LANES, (a + 1) * LANES) for a in range(chunks)]
        inverse = inv_ref[...]
        prev = [prev_ref[:, s] for s in lanes]
        cur = [cur_ref[:, s] for s in lanes]
        amp = [None] * chunks
        for row in range(block):
            if row % renorm == 0:
                for a in range(chunks):
                    total = jnp.maximum(jnp.abs(prev[a]) + jnp.abs(cur[a]), 1e-30)
                    prev[a] = prev[a] / total
                    cur[a] = cur[a] / total
                    log_scale = scale_ref[:, lanes[a]] + jnp.log(total)
                    scale_ref[:, lanes[a]] = log_scale
                    amp[a] = jnp.exp(log_scale) * geo_ref[1, :, lanes[a]]
            for a in range(chunks):
                rows_ref[a, row * slots : (row + 1) * slots, :] = cur[a] * amp[a]
            offset = first + (row + 1.0)
            degree = wave + offset
            numer = 4.0 * degree * degree - 1.0
            denom = offset * (wave + degree)
            root = lax.rsqrt(numer * denom)
            keep = degree < mode_count
            factor = jnp.where(keep, numer * root, 0.0)
            ratio = factor * inverse
            inverse = denom * root
            for a in range(chunks):
                following = (factor * geo_ref[0, :, lanes[a]]) * cur[a] - ratio * prev[a]
                prev[a] = cur[a]
                cur[a] = following
        inv_ref[...] = inverse
        for a in range(chunks):
            prev_ref[:, lanes[a]] = prev[a]
            cur_ref[:, lanes[a]] = cur[a]
        for slot in range(slots):
            for parity in range(2):
                for a in range(chunks):
                    value = rows_ref[a, pl.ds(parity * slots + slot, block // 2, stride=2 * slots), :]
                    high, low = split(value)
                    out_ref[slot, parity, 0, :, lanes[a]] = high
                    out_ref[slot, parity, 1, :, lanes[a]] = low

    return pl.pallas_call(
        body,
        name="legendre",
        grid=(mode_count // block,),
        in_specs=[
            pl.BlockSpec((slots, LANES), lambda i: (0, 0)),
            pl.BlockSpec((slots, half), lambda i: (0, 0)),
            pl.BlockSpec((2, slots, half), lambda i: (0, 0, 0)),
        ],
        out_specs=pl.BlockSpec((slots, 2, 2, block // 2, half), lambda i: (0, 0, 0, i, 0)),
        out_shape=jax.ShapeDtypeStruct((slots, 2, 2, mode_count // 2, half), jnp.bfloat16),
        scratch_shapes=[
            pltpu.VMEM((slots, half), jnp.float32),
            pltpu.VMEM((slots, half), jnp.float32),
            pltpu.VMEM((slots, half), jnp.float32),
            pltpu.VMEM((slots, LANES), jnp.float32),
            pltpu.VMEM((chunks, block * slots, LANES), jnp.float32),
        ],
        cost_estimate=pl.CostEstimate(
            flops=slots * half * mode_count * 10,
            bytes_accessed=slots * half * mode_count * 4,
            transcendentals=0,
        ),
    )(wave_lanes, log_start, geometry)


def project(received, legendre_table, field_order, belts, lons):
    slots, _, _, half_modes, half = legendre_table.shape
    sources = belts * lons
    lat_local = 2 * half // belts
    items = received.shape[2] // lat_local
    levels = items * lons
    rows = 2 * levels
    level_of = field_order.astype(jnp.int32)
    target = jnp.arange(2 * rows, dtype=jnp.int32)
    within = target % rows
    source_level = jnp.take(level_of, within % levels)
    source_row = (source_level % items) * (2 * lons) + (source_level // items) * 2 + within // levels
    source_row = source_row + (target // rows) * rows
    order = (source_row[:, None] == jnp.arange(2 * rows, dtype=jnp.int32)[None, :]).astype(jnp.bfloat16)
    mirror = (
        jnp.arange(lat_local)[:, None] + jnp.arange(lat_local)[None, :] == lat_local - 1
    ).astype(jnp.bfloat16)

    def body(received_ref, table_ref, order_ref, mirror_ref, out_ref, wide_ref, sums_ref):
        slot = pl.program_id(0)
        parity = pl.program_id(1)

        @pl.when((slot == 0) & (parity == 0))
        def _():
            @pl.loop(0, belts)
            def _(belt):
                for lon in range(lons):
                    value = received_ref[belt * lons + lon].astype(jnp.float32)
                    for item in range(items):
                        wide_ref[belt, item, lon * 2 * slots : (lon + 1) * 2 * slots, :] = value[
                            :, item * lat_local : (item + 1) * lat_local
                        ]

        @pl.when(parity == 0)
        def _():
            def rows_of(belt):
                return jnp.concatenate(
                    [wide_ref[belt, item, pl.ds(slot, 2 * lons, stride=slots), :] for item in range(items)],
                    axis=0,
                )

            for belt in range(belts // 2):
                north = rows_of(belt)
                south = jnp.dot(
                    rows_of(belts - 1 - belt).astype(LINK_DTYPE),
                    mirror_ref[...],
                    preferred_element_type=jnp.float32,
                )
                for index, value in enumerate((north + south, north - south)):
                    ordered = jnp.dot(
                        order_ref[...],
                        jnp.concatenate(split(value), axis=0),
                        preferred_element_type=jnp.float32,
                    )
                    sums_ref[index, :, belt * lat_local : (belt + 1) * lat_local] = ordered.astype(jnp.bfloat16)

        result = lax.dot_general(
            sums_ref[parity], table_ref[0, 0, 0], NT_DIMS, preferred_element_type=jnp.float32
        ) + lax.dot_general(
            sums_ref[parity], table_ref[0, 0, 1], NT_DIMS, preferred_element_type=jnp.float32
        )
        out_ref[0] = result[:rows] + result[rows:]

    return pl.pallas_call(
        body,
        name="project",
        grid=(slots, 2),
        in_specs=[
            pl.BlockSpec(received.shape, lambda s, p: (0, 0, 0)),
            pl.BlockSpec((1, 1, 2, half_modes, half), lambda s, p: (s, p, 0, 0, 0)),
            pl.BlockSpec((2 * rows, 2 * rows), lambda s, p: (0, 0)),
            pl.BlockSpec((lat_local, lat_local), lambda s, p: (0, 0)),
        ],
        out_specs=pl.BlockSpec((1, rows, half_modes), lambda s, p: (s, 0, p)),
        out_shape=jax.ShapeDtypeStruct((slots, rows, 2 * half_modes), jnp.float32),
        scratch_shapes=[
            pltpu.VMEM((belts, items, 2 * lons * slots, lat_local), jnp.float32),
            pltpu.VMEM((2, 2 * rows, half), jnp.bfloat16),
        ],
        compiler_params=pltpu.CompilerParams(vmem_limit_bytes=40 << 20),
    )(received, legendre_table, order, mirror)


def on_device(grid_fields, field_order, wave_order):
    belts = lax.axis_size("belt")
    lons = lax.axis_size("lon")
    levels, lat_local, lon_local = grid_fields.shape
    lat_count = lat_local * belts
    lon_count = lon_local * lons
    mode_count = wave_order.shape[0]
    slots = mode_count // (belts * lons)
    items = levels // lons
    blocks = grid_fields.reshape(lons, items * lat_local, lon_local)
    gathered = lax.all_to_all(blocks, "lon", split_axis=0, concat_axis=0, tiled=True)
    table = dft_table(wave_order, lon_count, slots)
    owner = lax.axis_index("belt") * lons + lax.axis_index("lon")
    own_waves = lax.dynamic_slice_in_dim(wave_order, owner * slots, slots, 0)
    legendre_table = legendre(own_waves, mode_count, lat_count)
    fourier = dft(table, gathered, 1.0 / math.sqrt(lon_count))
    fourier = fourier.reshape(belts * lons, 2 * slots, items * lat_local)
    received = lax.all_to_all(fourier, ("belt", "lon"), split_axis=0, concat_axis=0, tiled=True)
    spectral = project(received, legendre_table, field_order, belts, lons)
    return spectral.reshape(slots, 2, levels, 2, mode_count // 2)


def solution(mesh):
    return jax.shard_map(
        on_device,
        mesh=mesh,
        in_specs=(P(None, "belt", "lon"), P(), P()),
        out_specs=P(("belt", "lon"), None, None, None, None),
        check_vma=False,
    )
```

```python
import functools
import math

import jax
import jax.numpy as jnp
from jax import lax
from jax.experimental import pallas as pl
from jax.experimental.pallas import tpu as pltpu
from jax.sharding import PartitionSpec as P

LANES = 128
LINK_DTYPE = jnp.bfloat16
NT_DIMS = (((1,), (1,)), ((), ()))


def split(value):
    high = value.astype(jnp.bfloat16)
    return high, (value - high.astype(jnp.float32)).astype(jnp.bfloat16)


def angle_factors(wavenumbers, lon_count):
    coarse = jnp.arange(lon_count // LANES, dtype=jnp.int32) * LANES
    fine = jnp.arange(LANES, dtype=jnp.int32)
    steps = jnp.concatenate((coarse, fine))
    phase = wavenumbers[:, None] * steps[None, :] % lon_count
    angles = phase.astype(jnp.float32) * (2.0 * math.pi / lon_count)
    return jnp.cos(angles), jnp.sin(angles)


def dft_table(wave_order, lon_count, slot_count):
    cosine, sine = angle_factors(wave_order, lon_count)
    coarse_count = lon_count // LANES
    pad = -coarse_count % LANES
    if pad:
        fill = ((0, 0), (0, pad))
        cosine = jnp.concatenate(
            (jnp.pad(cosine[:, :coarse_count], fill), cosine[:, coarse_count:]), axis=1
        )
        sine = jnp.concatenate(
            (jnp.pad(sine[:, :coarse_count], fill), sine[:, coarse_count:]), axis=1
        )
    owners = wave_order.shape[0] // slot_count
    width = cosine.shape[1]
    cosine = cosine.reshape(owners, slot_count, width)
    sine = sine.reshape(owners, slot_count, width)
    step = 8

    def body(cos_ref, sin_ref, out_ref):
        @pl.loop(0, step)
        def _(owner):
            cos_all = cos_ref[owner]
            sin_all = sin_ref[owner]
            cos_fine = cos_all[:, width - LANES :]
            sin_fine = sin_all[:, width - LANES :]
            row = pl.multiple_of(owner * 16, 16)
            for a in range(coarse_count):
                ca = cos_all[:, a : a + 1]
                sa = sin_all[:, a : a + 1]
                cosine_rows = ca * cos_fine - sa * sin_fine
                sine_rows = sa * cos_fine + ca * sin_fine
                out_ref[pl.ds(row, 16), a * LANES : (a + 1) * LANES] = jnp.concatenate(
                    (cosine_rows, -sine_rows), axis=0
                ).astype(jnp.bfloat16)

    return pl.pallas_call(
        body,
        name="dft_table",
        grid=(owners // step,),
        in_specs=[pl.BlockSpec((step, slot_count, width), lambda i: (i, 0, 0))] * 2,
        out_specs=pl.BlockSpec((step * 16, lon_count), lambda i: (i, 0)),
        out_shape=jax.ShapeDtypeStruct((owners * 16, lon_count), jnp.bfloat16),
        cost_estimate=pl.CostEstimate(
            flops=owners * 16 * lon_count * 4, bytes_accessed=owners * 32 * lon_count, transcendentals=0
        ),
    )(cosine, sine)


def transform_and_exchange(table, samples, scale):
    belts = lax.axis_size("belt")
    lons = lax.axis_size("lon")
    parts, rows, length = samples.shape
    owners = belts * lons
    group = 2 * lons
    blocks = owners // group
    owner_rows = table.shape[0] // owners
    block_rows = group * owner_rows
    mesh_id = pl.DeviceIdType.MESH

    def body(table_ref, samples_ref, out_ref, stage_ref, send_ref, stage_sem, send_sem, recv_sem, local_sem):
        belt = lax.axis_index("belt")
        lon = lax.axis_index("lon")
        me = belt * lons + lon
        barrier = pltpu.get_barrier_semaphore()

        def place(step):
            away = blocks - 1 - step
            x = lax.rem(belt // 4 + away // 2, blocks // 2)
            return x * 2 + lax.rem(lax.rem(belt // 2, 2) + lax.rem(away, 2), 2)

        def member(index):
            away = lax.rem(index, lons)
            core = lax.rem(lax.rem(belt, 2) + index // lons, 2)
            half = lons // 2
            high = lax.rem(lon // half + away // half, 2)
            return core, high * half + lax.rem(lax.rem(lon, half) + lax.rem(away, half), half)

        def fetch(step, slot):
            return pltpu.make_async_copy(
                table_ref.at[pl.ds(pl.multiple_of(place(step) * block_rows, block_rows), block_rows)],
                stage_ref.at[slot],
                stage_sem.at[slot],
            )

        def send(step, index):
            core, target = member(index)
            return pltpu.make_async_remote_copy(
                send_ref.at[step, core * lons + target],
                out_ref.at[me],
                send_sem,
                recv_sem,
                device_id=(place(step) * 2 + core, target),
                device_id_type=mesh_id,
            )

        fetch(0, 0).start()

        @pl.loop(1, owners)
        def _(away):
            peer = lax.rem(me + away, owners)
            pl.semaphore_signal(
                barrier, inc=1, device_id=(peer // lons, lax.rem(peer, lons)), device_id_type=mesh_id
            )

        @pl.loop(0, blocks)
        def _(step):
            slot = lax.rem(step, 2)
            fetch(step, slot).wait()

            @pl.when(step < blocks - 1)
            def _():
                fetch(step + 1, 1 - slot).start()

            total = None
            for part in range(parts):
                term = lax.dot_general(
                    stage_ref[slot, :, part * length : (part + 1) * length],
                    samples_ref[part],
                    NT_DIMS,
                    preferred_element_type=jnp.float32,
                )
                total = term if total is None else total + term
            send_ref[step] = (total * scale).astype(LINK_DTYPE).reshape(group, owner_rows, rows)

            @pl.when(step == 0)
            def _():
                pl.semaphore_wait(barrier, owners - 1)

            @pl.loop(0, group)
            def _(back):
                index = group - 1 - back

                @pl.when((step < blocks - 1) | (index > 0))
                def _():
                    send(step, index).start()

        core, target = member(0)
        local = pltpu.make_async_copy(
            send_ref.at[blocks - 1, core * lons + target], out_ref.at[me], local_sem
        )
        local.start()
        local.wait()
        everything = pltpu.make_async_remote_copy(
            out_ref.at[pl.ds(0, owners - 1)],
            out_ref.at[pl.ds(0, owners - 1)],
            send_sem,
            recv_sem,
            device_id=(lax.rem(belt + 1, belts), lon),
            device_id_type=mesh_id,
        )
        everything.wait_recv()
        everything.wait_send()

    return pl.pallas_call(
        body,
        name="transform_and_exchange",
        in_specs=[pl.BlockSpec(memory_space=pl.ANY), pl.BlockSpec(memory_space=pltpu.VMEM)],
        out_specs=pl.BlockSpec(memory_space=pl.ANY),
        out_shape=jax.ShapeDtypeStruct((owners, owner_rows, rows), LINK_DTYPE),
        scratch_shapes=[
            pltpu.VMEM((2, block_rows, parts * length), jnp.bfloat16),
            pltpu.VMEM((blocks, group, owner_rows, rows), LINK_DTYPE),
            pltpu.SemaphoreType.DMA((2,)),
            pltpu.SemaphoreType.DMA,
            pltpu.SemaphoreType.DMA,
            pltpu.SemaphoreType.DMA,
        ],
        compiler_params=pltpu.CompilerParams(
            collective_id=0, has_side_effects=True, vmem_limit_bytes=40 << 20
        ),
    )(table, samples)


def latitude_geometry(lat_count):
    lat_index = jnp.arange(lat_count // 2).astype(jnp.float32)
    colatitude = math.pi * (lat_index + 0.75) / (lat_count + 0.5)
    sine_lat = jnp.sin(colatitude)
    weight = math.pi / (lat_count + 0.5) * sine_lat * math.sqrt(lat_count / 2.0)
    return (jnp.cos(colatitude), sine_lat, weight)


def legendre(wavenumbers, mode_count, lat_count):
    slots = wavenumbers.shape[0]
    half = lat_count // 2
    chunks = half // LANES
    wave_value = wavenumbers.astype(jnp.float32)[:, None]
    cosine, sine_lat, weight = latitude_geometry(lat_count)
    term_index = jnp.arange(1, mode_count + 1).astype(jnp.float32)
    log_terms = jnp.log1p(0.5 / term_index)
    start_sum = jnp.sum(
        jnp.where(term_index[None, :] <= wave_value, log_terms[None, :], 0.0), axis=1, keepdims=True
    )
    log_start = -0.5 * math.log(2.0) + 0.5 * start_sum + wave_value * jnp.log(sine_lat)[None, :]
    geometry = jnp.stack((cosine, weight))[:, None, :] * jnp.ones((2, slots, 1), jnp.float32)
    wave_lanes = jnp.broadcast_to(wave_value, (slots, LANES))
    block = 32
    renorm = 16

    def body(wave_ref, log_ref, geo_ref, out_ref, prev_ref, cur_ref, scale_ref, inv_ref, rows_ref):
        step = pl.program_id(0)

        @pl.when(step == 0)
        def _():
            prev_ref[...] = jnp.zeros_like(prev_ref)
            cur_ref[...] = jnp.ones_like(cur_ref)
            scale_ref[...] = log_ref[...]
            inv_ref[...] = jnp.zeros_like(inv_ref)

        wave = wave_ref[...]
        first = (step * block).astype(jnp.float32)
        lanes = [slice(a * LANES, (a + 1) * LANES) for a in range(chunks)]
        inverse = inv_ref[...]
        prev = [prev_ref[:, s] for s in lanes]
        cur = [cur_ref[:, s] for s in lanes]
        amp = [None] * chunks
        for row in range(block):
            if row % renorm == 0:
                for a in range(chunks):
                    total = jnp.maximum(jnp.abs(prev[a]) + jnp.abs(cur[a]), 1e-30)
                    prev[a] = prev[a] / total
                    cur[a] = cur[a] / total
                    log_scale = scale_ref[:, lanes[a]] + jnp.log(total)
                    scale_ref[:, lanes[a]] = log_scale
                    amp[a] = jnp.exp(log_scale) * geo_ref[1, :, lanes[a]]
            for a in range(chunks):
                rows_ref[a, row * slots : (row + 1) * slots, :] = cur[a] * amp[a]
            offset = first + (row + 1.0)
            degree = wave + offset
            numer = 4.0 * degree * degree - 1.0
            denom = offset * (wave + degree)
            root = lax.rsqrt(numer * denom)
            keep = degree < mode_count
            factor = jnp.where(keep, numer * root, 0.0)
            ratio = factor * inverse
            inverse = denom * root
            for a in range(chunks):
                following = (factor * geo_ref[0, :, lanes[a]]) * cur[a] - ratio * prev[a]
                prev[a] = cur[a]
                cur[a] = following
        inv_ref[...] = inverse
        for a in range(chunks):
            prev_ref[:, lanes[a]] = prev[a]
            cur_ref[:, lanes[a]] = cur[a]
        for slot in range(slots):
            for parity in range(2):
                for a in range(chunks):
                    value = rows_ref[a, pl.ds(parity * slots + slot, block // 2, stride=2 * slots), :]
                    high, low = split(value)
                    out_ref[slot, parity, 0, :, lanes[a]] = high
                    out_ref[slot, parity, 1, :, lanes[a]] = low

    return pl.pallas_call(
        body,
        name="legendre",
        grid=(mode_count // block,),
        in_specs=[
            pl.BlockSpec((slots, LANES), lambda i: (0, 0)),
            pl.BlockSpec((slots, half), lambda i: (0, 0)),
            pl.BlockSpec((2, slots, half), lambda i: (0, 0, 0)),
        ],
        out_specs=pl.BlockSpec((slots, 2, 2, block // 2, half), lambda i: (0, 0, 0, i, 0)),
        out_shape=jax.ShapeDtypeStruct((slots, 2, 2, mode_count // 2, half), jnp.bfloat16),
        scratch_shapes=[
            pltpu.VMEM((slots, half), jnp.float32),
            pltpu.VMEM((slots, half), jnp.float32),
            pltpu.VMEM((slots, half), jnp.float32),
            pltpu.VMEM((slots, LANES), jnp.float32),
            pltpu.VMEM((chunks, block * slots, LANES), jnp.float32),
        ],
        cost_estimate=pl.CostEstimate(
            flops=slots * half * mode_count * 10,
            bytes_accessed=slots * half * mode_count * 4,
            transcendentals=0,
        ),
    )(wave_lanes, log_start, geometry)


def project(received, legendre_table, field_order, belts, lons):
    slots, _, _, half_modes, half = legendre_table.shape
    sources = belts * lons
    lat_local = 2 * half // belts
    items = received.shape[2] // lat_local
    levels = items * lons
    rows = 2 * levels
    level_of = field_order.astype(jnp.int32)
    target = jnp.arange(2 * rows, dtype=jnp.int32)
    within = target % rows
    source_level = jnp.take(level_of, within % levels)
    source_row = (source_level % items) * (2 * lons) + (source_level // items) * 2 + within // levels
    source_row = source_row + (target // rows) * rows
    order = (source_row[:, None] == jnp.arange(2 * rows, dtype=jnp.int32)[None, :]).astype(jnp.bfloat16)
    mirror = (
        jnp.arange(lat_local)[:, None] + jnp.arange(lat_local)[None, :] == lat_local - 1
    ).astype(jnp.bfloat16)

    def body(received_ref, table_ref, order_ref, mirror_ref, out_ref, wide_ref, sums_ref):
        slot = pl.program_id(0)
        parity = pl.program_id(1)

        @pl.when((slot == 0) & (parity == 0))
        def _():
            @pl.loop(0, belts)
            def _(belt):
                for lon in range(lons):
                    value = received_ref[belt * lons + lon].astype(jnp.float32)
                    for item in range(items):
                        wide_ref[belt, item, lon * 2 * slots : (lon + 1) * 2 * slots, :] = value[
                            :, item * lat_local : (item + 1) * lat_local
                        ]

        @pl.when(parity == 0)
        def _():
            def rows_of(belt):
                return jnp.concatenate(
                    [wide_ref[belt, item, pl.ds(slot, 2 * lons, stride=slots), :] for item in range(items)],
                    axis=0,
                )

            for belt in range(belts // 2):
                north = rows_of(belt)
                south = jnp.dot(
                    rows_of(belts - 1 - belt).astype(LINK_DTYPE),
                    mirror_ref[...],
                    preferred_element_type=jnp.float32,
                )
                for index, value in enumerate((north + south, north - south)):
                    ordered = jnp.dot(
                        order_ref[...],
                        jnp.concatenate(split(value), axis=0),
                        preferred_element_type=jnp.float32,
                    )
                    sums_ref[index, :, belt * lat_local : (belt + 1) * lat_local] = ordered.astype(jnp.bfloat16)

        result = lax.dot_general(
            sums_ref[parity], table_ref[0, 0, 0], NT_DIMS, preferred_element_type=jnp.float32
        ) + lax.dot_general(
            sums_ref[parity], table_ref[0, 0, 1], NT_DIMS, preferred_element_type=jnp.float32
        )
        out_ref[0] = result[:rows] + result[rows:]

    return pl.pallas_call(
        body,
        name="project",
        grid=(slots, 2),
        in_specs=[
            pl.BlockSpec(received.shape, lambda s, p: (0, 0, 0)),
            pl.BlockSpec((1, 1, 2, half_modes, half), lambda s, p: (s, p, 0, 0, 0)),
            pl.BlockSpec((2 * rows, 2 * rows), lambda s, p: (0, 0)),
            pl.BlockSpec((lat_local, lat_local), lambda s, p: (0, 0)),
        ],
        out_specs=pl.BlockSpec((1, rows, half_modes), lambda s, p: (s, 0, p)),
        out_shape=jax.ShapeDtypeStruct((slots, rows, 2 * half_modes), jnp.float32),
        scratch_shapes=[
            pltpu.VMEM((belts, items, 2 * lons * slots, lat_local), jnp.float32),
            pltpu.VMEM((2, 2 * rows, half), jnp.bfloat16),
        ],
        compiler_params=pltpu.CompilerParams(vmem_limit_bytes=40 << 20),
    )(received, legendre_table, order, mirror)


def on_device(grid_fields, field_order, wave_order):
    belts = lax.axis_size("belt")
    lons = lax.axis_size("lon")
    levels, lat_local, lon_local = grid_fields.shape
    lat_count = lat_local * belts
    lon_count = lon_local * lons
    mode_count = wave_order.shape[0]
    slots = mode_count // (belts * lons)
    items = levels // lons
    blocks = grid_fields.reshape(lons, items * lat_local, lon_local)
    gathered = lax.all_to_all(blocks, "lon", split_axis=0, concat_axis=0, tiled=True)
    table = dft_table(wave_order, lon_count, slots)
    owner = lax.axis_index("belt") * lons + lax.axis_index("lon")
    own_waves = lax.dynamic_slice_in_dim(wave_order, owner * slots, slots, 0)
    legendre_table = legendre(own_waves, mode_count, lat_count)
    table, legendre_table = lax.optimization_barrier((table, legendre_table))
    received = transform_and_exchange(table, gathered, 1.0 / math.sqrt(lon_count))
    spectral = project(received, legendre_table, field_order, belts, lons)
    return spectral.reshape(slots, 2, levels, 2, mode_count // 2)


def solution(mesh):
    return jax.shard_map(
        on_device,
        mesh=mesh,
        in_specs=(P(None, "belt", "lon"), P(), P()),
        out_specs=P(("belt", "lon"), None, None, None, None),
        check_vma=False,
    )
```

```python
import math

import jax
import jax.numpy as jnp
from jax import lax
from jax.experimental import pallas as pl
from jax.experimental.pallas import tpu as pltpu
from jax.sharding import PartitionSpec as P

LANES = 128
NT_DIMS = (((1,), (1,)), ((), ()))

CODE_STEPS = 1024.0
CODE_LOW = -20.0


def encode(value):
    magnitude = jnp.abs(value)
    exponent = jnp.floor(jnp.log(jnp.maximum(magnitude, 2.0**CODE_LOW)) * (1.0 / math.log(2.0)))
    exponent = jnp.maximum(exponent, CODE_LOW)
    code = jnp.round(((exponent - CODE_LOW) + magnitude * jnp.exp2(-exponent)) * CODE_STEPS)
    return jnp.where(value < 0.0, -code, code).astype(jnp.int32).astype(jnp.int16)


def decode(code):
    level = code.astype(jnp.int32).astype(jnp.float32) * (1.0 / CODE_STEPS)
    magnitude = jnp.abs(level)
    octave = jnp.maximum(jnp.floor(magnitude), 1.0)
    value = (magnitude - octave + 1.0) * jnp.exp2(octave + (CODE_LOW - 1.0))
    return jnp.where(level < 0.0, -value, value)


def split(value):
    high = value.astype(jnp.bfloat16)
    return high, (value - high.astype(jnp.float32)).astype(jnp.bfloat16)


def dft_table(wave_order, lon_count, slot_count):
    quarter = lon_count // 4
    coarse_count = quarter // LANES
    owners = wave_order.shape[0] // slot_count
    steps = jnp.concatenate(
        (jnp.arange(LANES, dtype=jnp.int32), jnp.arange(LANES, dtype=jnp.int32) % coarse_count * LANES)
    )
    phase = wave_order[:, None] * steps[None, :] % lon_count
    angles = phase.astype(jnp.float32) * (2.0 * math.pi / lon_count)
    width = 2 * LANES
    cosine = jnp.cos(angles).reshape(owners, slot_count, width)
    sine = jnp.sin(angles).reshape(owners, slot_count, width)
    turns = jnp.broadcast_to(
        (wave_order % 4).astype(jnp.float32).reshape(owners, slot_count, 1), (owners, slot_count, LANES)
    )
    step = 8

    def body(cos_ref, sin_ref, turn_ref, out_ref):
        @pl.loop(0, step)
        def _(owner):
            cos_all = cos_ref[owner]
            sin_all = sin_ref[owner]
            cos_fine = cos_all[:, :LANES]
            sin_fine = sin_all[:, :LANES]
            turn = turn_ref[owner]
            turn = jnp.concatenate((turn, turn), axis=0)
            one = jnp.ones_like(turn)
            zero = jnp.zeros_like(turn)
            keep = jnp.where(turn == 0.0, one, jnp.where(turn == 2.0, -one, zero)).astype(jnp.bfloat16)
            swap = jnp.where(turn == 1.0, -one, jnp.where(turn == 3.0, one, zero)).astype(jnp.bfloat16)
            opposite = jnp.where((turn == 1.0) | (turn == 3.0), -one, one).astype(jnp.bfloat16)
            row = pl.multiple_of(owner * 2 * slot_count, 2 * slot_count)
            for a in range(coarse_count):
                ca = cos_all[:, LANES + a : LANES + a + 1]
                sa = sin_all[:, LANES + a : LANES + a + 1]
                cosine_rows = ca * cos_fine - sa * sin_fine
                sine_rows = sa * cos_fine + ca * sin_fine
                plain = jnp.concatenate((cosine_rows, -sine_rows), axis=0).astype(jnp.bfloat16)
                other = jnp.concatenate((sine_rows, cosine_rows), axis=0).astype(jnp.bfloat16)
                turned = plain * keep + other * swap
                for index, value in enumerate((plain, turned, plain * opposite, turned * opposite)):
                    start = index * quarter + a * LANES
                    out_ref[pl.ds(row, 2 * slot_count), start : start + LANES] = value

    return pl.pallas_call(
        body,
        name="dft_table",
        grid=(owners // step,),
        in_specs=[pl.BlockSpec((step, slot_count, width), lambda i: (i, 0, 0))] * 2
        + [pl.BlockSpec((step, slot_count, LANES), lambda i: (i, 0, 0))],
        out_specs=pl.BlockSpec((step * 2 * slot_count, lon_count), lambda i: (i, 0)),
        out_shape=jax.ShapeDtypeStruct((owners * 2 * slot_count, lon_count), jnp.bfloat16),
        compiler_params=pltpu.CompilerParams(vmem_limit_bytes=8 << 20),
        cost_estimate=pl.CostEstimate(
            flops=owners * 16 * lon_count * 4, bytes_accessed=owners * 32 * lon_count, transcendentals=0
        ),
    )(cosine, sine, turns)


def transform_and_exchange(table, samples, scale):
    belts = lax.axis_size("belt")
    lons = lax.axis_size("lon")
    parts, rows, length = samples.shape
    owners = belts * lons
    group = 2 * lons
    blocks = owners // group
    owner_rows = table.shape[0] // owners
    block_rows = group * owner_rows
    mesh_id = pl.DeviceIdType.MESH

    def body(table_ref, samples_ref, out_ref, stage_ref, send_ref, stage_sem, send_sem, recv_sem, local_sem):
        belt = lax.axis_index("belt")
        lon = lax.axis_index("lon")
        me = belt * lons + lon
        barrier = pltpu.get_barrier_semaphore()

        def place(step):
            away = blocks - 1 - step
            x = lax.rem(belt // 4 + away // 2, blocks // 2)
            return x * 2 + lax.rem(lax.rem(belt // 2, 2) + lax.rem(away, 2), 2)

        def member(index):
            away = lax.rem(index, lons)
            core = lax.rem(lax.rem(belt, 2) + index // lons, 2)
            half = lons // 2
            high = lax.rem(lon // half + away // half, 2)
            return core, high * half + lax.rem(lax.rem(lon, half) + lax.rem(away, half), half)

        def fetch(step, slot):
            return pltpu.make_async_copy(
                table_ref.at[pl.ds(pl.multiple_of(place(step) * block_rows, block_rows), block_rows)],
                stage_ref.at[slot],
                stage_sem.at[slot],
            )

        def send(step, index):
            core, target = member(index)
            return pltpu.make_async_remote_copy(
                send_ref.at[step, core * lons + target],
                out_ref.at[me],
                send_sem,
                recv_sem,
                device_id=(place(step) * 2 + core, target),
                device_id_type=mesh_id,
            )

        fetch(0, 0).start()

        @pl.loop(1, owners)
        def _(away):
            peer = lax.rem(me + away, owners)
            pl.semaphore_signal(
                barrier, inc=1, device_id=(peer // lons, lax.rem(peer, lons)), device_id_type=mesh_id
            )

        @pl.loop(0, blocks)
        def _(step):
            slot = lax.rem(step, 2)
            fetch(step, slot).wait()

            @pl.when(step < blocks - 1)
            def _():
                fetch(step + 1, 1 - slot).start()

            total = None
            for part in range(parts):
                term = lax.dot_general(
                    stage_ref[slot, :, part * length : (part + 1) * length],
                    samples_ref[part],
                    NT_DIMS,
                    preferred_element_type=jnp.float32,
                )
                total = term if total is None else total + term
            send_ref[step] = encode(total * scale).reshape(group, owner_rows, rows)

            @pl.when(step == 0)
            def _():
                pl.semaphore_wait(barrier, owners - 1)

            @pl.loop(0, group)
            def _(back):
                index = group - 1 - back

                @pl.when((step < blocks - 1) | (index > 0))
                def _():
                    send(step, index).start()

        core, target = member(0)
        local = pltpu.make_async_copy(
            send_ref.at[blocks - 1, core * lons + target], out_ref.at[me], local_sem
        )
        local.start()
        local.wait()
        everything = pltpu.make_async_remote_copy(
            out_ref.at[pl.ds(0, owners - 1)],
            out_ref.at[pl.ds(0, owners - 1)],
            send_sem,
            recv_sem,
            device_id=(lax.rem(belt + 1, belts), lon),
            device_id_type=mesh_id,
        )
        everything.wait_recv()
        everything.wait_send()

    return pl.pallas_call(
        body,
        name="transform_and_exchange",
        in_specs=[pl.BlockSpec(memory_space=pl.ANY), pl.BlockSpec(memory_space=pltpu.VMEM)],
        out_specs=pl.BlockSpec(memory_space=pl.ANY),
        out_shape=jax.ShapeDtypeStruct((owners, owner_rows, rows), jnp.int16),
        scratch_shapes=[
            pltpu.VMEM((2, block_rows, parts * length), jnp.bfloat16),
            pltpu.VMEM((blocks, group, owner_rows, rows), jnp.int16),
            pltpu.SemaphoreType.DMA((2,)),
            pltpu.SemaphoreType.DMA,
            pltpu.SemaphoreType.DMA,
            pltpu.SemaphoreType.DMA,
        ],
        compiler_params=pltpu.CompilerParams(
            collective_id=0, has_side_effects=True, vmem_limit_bytes=20 << 20
        ),
    )(table, samples)


def latitude_geometry(lat_count):
    lat_index = jnp.arange(lat_count // 2).astype(jnp.float32)
    colatitude = math.pi * (lat_index + 0.75) / (lat_count + 0.5)
    sine_lat = jnp.sin(colatitude)
    weight = math.pi / (lat_count + 0.5) * sine_lat * math.sqrt(lat_count / 2.0)
    return (jnp.cos(colatitude), sine_lat, weight)


def legendre(wavenumbers, mode_count, lat_count):
    slots = wavenumbers.shape[0]
    half = lat_count // 2
    chunks = half // LANES
    wave_value = wavenumbers.astype(jnp.float32)[:, None]
    cosine, sine_lat, weight = latitude_geometry(lat_count)
    term_index = jnp.arange(1, mode_count + 1).astype(jnp.float32)
    log_terms = jnp.log1p(0.5 / term_index)
    start_sum = jnp.sum(
        jnp.where(term_index[None, :] <= wave_value, log_terms[None, :], 0.0), axis=1, keepdims=True
    )
    log_start = -0.5 * math.log(2.0) + 0.5 * start_sum + wave_value * jnp.log(sine_lat)[None, :]
    geometry = jnp.stack((cosine, weight))[:, None, :] * jnp.ones((2, slots, 1), jnp.float32)
    wave_lanes = jnp.broadcast_to(wave_value, (slots, LANES))
    block = 32
    renorm = 16

    def body(wave_ref, log_ref, geo_ref, out_ref, prev_ref, cur_ref, scale_ref, inv_ref, rows_ref):
        step = pl.program_id(0)

        @pl.when(step == 0)
        def _():
            prev_ref[...] = jnp.zeros_like(prev_ref)
            cur_ref[...] = jnp.ones_like(cur_ref)
            scale_ref[...] = log_ref[...]
            inv_ref[...] = jnp.zeros_like(inv_ref)

        wave = wave_ref[...]
        first = (step * block).astype(jnp.float32)
        lanes = [slice(a * LANES, (a + 1) * LANES) for a in range(chunks)]
        inverse = inv_ref[...]
        prev = [prev_ref[:, s] for s in lanes]
        cur = [cur_ref[:, s] for s in lanes]
        amp = [None] * chunks
        for row in range(block):
            if row % renorm == 0:
                for a in range(chunks):
                    total = jnp.maximum(jnp.abs(prev[a]) + jnp.abs(cur[a]), 1e-30)
                    prev[a] = prev[a] / total
                    cur[a] = cur[a] / total
                    log_scale = scale_ref[:, lanes[a]] + jnp.log(total)
                    scale_ref[:, lanes[a]] = log_scale
                    amp[a] = jnp.exp(log_scale) * geo_ref[1, :, lanes[a]]
            for a in range(chunks):
                rows_ref[a, row * slots : (row + 1) * slots, :] = cur[a] * amp[a]
            offset = first + (row + 1.0)
            degree = wave + offset
            numer = 4.0 * degree * degree - 1.0
            denom = offset * (wave + degree)
            root = lax.rsqrt(numer * denom)
            keep = degree < mode_count
            factor = jnp.where(keep, numer * root, 0.0)
            ratio = factor * inverse
            inverse = denom * root
            for a in range(chunks):
                following = (factor * geo_ref[0, :, lanes[a]]) * cur[a] - ratio * prev[a]
                prev[a] = cur[a]
                cur[a] = following
        inv_ref[...] = inverse
        for a in range(chunks):
            prev_ref[:, lanes[a]] = prev[a]
            cur_ref[:, lanes[a]] = cur[a]
        for slot in range(slots):
            for parity in range(2):
                for a in range(chunks):
                    out_ref[slot, parity, :, lanes[a]] = rows_ref[
                        a, pl.ds(parity * slots + slot, block // 2, stride=2 * slots), :
                    ].astype(jnp.bfloat16)

    return pl.pallas_call(
        body,
        name="legendre",
        grid=(mode_count // block,),
        in_specs=[
            pl.BlockSpec((slots, LANES), lambda i: (0, 0)),
            pl.BlockSpec((slots, half), lambda i: (0, 0)),
            pl.BlockSpec((2, slots, half), lambda i: (0, 0, 0)),
        ],
        out_specs=pl.BlockSpec((slots, 2, block // 2, half), lambda i: (0, 0, i, 0)),
        out_shape=jax.ShapeDtypeStruct((slots, 2, mode_count // 2, half), jnp.bfloat16),
        scratch_shapes=[
            pltpu.VMEM((slots, half), jnp.float32),
            pltpu.VMEM((slots, half), jnp.float32),
            pltpu.VMEM((slots, half), jnp.float32),
            pltpu.VMEM((slots, LANES), jnp.float32),
            pltpu.VMEM((chunks, block * slots, LANES), jnp.float32),
        ],
        cost_estimate=pl.CostEstimate(
            flops=slots * half * mode_count * 10,
            bytes_accessed=slots * half * mode_count * 2,
            transcendentals=0,
        ),
        compiler_params=pltpu.CompilerParams(vmem_limit_bytes=8 << 20),
    )(wave_lanes, log_start, geometry)


def project(received, legendre_table, field_order, belts, lons):
    slots, _, half_modes, half = legendre_table.shape
    lat_local = 2 * half // belts
    items = received.shape[2] // lat_local
    levels = items * lons
    rows = 2 * levels
    target = jnp.arange(2 * rows, dtype=jnp.int32)
    within = target % rows
    source_level = jnp.take(field_order.astype(jnp.int32), within % levels)
    source_row = (source_level % items) * (2 * lons) + (source_level // items) * 2 + within // levels
    source_row = source_row + (target // rows) * rows
    order = (source_row[:, None] == jnp.arange(2 * rows, dtype=jnp.int32)[None, :]).astype(jnp.bfloat16)
    mirror = (
        jnp.arange(lat_local)[:, None] + jnp.arange(lat_local)[None, :] == lat_local - 1
    ).astype(jnp.bfloat16)

    def body(received_ref, table_ref, order_ref, mirror_ref, out_ref, wide_ref):
        slot = pl.program_id(0)
        parity = pl.program_id(1)

        @pl.when((slot == 0) & (parity == 0))
        def _():
            @pl.loop(0, belts // 2)
            def _(belt):
                other = belts - 1 - belt
                for item in range(items):
                    lanes = slice(item * lat_local, (item + 1) * lat_local)
                    north = decode(received_ref[pl.ds(belt * lons, lons), :, lanes]).reshape(-1, lat_local)
                    south = decode(received_ref[pl.ds(other * lons, lons), :, lanes]).reshape(-1, lat_local)
                    high, low = split(south)
                    south = jnp.dot(high, mirror_ref[...], preferred_element_type=jnp.float32) + jnp.dot(
                        low, mirror_ref[...], preferred_element_type=jnp.float32
                    )
                    wide_ref[0, belt, item] = north + south
                    wide_ref[1, belt, item] = north - south

        value = jnp.concatenate(
            [
                jnp.concatenate(
                    [
                        wide_ref[parity, belt, item, pl.ds(slot, 2 * lons, stride=slots), :]
                        for item in range(items)
                    ],
                    axis=0,
                )
                for belt in range(belts // 2)
            ],
            axis=1,
        )
        sums = jnp.dot(
            order_ref[...], jnp.concatenate(split(value), axis=0), preferred_element_type=jnp.float32
        ).astype(jnp.bfloat16)
        result = lax.dot_general(sums, table_ref[0, 0], NT_DIMS, preferred_element_type=jnp.float32)
        out_ref[0] = result[:rows] + result[rows:]

    return pl.pallas_call(
        body,
        name="project",
        grid=(slots, 2),
        in_specs=[
            pl.BlockSpec(received.shape, lambda s, p: (0, 0, 0)),
            pl.BlockSpec((1, 1, half_modes, half), lambda s, p: (s, p, 0, 0)),
            pl.BlockSpec((2 * rows, 2 * rows), lambda s, p: (0, 0)),
            pl.BlockSpec((lat_local, lat_local), lambda s, p: (0, 0)),
        ],
        out_specs=pl.BlockSpec((1, rows, half_modes), lambda s, p: (s, 0, p)),
        out_shape=jax.ShapeDtypeStruct((slots, rows, 2 * half_modes), jnp.float32),
        scratch_shapes=[pltpu.VMEM((2, belts // 2, items, 2 * lons * slots, lat_local), jnp.float32)],
        compiler_params=pltpu.CompilerParams(vmem_limit_bytes=20 << 20),
    )(received, legendre_table, order, mirror)


def on_device(grid_fields, field_order, wave_order):
    belts = lax.axis_size("belt")
    lons = lax.axis_size("lon")
    levels, lat_local, lon_local = grid_fields.shape
    lat_count = lat_local * belts
    lon_count = lon_local * lons
    mode_count = wave_order.shape[0]
    slots = mode_count // (belts * lons)
    items = levels // lons
    blocks = grid_fields.reshape(lons, items * lat_local, lon_local)
    gathered = lax.all_to_all(blocks, "lon", split_axis=0, concat_axis=0, tiled=True)
    table = dft_table(wave_order, lon_count, slots)
    owner = lax.axis_index("belt") * lons + lax.axis_index("lon")
    own_waves = lax.dynamic_slice_in_dim(wave_order, owner * slots, slots, 0)
    legendre_table = legendre(own_waves, mode_count, lat_count)
    table, legendre_table = lax.optimization_barrier((table, legendre_table))
    received = transform_and_exchange(table, gathered, 1.0 / math.sqrt(lon_count))
    spectral = project(received, legendre_table, field_order, belts, lons)
    return spectral.reshape(slots, 2, levels, 2, mode_count // 2)


def solution(mesh):
    return jax.shard_map(
        on_device,
        mesh=mesh,
        in_specs=(P(None, "belt", "lon"), P(), P()),
        out_specs=P(("belt", "lon"), None, None, None, None),
        check_vma=False,
    )
```

```python
import math

import jax
import jax.numpy as jnp
from jax import lax
from jax.experimental import pallas as pl
from jax.experimental.pallas import tpu as pltpu
from jax.sharding import PartitionSpec as P

LANES = 128
NT_DIMS = (((1,), (1,)), ((), ()))

CODE_STEPS = 1024.0
CODE_LOW = -20.0


def encode(value):
    magnitude = jnp.abs(value)
    exponent = jnp.floor(jnp.log(jnp.maximum(magnitude, 2.0**CODE_LOW)) * (1.0 / math.log(2.0)))
    exponent = jnp.maximum(exponent, CODE_LOW)
    code = jnp.round(((exponent - CODE_LOW) + magnitude * jnp.exp2(-exponent)) * CODE_STEPS)
    return jnp.where(value < 0.0, -code, code).astype(jnp.int32).astype(jnp.int16)


def decode(code):
    level = code.astype(jnp.int32).astype(jnp.float32) * (1.0 / CODE_STEPS)
    magnitude = jnp.abs(level)
    octave = jnp.maximum(jnp.floor(magnitude), 1.0)
    value = (magnitude - octave + 1.0) * jnp.exp2(octave + (CODE_LOW - 1.0))
    return jnp.where(level < 0.0, -value, value)


def split(value):
    high = value.astype(jnp.bfloat16)
    return high, (value - high.astype(jnp.float32)).astype(jnp.bfloat16)


def dft_table(wave_order, lon_count, slot_count):
    quarter = lon_count // 4
    coarse_count = quarter // LANES
    owners = wave_order.shape[0] // slot_count
    steps = jnp.concatenate(
        (jnp.arange(LANES, dtype=jnp.int32), jnp.arange(LANES, dtype=jnp.int32) % coarse_count * LANES)
    )
    phase = wave_order[:, None] * steps[None, :] % lon_count
    angles = phase.astype(jnp.float32) * (2.0 * math.pi / lon_count)
    width = 2 * LANES
    cosine = jnp.cos(angles).reshape(owners, slot_count, width)
    sine = jnp.sin(angles).reshape(owners, slot_count, width)
    turns = jnp.broadcast_to(
        (wave_order % 4).astype(jnp.float32).reshape(owners, slot_count, 1), (owners, slot_count, LANES)
    )
    step = 8

    def body(cos_ref, sin_ref, turn_ref, out_ref):
        @pl.loop(0, step)
        def _(owner):
            cos_all = cos_ref[owner]
            sin_all = sin_ref[owner]
            cos_fine = cos_all[:, :LANES]
            sin_fine = sin_all[:, :LANES]
            turn = turn_ref[owner]
            turn = jnp.concatenate((turn, turn), axis=0)
            one = jnp.ones_like(turn)
            zero = jnp.zeros_like(turn)
            keep = jnp.where(turn == 0.0, one, jnp.where(turn == 2.0, -one, zero)).astype(jnp.bfloat16)
            swap = jnp.where(turn == 1.0, -one, jnp.where(turn == 3.0, one, zero)).astype(jnp.bfloat16)
            opposite = jnp.where((turn == 1.0) | (turn == 3.0), -one, one).astype(jnp.bfloat16)
            row = pl.multiple_of(owner * 2 * slot_count, 2 * slot_count)
            for a in range(coarse_count):
                ca = cos_all[:, LANES + a : LANES + a + 1]
                sa = sin_all[:, LANES + a : LANES + a + 1]
                cosine_rows = ca * cos_fine - sa * sin_fine
                sine_rows = sa * cos_fine + ca * sin_fine
                plain = jnp.concatenate((cosine_rows, -sine_rows), axis=0).astype(jnp.bfloat16)
                other = jnp.concatenate((sine_rows, cosine_rows), axis=0).astype(jnp.bfloat16)
                turned = plain * keep + other * swap
                for index, value in enumerate((plain, turned, plain * opposite, turned * opposite)):
                    start = index * quarter + a * LANES
                    out_ref[pl.ds(row, 2 * slot_count), start : start + LANES] = value

    return pl.pallas_call(
        body,
        name="dft_table",
        grid=(owners // step,),
        in_specs=[pl.BlockSpec((step, slot_count, width), lambda i: (i, 0, 0))] * 2
        + [pl.BlockSpec((step, slot_count, LANES), lambda i: (i, 0, 0))],
        out_specs=pl.BlockSpec((step * 2 * slot_count, lon_count), lambda i: (i, 0)),
        out_shape=jax.ShapeDtypeStruct((owners * 2 * slot_count, lon_count), jnp.bfloat16),
        cost_estimate=pl.CostEstimate(
            flops=owners * 16 * lon_count * 4, bytes_accessed=owners * 32 * lon_count, transcendentals=0
        ),
    )(cosine, sine, turns)


def transform_and_exchange(table, samples, scale):
    belts = lax.axis_size("belt")
    lons = lax.axis_size("lon")
    parts, rows, length = samples.shape
    owners = belts * lons
    group = 2 * lons
    blocks = owners // group
    owner_rows = table.shape[0] // owners
    block_rows = group * owner_rows
    mesh_id = pl.DeviceIdType.MESH

    def body(table_ref, samples_ref, out_ref, stage_ref, send_ref, stage_sem, send_sem, recv_sem, local_sem):
        belt = lax.axis_index("belt")
        lon = lax.axis_index("lon")
        me = belt * lons + lon
        barrier = pltpu.get_barrier_semaphore()

        def place(step):
            away = blocks - 1 - step
            x = lax.rem(belt // 4 + away // 2, blocks // 2)
            return x * 2 + lax.rem(lax.rem(belt // 2, 2) + lax.rem(away, 2), 2)

        def member(index):
            away = lax.rem(index, lons)
            core = lax.rem(lax.rem(belt, 2) + index // lons, 2)
            half = lons // 2
            high = lax.rem(lon // half + away // half, 2)
            return core, high * half + lax.rem(lax.rem(lon, half) + lax.rem(away, half), half)

        def fetch(step, slot):
            return pltpu.make_async_copy(
                table_ref.at[pl.ds(pl.multiple_of(place(step) * block_rows, block_rows), block_rows)],
                stage_ref.at[slot],
                stage_sem.at[slot],
            )

        def send(step, index):
            core, target = member(index)
            return pltpu.make_async_remote_copy(
                send_ref.at[step, core * lons + target],
                out_ref.at[me],
                send_sem,
                recv_sem,
                device_id=(place(step) * 2 + core, target),
                device_id_type=mesh_id,
            )

        fetch(0, 0).start()

        @pl.loop(1, owners)
        def _(away):
            peer = lax.rem(me + away, owners)
            pl.semaphore_signal(
                barrier, inc=1, device_id=(peer // lons, lax.rem(peer, lons)), device_id_type=mesh_id
            )

        @pl.loop(0, blocks)
        def _(step):
            slot = lax.rem(step, 2)
            fetch(step, slot).wait()

            @pl.when(step < blocks - 1)
            def _():
                fetch(step + 1, 1 - slot).start()

            total = None
            for part in range(parts):
                term = lax.dot_general(
                    stage_ref[slot, :, part * length : (part + 1) * length],
                    samples_ref[part],
                    NT_DIMS,
                    preferred_element_type=jnp.float32,
                )
                total = term if total is None else total + term
            send_ref[step] = encode(total * scale).reshape(group, owner_rows, rows)

            @pl.when(step == 0)
            def _():
                pl.semaphore_wait(barrier, owners - 1)

            @pl.loop(0, group)
            def _(back):
                index = group - 1 - back

                @pl.when((step < blocks - 1) | (index > 0))
                def _():
                    send(step, index).start()

        core, target = member(0)
        local = pltpu.make_async_copy(
            send_ref.at[blocks - 1, core * lons + target], out_ref.at[me], local_sem
        )
        local.start()
        local.wait()
        everything = pltpu.make_async_remote_copy(
            out_ref.at[pl.ds(0, owners - 1)],
            out_ref.at[pl.ds(0, owners - 1)],
            send_sem,
            recv_sem,
            device_id=(lax.rem(belt + 1, belts), lon),
            device_id_type=mesh_id,
        )
        everything.wait_recv()
        everything.wait_send()

    return pl.pallas_call(
        body,
        name="transform_and_exchange",
        in_specs=[pl.BlockSpec(memory_space=pl.ANY), pl.BlockSpec(memory_space=pltpu.VMEM)],
        out_specs=pl.BlockSpec(memory_space=pl.ANY),
        out_shape=jax.ShapeDtypeStruct((owners, owner_rows, rows), jnp.int16),
        scratch_shapes=[
            pltpu.VMEM((2, block_rows, parts * length), jnp.bfloat16),
            pltpu.VMEM((blocks, group, owner_rows, rows), jnp.int16),
            pltpu.SemaphoreType.DMA((2,)),
            pltpu.SemaphoreType.DMA,
            pltpu.SemaphoreType.DMA,
            pltpu.SemaphoreType.DMA,
        ],
        compiler_params=pltpu.CompilerParams(
            collective_id=0, has_side_effects=True, vmem_limit_bytes=40 << 20
        ),
    )(table, samples)


def latitude_geometry(lat_count):
    lat_index = jnp.arange(lat_count // 2).astype(jnp.float32)
    colatitude = math.pi * (lat_index + 0.75) / (lat_count + 0.5)
    sine_lat = jnp.sin(colatitude)
    weight = math.pi / (lat_count + 0.5) * sine_lat * math.sqrt(lat_count / 2.0)
    return (jnp.cos(colatitude), sine_lat, weight)


def legendre(wavenumbers, mode_count, lat_count):
    slots = wavenumbers.shape[0]
    half = lat_count // 2
    chunks = half // LANES
    wave_value = wavenumbers.astype(jnp.float32)[:, None]
    cosine, sine_lat, weight = latitude_geometry(lat_count)
    term_index = jnp.arange(1, mode_count + 1).astype(jnp.float32)
    log_terms = jnp.log1p(0.5 / term_index)
    start_sum = jnp.sum(
        jnp.where(term_index[None, :] <= wave_value, log_terms[None, :], 0.0), axis=1, keepdims=True
    )
    log_start = -0.5 * math.log(2.0) + 0.5 * start_sum + wave_value * jnp.log(sine_lat)[None, :]
    geometry = jnp.stack((cosine, weight))[:, None, :] * jnp.ones((2, slots, 1), jnp.float32)
    wave_lanes = jnp.broadcast_to(wave_value, (slots, LANES))
    block = 32
    renorm = 16

    def body(wave_ref, log_ref, geo_ref, out_ref, prev_ref, cur_ref, scale_ref, inv_ref, rows_ref):
        step = pl.program_id(0)

        @pl.when(step == 0)
        def _():
            prev_ref[...] = jnp.zeros_like(prev_ref)
            cur_ref[...] = jnp.ones_like(cur_ref)
            scale_ref[...] = log_ref[...]
            inv_ref[...] = jnp.zeros_like(inv_ref)

        wave = wave_ref[...]
        first = (step * block).astype(jnp.float32)
        lanes = [slice(a * LANES, (a + 1) * LANES) for a in range(chunks)]
        inverse = inv_ref[...]
        prev = [prev_ref[:, s] for s in lanes]
        cur = [cur_ref[:, s] for s in lanes]
        amp = [None] * chunks
        for row in range(block):
            if row % renorm == 0:
                for a in range(chunks):
                    total = jnp.maximum(jnp.abs(prev[a]) + jnp.abs(cur[a]), 1e-30)
                    prev[a] = prev[a] / total
                    cur[a] = cur[a] / total
                    log_scale = scale_ref[:, lanes[a]] + jnp.log(total)
                    scale_ref[:, lanes[a]] = log_scale
                    amp[a] = jnp.exp(log_scale) * geo_ref[1, :, lanes[a]]
            for a in range(chunks):
                rows_ref[a, row * slots : (row + 1) * slots, :] = cur[a] * amp[a]
            offset = first + (row + 1.0)
            degree = wave + offset
            numer = 4.0 * degree * degree - 1.0
            denom = offset * (wave + degree)
            root = lax.rsqrt(numer * denom)
            keep = degree < mode_count
            factor = jnp.where(keep, numer * root, 0.0)
            ratio = factor * inverse
            inverse = denom * root
            for a in range(chunks):
                following = (factor * geo_ref[0, :, lanes[a]]) * cur[a] - ratio * prev[a]
                prev[a] = cur[a]
                cur[a] = following
        inv_ref[...] = inverse
        for a in range(chunks):
            prev_ref[:, lanes[a]] = prev[a]
            cur_ref[:, lanes[a]] = cur[a]
        for slot in range(slots):
            for parity in range(2):
                for a in range(chunks):
                    out_ref[slot, parity, :, lanes[a]] = rows_ref[
                        a, pl.ds(parity * slots + slot, block // 2, stride=2 * slots), :
                    ].astype(jnp.bfloat16)

    return pl.pallas_call(
        body,
        name="legendre",
        grid=(mode_count // block,),
        in_specs=[
            pl.BlockSpec((slots, LANES), lambda i: (0, 0)),
            pl.BlockSpec((slots, half), lambda i: (0, 0)),
            pl.BlockSpec((2, slots, half), lambda i: (0, 0, 0)),
        ],
        out_specs=pl.BlockSpec((slots, 2, block // 2, half), lambda i: (0, 0, i, 0)),
        out_shape=jax.ShapeDtypeStruct((slots, 2, mode_count // 2, half), jnp.bfloat16),
        scratch_shapes=[
            pltpu.VMEM((slots, half), jnp.float32),
            pltpu.VMEM((slots, half), jnp.float32),
            pltpu.VMEM((slots, half), jnp.float32),
            pltpu.VMEM((slots, LANES), jnp.float32),
            pltpu.VMEM((chunks, block * slots, LANES), jnp.float32),
        ],
        cost_estimate=pl.CostEstimate(
            flops=slots * half * mode_count * 10,
            bytes_accessed=slots * half * mode_count * 2,
            transcendentals=0,
        ),
    )(wave_lanes, log_start, geometry)


def project(received, legendre_table, field_order, belts, lons):
    slots, _, half_modes, half = legendre_table.shape
    lat_local = 2 * half // belts
    items = received.shape[2] // lat_local
    levels = items * lons
    rows = 2 * levels
    target = jnp.arange(2 * rows, dtype=jnp.int32)
    within = target % rows
    source_level = jnp.take(field_order.astype(jnp.int32), within % levels)
    source_row = (source_level % items) * (2 * lons) + (source_level // items) * 2 + within // levels
    source_row = source_row + (target // rows) * rows
    order = (source_row[:, None] == jnp.arange(2 * rows, dtype=jnp.int32)[None, :]).astype(jnp.bfloat16)
    mirror = (
        jnp.arange(lat_local)[:, None] + jnp.arange(lat_local)[None, :] == lat_local - 1
    ).astype(jnp.bfloat16)

    def body(received_ref, table_ref, order_ref, mirror_ref, out_ref, wide_ref):
        slot = pl.program_id(0)
        parity = pl.program_id(1)

        @pl.when((slot == 0) & (parity == 0))
        def _():
            @pl.loop(0, belts // 2)
            def _(belt):
                other = belts - 1 - belt
                for item in range(items):
                    lanes = slice(item * lat_local, (item + 1) * lat_local)
                    north = decode(received_ref[pl.ds(belt * lons, lons), :, lanes]).reshape(-1, lat_local)
                    south = decode(received_ref[pl.ds(other * lons, lons), :, lanes]).reshape(-1, lat_local)
                    high, low = split(south)
                    south = jnp.dot(high, mirror_ref[...], preferred_element_type=jnp.float32) + jnp.dot(
                        low, mirror_ref[...], preferred_element_type=jnp.float32
                    )
                    wide_ref[0, belt, item] = north + south
                    wide_ref[1, belt, item] = north - south

        value = jnp.concatenate(
            [
                jnp.concatenate(
                    [
                        wide_ref[parity, belt, item, pl.ds(slot, 2 * lons, stride=slots), :]
                        for item in range(items)
                    ],
                    axis=0,
                )
                for belt in range(belts // 2)
            ],
            axis=1,
        )
        sums = jnp.dot(
            order_ref[...], jnp.concatenate(split(value), axis=0), preferred_element_type=jnp.float32
        ).astype(jnp.bfloat16)
        result = lax.dot_general(sums, table_ref[0, 0], NT_DIMS, preferred_element_type=jnp.float32)
        out_ref[0] = result[:rows] + result[rows:]

    return pl.pallas_call(
        body,
        name="project",
        grid=(slots, 2),
        in_specs=[
            pl.BlockSpec(received.shape, lambda s, p: (0, 0, 0)),
            pl.BlockSpec((1, 1, half_modes, half), lambda s, p: (s, p, 0, 0)),
            pl.BlockSpec((2 * rows, 2 * rows), lambda s, p: (0, 0)),
            pl.BlockSpec((lat_local, lat_local), lambda s, p: (0, 0)),
        ],
        out_specs=pl.BlockSpec((1, rows, half_modes), lambda s, p: (s, 0, p)),
        out_shape=jax.ShapeDtypeStruct((slots, rows, 2 * half_modes), jnp.float32),
        scratch_shapes=[pltpu.VMEM((2, belts // 2, items, 2 * lons * slots, lat_local), jnp.float32)],
        compiler_params=pltpu.CompilerParams(vmem_limit_bytes=20 << 20),
    )(received, legendre_table, order, mirror)


def on_device(grid_fields, field_order, wave_order):
    belts = lax.axis_size("belt")
    lons = lax.axis_size("lon")
    levels, lat_local, lon_local = grid_fields.shape
    lat_count = lat_local * belts
    lon_count = lon_local * lons
    mode_count = wave_order.shape[0]
    slots = mode_count // (belts * lons)
    items = levels // lons
    blocks = grid_fields.reshape(lons, items * lat_local, lon_local)
    gathered = lax.all_to_all(blocks, "lon", split_axis=0, concat_axis=0, tiled=True)
    table = dft_table(wave_order, lon_count, slots)
    owner = lax.axis_index("belt") * lons + lax.axis_index("lon")
    own_waves = lax.dynamic_slice_in_dim(wave_order, owner * slots, slots, 0)
    legendre_table = legendre(own_waves, mode_count, lat_count)
    table, legendre_table = lax.optimization_barrier((table, legendre_table))
    received = transform_and_exchange(table, gathered, 1.0 / math.sqrt(lon_count))
    spectral = project(received, legendre_table, field_order, belts, lons)
    return spectral.reshape(slots, 2, levels, 2, mode_count // 2)


def solution(mesh):
    return jax.shard_map(
        on_device,
        mesh=mesh,
        in_specs=(P(None, "belt", "lon"), P(), P()),
        out_specs=P(("belt", "lon"), None, None, None, None),
        check_vma=False,
    )
```

```python
import math

import jax
import jax.numpy as jnp
from jax import lax
from jax.experimental import pallas as pl
from jax.experimental.pallas import tpu as pltpu
from jax.sharding import PartitionSpec as P

LANES = 128
NT_DIMS = (((1,), (1,)), ((), ()))

CODE_STEPS = 1024.0
CODE_LOW = -20.0

CHUNKS = 2
BLOCK = 32
RENORM = 16
EARLY = 19


def encode(value):
    magnitude = jnp.abs(value)
    exponent = jnp.floor(jnp.log(jnp.maximum(magnitude, 2.0**CODE_LOW)) * (1.0 / math.log(2.0)))
    exponent = jnp.maximum(exponent, CODE_LOW)
    code = jnp.round(((exponent - CODE_LOW) + magnitude * jnp.exp2(-exponent)) * CODE_STEPS)
    return jnp.where(value < 0.0, -code, code).astype(jnp.int32).astype(jnp.int16)


def decode(code):
    level = code.astype(jnp.int32).astype(jnp.float32) * (1.0 / CODE_STEPS)
    magnitude = jnp.abs(level)
    octave = jnp.maximum(jnp.floor(magnitude), 1.0)
    value = (magnitude - octave + 1.0) * jnp.exp2(octave + (CODE_LOW - 1.0))
    return jnp.where(level < 0.0, -value, value)


def split(value):
    high = value.astype(jnp.bfloat16)
    return high, (value - high.astype(jnp.float32)).astype(jnp.bfloat16)


def iota(shape, dim):
    return lax.broadcasted_iota(jnp.int32, shape, dim)


def column_of(waves, owner):
    return jnp.sum(jnp.where(iota(waves.shape, 1) == owner, waves, 0.0), axis=1, keepdims=True)


def fill_table(waves_ref, table_ref, slots, owners, lon_count):
    quarter = lon_count // 4
    coarse_count = quarter // LANES
    lane = iota((slots, LANES), 1)
    steps = (lane, lax.rem(lane, coarse_count) * LANES)

    def one_owner(owner):
        wave = jnp.broadcast_to(column_of(waves_ref[...], owner), (slots, LANES)).astype(jnp.int32)
        angles = [
            lax.rem(wave * step, lon_count).astype(jnp.float32) * (2.0 * math.pi / lon_count) for step in steps
        ]
        cos_fine, cos_coarse = [jnp.cos(angle) for angle in angles]
        sin_fine, sin_coarse = [jnp.sin(angle) for angle in angles]
        turn = lax.rem(wave, 4).astype(jnp.float32)
        turn = jnp.concatenate((turn, turn), axis=0)
        one = jnp.ones_like(turn)
        zero = jnp.zeros_like(turn)
        keep = jnp.where(turn == 0.0, one, jnp.where(turn == 2.0, -one, zero)).astype(jnp.bfloat16)
        swap = jnp.where(turn == 1.0, -one, jnp.where(turn == 3.0, one, zero)).astype(jnp.bfloat16)
        opposite = jnp.where((turn == 1.0) | (turn == 3.0), -one, one).astype(jnp.bfloat16)
        row = pl.multiple_of(owner * 2 * slots, 2 * slots)
        for a in range(coarse_count):
            ca = cos_coarse[:, a : a + 1]
            sa = sin_coarse[:, a : a + 1]
            cosine = ca * cos_fine - sa * sin_fine
            sine = sa * cos_fine + ca * sin_fine
            plain = jnp.concatenate((cosine, -sine), axis=0).astype(jnp.bfloat16)
            other = jnp.concatenate((sine, cosine), axis=0).astype(jnp.bfloat16)
            turned = plain * keep + other * swap
            for index, value in enumerate((plain, turned, plain * opposite, turned * opposite)):
                start = index * quarter + a * LANES
                table_ref[pl.ds(row, 2 * slots), start : start + LANES] = value

    @pl.loop(0, owners // 2)
    def _(pair):
        one_owner(2 * pair)
        one_owner(2 * pair + 1)


def start_legendre(wave, refs, mode_count, half):
    prev_ref, cur_ref, scale_ref, inv_ref, geo_ref, _ = refs
    lane = iota(wave.shape, 1).astype(jnp.float32)
    terms = None
    for a in range(mode_count // LANES):
        index = lane + (a * LANES + 1.0)
        term = jnp.where(index <= wave, jnp.log1p(0.5 / index), 0.0)
        terms = term if terms is None else terms + term
    start_sum = jnp.sum(terms, axis=1, keepdims=True)
    prev_ref[...] = jnp.zeros_like(prev_ref)
    cur_ref[...] = jnp.ones_like(cur_ref)
    inv_ref[...] = jnp.zeros_like(inv_ref)
    for a in range(half // LANES):
        lanes = slice(a * LANES, (a + 1) * LANES)
        colatitude = (math.pi / (2 * half + 0.5)) * (lane + (a * LANES + 0.75))
        sine = jnp.sin(colatitude)
        geo_ref[0, :, lanes] = jnp.cos(colatitude)
        geo_ref[1, :, lanes] = (math.pi / (2 * half + 0.5) * math.sqrt(half)) * sine
        scale_ref[:, lanes] = -0.5 * math.log(2.0) + 0.5 * start_sum + wave * jnp.log(sine)


def legendre_block(step, wave, refs, table_ref, mode_count, half):
    prev_ref, cur_ref, scale_ref, inv_ref, geo_ref, rows_ref = refs
    slots = wave.shape[0]
    first = (step * BLOCK).astype(jnp.float32)
    chunks = half // LANES
    lanes = [slice(a * LANES, (a + 1) * LANES) for a in range(chunks)]
    inverse = inv_ref[...]
    prev = [prev_ref[:, s] for s in lanes]
    cur = [cur_ref[:, s] for s in lanes]
    amp = [None] * chunks
    for row in range(BLOCK):
        if row % RENORM == 0:
            for a in range(chunks):
                total = jnp.maximum(jnp.abs(prev[a]) + jnp.abs(cur[a]), 1e-30)
                prev[a] = prev[a] / total
                cur[a] = cur[a] / total
                log_scale = scale_ref[:, lanes[a]] + jnp.log(total)
                scale_ref[:, lanes[a]] = log_scale
                amp[a] = jnp.exp(log_scale) * geo_ref[1, :, lanes[a]]
        for a in range(chunks):
            rows_ref[a, row * slots : (row + 1) * slots, :] = cur[a] * amp[a]
        offset = first + (row + 1.0)
        degree = wave + offset
        numer = 4.0 * degree * degree - 1.0
        denom = offset * (wave + degree)
        root = lax.rsqrt(numer * denom)
        factor = jnp.where(degree < mode_count, numer * root, 0.0)
        ratio = factor * inverse
        inverse = denom * root
        for a in range(chunks):
            following = (factor * geo_ref[0, :, lanes[a]]) * cur[a] - ratio * prev[a]
            prev[a] = cur[a]
            cur[a] = following
    inv_ref[...] = inverse
    for a in range(chunks):
        prev_ref[:, lanes[a]] = prev[a]
        cur_ref[:, lanes[a]] = cur[a]
    out_row = pl.multiple_of(step * (BLOCK // 2), BLOCK // 2)
    for slot in range(slots):
        for parity in range(2):
            for a in range(chunks):
                table_ref[slot, parity, pl.ds(out_row, BLOCK // 2), lanes[a]] = rows_ref[
                    a, pl.ds(parity * slots + slot, BLOCK // 2, stride=2 * slots), :
                ].astype(jnp.bfloat16)


def analyse(grid_fields, waves, order_lanes):
    belts = lax.axis_size("belt")
    lons = lax.axis_size("lon")
    levels, lat_local, lon_local = grid_fields.shape
    owners = belts * lons
    slots = waves.shape[0]
    lat_count = lat_local * belts
    half = lat_count // 2
    lon_count = lon_local * lons
    mode_count = slots * owners
    half_modes = mode_count // 2
    items = levels // lons
    chunk_items = items // CHUNKS
    chunk_rows = chunk_items * lat_local
    group = 2 * lons
    blocks = owners // group
    owner_rows = 2 * slots
    block_rows = group * owner_rows
    rows = 2 * levels
    half_lons = lons // 2
    piece = lat_local // 2
    scale = 1.0 / math.sqrt(lon_count)
    mesh_id = pl.DeviceIdType.MESH
    legendre_steps = mode_count // BLOCK

    def body(
        fields_ref, waves_ref, order_ref, out_ref, dft_ref, leg_ref, rows_in_ref, send_ref, recv_ref, wide_ref,
        prev_ref, cur_ref, scale_ref, inv_ref, geo_ref, step_rows_ref,
        in_send, in_recv, in_local, out_send, out_recv, out_local,
    ):
        belt = lax.axis_index("belt")
        lon = lax.axis_index("lon")
        me = belt * lons + lon
        barrier = pltpu.get_barrier_semaphore()
        refs = (prev_ref, cur_ref, scale_ref, inv_ref, geo_ref, step_rows_ref)

        def lon_away(away):
            high = lax.rem(lon // half_lons + away // half_lons, 2)
            return high * half_lons + lax.rem(lax.rem(lon, half_lons) + lax.rem(away, half_lons), half_lons)

        def place(step):
            away = blocks - 1 - step
            x = lax.rem(belt // 4 + away // 2, blocks // 2)
            return x * 2 + lax.rem(lax.rem(belt // 2, 2) + lax.rem(away, 2), 2)

        def member(index):
            return lax.rem(lax.rem(belt, 2) + index // lons, 2), lon_away(lax.rem(index, lons))

        def gather(chunk, away, item, part):
            target = lon_away(away)
            return pltpu.make_async_remote_copy(
                fields_ref.at[target * items + chunk * chunk_items + item, pl.ds(part * piece, piece)],
                rows_in_ref.at[chunk, lon, pl.ds(item * lat_local + part * piece, piece)],
                in_send.at[chunk],
                in_recv.at[chunk],
                device_id=(belt, target),
                device_id_type=mesh_id,
            )

        def own_rows(chunk, item):
            return pltpu.make_async_copy(
                fields_ref.at[lon * items + chunk * chunk_items + item],
                rows_in_ref.at[chunk, lon, pl.ds(item * lat_local, lat_local)],
                in_local.at[chunk, item],
            )

        def send(chunk, step, index):
            core, target = member(index)
            return pltpu.make_async_remote_copy(
                send_ref.at[chunk, step, core * lons + target],
                recv_ref.at[chunk, me],
                out_send.at[chunk],
                out_recv.at[chunk],
                device_id=(place(step) * 2 + core, target),
                device_id_type=mesh_id,
            )

        def own_block(chunk):
            core, target = member(0)
            return pltpu.make_async_copy(
                send_ref.at[chunk, blocks - 1, core * lons + target], recv_ref.at[chunk, me], out_local.at[chunk]
            )

        def gathered(chunk):
            whole = rows_in_ref.at[chunk, pl.ds(0, lons - 1)]
            return pltpu.make_async_remote_copy(
                whole, whole, in_send.at[chunk], in_recv.at[chunk],
                device_id=(belt, lon_away(1)), device_id_type=mesh_id,
            )

        def exchanged(chunk):
            whole = recv_ref.at[chunk, pl.ds(0, owners - 1)]
            return pltpu.make_async_remote_copy(
                whole, whole, out_send.at[chunk], out_recv.at[chunk],
                device_id=(belt, lon_away(1)), device_id_type=mesh_id,
            )

        def legendre_range(start, stop):
            wave = jnp.broadcast_to(column_of(waves_ref[...], me), (slots, LANES))

            @pl.loop(start, stop)
            def _(step):
                legendre_block(step, wave, refs, leg_ref, mode_count, half)

        def transform(chunk):
            for item in range(chunk_items):
                own_rows(chunk, item).wait()
            gathered(chunk).wait_recv()

            @pl.loop(0, blocks)
            def _(step):
                start = pl.multiple_of(place(step) * block_rows, block_rows)
                total = None
                for part in range(lons):
                    term = lax.dot_general(
                        dft_ref[pl.ds(start, block_rows), part * lon_local : (part + 1) * lon_local],
                        rows_in_ref[chunk, part],
                        NT_DIMS,
                        preferred_element_type=jnp.float32,
                    )
                    total = term if total is None else total + term
                send_ref[chunk, step] = encode(total * scale).reshape(group, owner_rows, chunk_rows)

                @pl.loop(0, group)
                def _(back):
                    index = group - 1 - back

                    @pl.when((step < blocks - 1) | (index > 0))
                    def _():
                        send(chunk, step, index).start()

            own_block(chunk).start()

        def mirror_sums(chunk):
            own_block(chunk).wait()
            exchanged(chunk).wait_recv()
            mirror = (iota((lat_local, lat_local), 0) + iota((lat_local, lat_local), 1)).astype(jnp.float32)
            mirror = jnp.where(mirror == lat_local - 1.0, 1.0, 0.0).astype(jnp.bfloat16)

            @pl.loop(0, belts // 2)
            def _(near):
                far = belts - 1 - near
                for item in range(chunk_items):
                    lanes = slice(item * lat_local, (item + 1) * lat_local)
                    north = decode(recv_ref[chunk, pl.ds(near * lons, lons), :, lanes]).reshape(-1, lat_local)
                    south = decode(recv_ref[chunk, pl.ds(far * lons, lons), :, lanes]).reshape(-1, lat_local)
                    high, low = split(south)
                    south = jnp.dot(high, mirror, preferred_element_type=jnp.float32) + jnp.dot(
                        low, mirror, preferred_element_type=jnp.float32
                    )
                    wide_ref[0, near, chunk * chunk_items + item] = north + south
                    wide_ref[1, near, chunk * chunk_items + item] = north - south

        @pl.loop(1, owners)
        def _(away):
            peer = lax.rem(me + away, owners)
            pl.semaphore_signal(
                barrier, inc=1, device_id=(peer // lons, lax.rem(peer, lons)), device_id_type=mesh_id
            )

        for chunk in range(CHUNKS):
            for item in range(chunk_items):
                own_rows(chunk, item).start()
        start_legendre(
            jnp.broadcast_to(column_of(waves_ref[...], me), (slots, LANES)), refs, mode_count, half
        )
        pl.semaphore_wait(barrier, owners - 1)

        @pl.loop(0, CHUNKS * chunk_items * 2)
        def _(index):
            chunk = index // (2 * chunk_items)
            item = lax.rem(index // 2, chunk_items)

            @pl.loop(1, lons)
            def _(away):
                gather(chunk, lons - away, item, lax.rem(index, 2)).start()

        fill_table(waves_ref, dft_ref, slots, owners, lon_count)
        legendre_range(0, EARLY)
        transform(0)
        legendre_range(EARLY, legendre_steps)
        transform(1)
        mirror_sums(0)
        mirror_sums(1)

        source = iota((2 * rows, 2 * rows), 0)
        target = iota((2 * rows, 2 * rows), 1)
        within = lax.rem(source, rows)
        level = lax.rem(within // 2, lons) * items + within // (2 * lons)
        match = (
            (level == order_ref[...])
            & (lax.rem(within, 2) == lax.rem(target, rows) // levels)
            & (source // rows == target // rows)
        )
        order = jnp.where(match, 1.0, 0.0).T.astype(jnp.bfloat16)

        @pl.loop(0, slots)
        def _(slot):
            for parity in range(2):
                value = jnp.concatenate(
                    [
                        jnp.concatenate(
                            [
                                wide_ref[parity, near, item, pl.ds(slot, 2 * lons, stride=slots), :]
                                for item in range(items)
                            ],
                            axis=0,
                        )
                        for near in range(belts // 2)
                    ],
                    axis=1,
                )
                sums = jnp.dot(
                    order, jnp.concatenate(split(value), axis=0), preferred_element_type=jnp.float32
                ).astype(jnp.bfloat16)
                result = lax.dot_general(sums, leg_ref[slot, parity], NT_DIMS, preferred_element_type=jnp.float32)
                out_ref[slot, :, parity * half_modes : (parity + 1) * half_modes] = result[:rows] + result[rows:]

        for chunk in range(CHUNKS):
            gathered(chunk).wait_send()
            exchanged(chunk).wait_send()

    dma = pltpu.SemaphoreType.DMA
    return pl.pallas_call(
        body,
        name="analyse",
        in_specs=[
            pl.BlockSpec(memory_space=pl.ANY),
            pl.BlockSpec(memory_space=pltpu.VMEM),
            pl.BlockSpec(memory_space=pltpu.VMEM),
        ],
        out_specs=pl.BlockSpec(memory_space=pltpu.VMEM),
        out_shape=jax.ShapeDtypeStruct((slots, rows, mode_count), jnp.float32),
        scratch_shapes=[
            pltpu.VMEM((owners * owner_rows, lon_count), jnp.bfloat16),
            pltpu.VMEM((slots, 2, half_modes, half), jnp.bfloat16),
            pltpu.VMEM((CHUNKS, lons, chunk_rows, lon_local), jnp.bfloat16),
            pltpu.VMEM((CHUNKS, blocks, group, owner_rows, chunk_rows), jnp.int16),
            pltpu.VMEM((CHUNKS, owners, owner_rows, chunk_rows), jnp.int16),
            pltpu.VMEM((2, belts // 2, items, 2 * lons * slots, lat_local), jnp.float32),
            pltpu.VMEM((slots, half), jnp.float32),
            pltpu.VMEM((slots, half), jnp.float32),
            pltpu.VMEM((slots, half), jnp.float32),
            pltpu.VMEM((slots, LANES), jnp.float32),
            pltpu.VMEM((2, slots, half), jnp.float32),
            pltpu.VMEM((half // LANES, BLOCK * slots, LANES), jnp.float32),
            dma((CHUNKS,)),
            dma((CHUNKS,)),
            dma((CHUNKS, chunk_items)),
            dma((CHUNKS,)),
            dma((CHUNKS,)),
            dma((CHUNKS,)),
        ],
        compiler_params=pltpu.CompilerParams(
            collective_id=0, has_side_effects=True, vmem_limit_bytes=60 << 20
        ),
    )(grid_fields, waves, order_lanes)


def on_device(grid_fields, field_order, wave_order):
    owners = lax.axis_size("belt") * lax.axis_size("lon")
    mode_count = wave_order.shape[0]
    slots = mode_count // owners
    levels = grid_fields.shape[0]
    waves = wave_order.astype(jnp.float32).reshape(owners, slots).T
    spectral = analyse(grid_fields, waves, jnp.tile(field_order.astype(jnp.int32), 4)[None, :])
    return spectral.reshape(slots, 2, levels, 2, mode_count // 2)


def solution(mesh):
    return jax.shard_map(
        on_device,
        mesh=mesh,
        in_specs=(P(None, "belt", "lon"), P(), P()),
        out_specs=P(("belt", "lon"), None, None, None, None),
        check_vma=False,
    )
```

```python
import math

import jax
import jax.numpy as jnp
from jax import lax
from jax.experimental import pallas as pl
from jax.experimental.pallas import tpu as pltpu
from jax.sharding import PartitionSpec as P

LANES = 128
NT_DIMS = (((1,), (1,)), ((), ()))

CODE_STEPS = 1024.0
CODE_LOW = -20.0

CHUNKS = 2
BLOCK = 32
RENORM = 16
EARLY = 19


def encode(value):
    magnitude = jnp.abs(value)
    exponent = jnp.floor(jnp.log(jnp.maximum(magnitude, 2.0**CODE_LOW)) * (1.0 / math.log(2.0)))
    exponent = jnp.maximum(exponent, CODE_LOW)
    code = jnp.round(((exponent - CODE_LOW) + magnitude * jnp.exp2(-exponent)) * CODE_STEPS)
    return jnp.where(value < 0.0, -code, code).astype(jnp.int32).astype(jnp.int16)


def decode(code):
    level = code.astype(jnp.int32).astype(jnp.float32) * (1.0 / CODE_STEPS)
    magnitude = jnp.abs(level)
    octave = jnp.maximum(jnp.floor(magnitude), 1.0)
    value = (magnitude - octave + 1.0) * jnp.exp2(octave + (CODE_LOW - 1.0))
    return jnp.where(level < 0.0, -value, value)


def split(value):
    high = value.astype(jnp.bfloat16)
    return high, (value - high.astype(jnp.float32)).astype(jnp.bfloat16)


def iota(shape, dim):
    return lax.broadcasted_iota(jnp.int32, shape, dim)


def column_of(waves, owner, slots):
    waves = waves.astype(jnp.float32)
    per_row = LANES // slots
    row = jnp.sum(jnp.where(iota(waves.shape, 0) == owner // per_row, waves, 0.0), axis=0, keepdims=True)
    shape = (slots, LANES)
    mine = iota(shape, 1) == lax.rem(owner, per_row) * slots + iota(shape, 0)
    return jnp.sum(jnp.where(mine, jnp.broadcast_to(row, shape), 0.0), axis=1, keepdims=True)


def fill_table(waves_ref, table_ref, slots, owners, lon_count):
    quarter = lon_count // 4
    coarse_count = quarter // LANES
    lane = iota((slots, LANES), 1)
    steps = (lane, lax.rem(lane, coarse_count) * LANES)

    def one_owner(owner):
        wave = jnp.broadcast_to(column_of(waves_ref[...], owner, slots), (slots, LANES)).astype(jnp.int32)
        angles = [
            lax.rem(wave * step, lon_count).astype(jnp.float32) * (2.0 * math.pi / lon_count) for step in steps
        ]
        cos_fine, cos_coarse = [jnp.cos(angle) for angle in angles]
        sin_fine, sin_coarse = [jnp.sin(angle) for angle in angles]
        turn = lax.rem(wave, 4).astype(jnp.float32)
        turn = jnp.concatenate((turn, turn), axis=0)
        one = jnp.ones_like(turn)
        zero = jnp.zeros_like(turn)
        keep = jnp.where(turn == 0.0, one, jnp.where(turn == 2.0, -one, zero)).astype(jnp.bfloat16)
        swap = jnp.where(turn == 1.0, -one, jnp.where(turn == 3.0, one, zero)).astype(jnp.bfloat16)
        opposite = jnp.where((turn == 1.0) | (turn == 3.0), -one, one).astype(jnp.bfloat16)
        row = pl.multiple_of(owner * 2 * slots, 2 * slots)
        for a in range(coarse_count):
            ca = cos_coarse[:, a : a + 1]
            sa = sin_coarse[:, a : a + 1]
            cosine = ca * cos_fine - sa * sin_fine
            sine = sa * cos_fine + ca * sin_fine
            plain = jnp.concatenate((cosine, -sine), axis=0).astype(jnp.bfloat16)
            other = jnp.concatenate((sine, cosine), axis=0).astype(jnp.bfloat16)
            turned = plain * keep + other * swap
            for index, value in enumerate((plain, turned, plain * opposite, turned * opposite)):
                start = index * quarter + a * LANES
                table_ref[pl.ds(row, 2 * slots), start : start + LANES] = value

    @pl.loop(0, owners // 2)
    def _(pair):
        one_owner(2 * pair)
        one_owner(2 * pair + 1)


def start_legendre(wave, refs, mode_count, half):
    prev_ref, cur_ref, scale_ref, inv_ref, geo_ref, _ = refs
    lane = iota(wave.shape, 1).astype(jnp.float32)
    terms = None
    for a in range(mode_count // LANES):
        index = lane + (a * LANES + 1.0)
        term = jnp.where(index <= wave, jnp.log1p(0.5 / index), 0.0)
        terms = term if terms is None else terms + term
    start_sum = jnp.sum(terms, axis=1, keepdims=True)
    prev_ref[...] = jnp.zeros_like(prev_ref)
    cur_ref[...] = jnp.ones_like(cur_ref)
    inv_ref[...] = jnp.zeros_like(inv_ref)
    for a in range(half // LANES):
        lanes = slice(a * LANES, (a + 1) * LANES)
        colatitude = (math.pi / (2 * half + 0.5)) * (lane + (a * LANES + 0.75))
        sine = jnp.sin(colatitude)
        geo_ref[0, :, lanes] = jnp.cos(colatitude)
        geo_ref[1, :, lanes] = (math.pi / (2 * half + 0.5) * math.sqrt(half)) * sine
        scale_ref[:, lanes] = -0.5 * math.log(2.0) + 0.5 * start_sum + wave * jnp.log(sine)


def legendre_block(step, wave, refs, table_ref, mode_count, half):
    prev_ref, cur_ref, scale_ref, inv_ref, geo_ref, rows_ref = refs
    slots = wave.shape[0]
    first = (step * BLOCK).astype(jnp.float32)
    chunks = half // LANES
    lanes = [slice(a * LANES, (a + 1) * LANES) for a in range(chunks)]
    inverse = inv_ref[...]
    prev = [prev_ref[:, s] for s in lanes]
    cur = [cur_ref[:, s] for s in lanes]
    amp = [None] * chunks
    for row in range(BLOCK):
        if row % RENORM == 0:
            for a in range(chunks):
                total = jnp.maximum(jnp.abs(prev[a]) + jnp.abs(cur[a]), 1e-30)
                prev[a] = prev[a] / total
                cur[a] = cur[a] / total
                log_scale = scale_ref[:, lanes[a]] + jnp.log(total)
                scale_ref[:, lanes[a]] = log_scale
                amp[a] = jnp.exp(log_scale) * geo_ref[1, :, lanes[a]]
        for a in range(chunks):
            rows_ref[a, row * slots : (row + 1) * slots, :] = cur[a] * amp[a]
        offset = first + (row + 1.0)
        degree = wave + offset
        numer = 4.0 * degree * degree - 1.0
        denom = offset * (wave + degree)
        root = lax.rsqrt(numer * denom)
        factor = jnp.where(degree < mode_count, numer * root, 0.0)
        ratio = factor * inverse
        inverse = denom * root
        for a in range(chunks):
            following = (factor * geo_ref[0, :, lanes[a]]) * cur[a] - ratio * prev[a]
            prev[a] = cur[a]
            cur[a] = following
    inv_ref[...] = inverse
    for a in range(chunks):
        prev_ref[:, lanes[a]] = prev[a]
        cur_ref[:, lanes[a]] = cur[a]
    out_row = pl.multiple_of(step * (BLOCK // 2), BLOCK // 2)
    for slot in range(slots):
        for parity in range(2):
            for a in range(chunks):
                table_ref[slot, parity, pl.ds(out_row, BLOCK // 2), lanes[a]] = rows_ref[
                    a, pl.ds(parity * slots + slot, BLOCK // 2, stride=2 * slots), :
                ].astype(jnp.bfloat16)


def analyse(grid_fields, waves, field_order):
    belts = lax.axis_size("belt")
    lons = lax.axis_size("lon")
    levels, lat_local, lon_local = grid_fields.shape
    owners = belts * lons
    mode_count = waves.shape[0] * waves.shape[1]
    slots = mode_count // owners
    lat_count = lat_local * belts
    half = lat_count // 2
    lon_count = lon_local * lons
    half_modes = mode_count // 2
    items = levels // lons
    chunk_items = items // CHUNKS
    chunk_rows = chunk_items * lat_local
    group = 2 * lons
    blocks = owners // group
    owner_rows = 2 * slots
    block_rows = group * owner_rows
    rows = 2 * levels
    half_lons = lons // 2
    side_belts = belts // 4
    piece = lat_local // 2
    scale = 1.0 / math.sqrt(lon_count)
    mesh_id = pl.DeviceIdType.MESH
    legendre_steps = mode_count // BLOCK

    def body(
        fields_ref, waves_ref, order_ref, out_ref, dft_ref, leg_ref, rows_in_ref, send_ref, recv_ref, wide_ref, sum_ref,
        prev_ref, cur_ref, scale_ref, inv_ref, geo_ref, step_rows_ref,
        in_send, in_recv, in_local, out_send, out_recv, out_local, ready,
    ):
        belt = lax.axis_index("belt")
        lon = lax.axis_index("lon")
        me = belt * lons + lon
        barrier = pltpu.get_barrier_semaphore()
        refs = (prev_ref, cur_ref, scale_ref, inv_ref, geo_ref, step_rows_ref)

        def lon_away(away):
            high = lax.rem(lon // half_lons + away // half_lons, 2)
            return high * half_lons + lax.rem(lax.rem(lon, half_lons) + lax.rem(away, half_lons), half_lons)

        side = lax.rem((belt // 4 + 1) // 2, 2)

        def place(step):
            turn = step // 2
            high = lax.rem(belt // 8 + lax.rem(turn + 1, 2), 2)
            low = lax.rem(lax.rem(belt // 4, 2) + lax.rem((turn + 1) // 2, 2), 2)
            return high * 4 + low * 2 + lax.rem(lax.rem(belt // 2, 2) + lax.rem(step + 1, 2), 2)

        def member(index):
            return lax.rem(lax.rem(belt, 2) + index // lons, 2), lon_away(lax.rem(index, lons))

        def gather(chunk, away, item, part):
            target = lon_away(away)
            return pltpu.make_async_remote_copy(
                fields_ref.at[target * items + chunk * chunk_items + item, pl.ds(part * piece, piece)],
                rows_in_ref.at[chunk, lon, pl.ds(item * lat_local + part * piece, piece)],
                in_send.at[chunk],
                in_recv.at[chunk],
                device_id=(belt, target),
                device_id_type=mesh_id,
            )

        def own_rows(chunk, item):
            return pltpu.make_async_copy(
                fields_ref.at[lon * items + chunk * chunk_items + item],
                rows_in_ref.at[chunk, lon, pl.ds(item * lat_local, lat_local)],
                in_local.at[chunk, item],
            )

        def send(chunk, step, index):
            core, target = member(index)
            return pltpu.make_async_remote_copy(
                send_ref.at[chunk, step, core * lons + target],
                recv_ref.at[chunk, me],
                out_send.at[chunk],
                out_recv.at[chunk, side],
                device_id=(place(step) * 2 + core, target),
                device_id_type=mesh_id,
            )

        def own_block(chunk):
            core, target = member(0)
            return pltpu.make_async_copy(
                send_ref.at[chunk, blocks - 1, core * lons + target], recv_ref.at[chunk, me], out_local.at[chunk]
            )

        def gathered(chunk):
            whole = rows_in_ref.at[chunk, pl.ds(0, lons - 1)]
            return pltpu.make_async_remote_copy(
                whole, whole, in_send.at[chunk], in_recv.at[chunk],
                device_id=(belt, lon_away(1)), device_id_type=mesh_id,
            )

        def exchanged(chunk, from_side, count):
            whole = recv_ref.at[chunk, pl.ds(0, count)]
            return pltpu.make_async_remote_copy(
                whole, whole, out_send.at[chunk], out_recv.at[chunk, from_side],
                device_id=(belt, lon_away(1)), device_id_type=mesh_id,
            )

        def legendre_range(start, stop):
            wave = jnp.broadcast_to(column_of(waves_ref[...], me, slots), (slots, LANES))

            @pl.loop(start, stop)
            def _(step):
                legendre_block(step, wave, refs, leg_ref, mode_count, half)

        def transform(chunk):
            for item in range(chunk_items):
                own_rows(chunk, item).wait()
            gathered(chunk).wait_recv()

            @pl.loop(0, blocks)
            def _(step):
                start = pl.multiple_of(place(step) * block_rows, block_rows)
                total = None
                for part in range(lons):
                    term = lax.dot_general(
                        dft_ref[pl.ds(start, block_rows), part * lon_local : (part + 1) * lon_local],
                        rows_in_ref[chunk, part],
                        NT_DIMS,
                        preferred_element_type=jnp.float32,
                    )
                    total = term if total is None else total + term
                send_ref[chunk, step] = encode(total * scale).reshape(group, owner_rows, chunk_rows)

                @pl.loop(0, group)
                def _(back):
                    index = group - 1 - back

                    @pl.when((step < blocks - 1) | (index > 0))
                    def _():
                        send(chunk, step, index).start()

            own_block(chunk).start()

        def mirror_sums(chunk, from_side):
            mirror = (iota((lat_local, lat_local), 0) + iota((lat_local, lat_local), 1)).astype(jnp.float32)
            mirror = jnp.where(mirror == lat_local - 1.0, 1.0, 0.0).astype(jnp.bfloat16)

            @pl.loop(0, side_belts)
            def _(index):
                near = from_side * side_belts + index
                far = belts - 1 - near
                for item in range(chunk_items):
                    lanes = slice(item * lat_local, (item + 1) * lat_local)
                    north = decode(recv_ref[chunk, pl.ds(near * lons, lons), :, lanes]).reshape(-1, lat_local)
                    south = decode(recv_ref[chunk, pl.ds(far * lons, lons), :, lanes]).reshape(-1, lat_local)
                    high, low = split(south)
                    south = jnp.dot(high, mirror, preferred_element_type=jnp.float32) + jnp.dot(
                        low, mirror, preferred_element_type=jnp.float32
                    )
                    wide_ref[0, near, chunk * chunk_items + item] = north + south
                    wide_ref[1, near, chunk * chunk_items + item] = north - south

        def project(from_side, order, emit):
            start = pl.multiple_of(from_side * side_belts * lat_local, LANES)

            @pl.loop(0, slots)
            def _(slot):
                for parity in range(2):
                    value = jnp.concatenate(
                        [
                            jnp.concatenate(
                                [
                                    wide_ref[
                                        parity, from_side * side_belts + near, item,
                                        pl.ds(slot, 2 * lons, stride=slots), :,
                                    ]
                                    for item in range(items)
                                ],
                                axis=0,
                            )
                            for near in range(side_belts)
                        ],
                        axis=1,
                    )
                    sums = jnp.dot(
                        order, jnp.concatenate(split(value), axis=0), preferred_element_type=jnp.float32
                    ).astype(jnp.bfloat16)
                    result = lax.dot_general(
                        sums,
                        leg_ref[slot, parity, :, pl.ds(start, side_belts * lat_local)],
                        NT_DIMS,
                        preferred_element_type=jnp.float32,
                    )
                    emit(slot, parity, result[:rows] + result[rows:])

        def belt_peers(semaphore):
            @pl.loop(1, belts)
            def _(away):
                peer = (lax.rem(belt + away, belts), lon)
                pl.semaphore_signal(semaphore, inc=1, device_id=peer, device_id_type=mesh_id)

        @pl.loop(1, lons)
        def _(away):
            pl.semaphore_signal(barrier, inc=1, device_id=(belt, lon_away(away)), device_id_type=mesh_id)

        belt_peers(barrier)

        for chunk in range(CHUNKS):
            for item in range(chunk_items):
                own_rows(chunk, item).start()
        start_legendre(
            jnp.broadcast_to(column_of(waves_ref[...], me, slots), (slots, LANES)), refs, mode_count, half
        )
        pl.semaphore_wait(barrier, lons + belts - 2)

        @pl.loop(0, CHUNKS * chunk_items * 2)
        def _(index):
            chunk = index // (2 * chunk_items)
            item = lax.rem(index // 2, chunk_items)

            @pl.loop(1, lons)
            def _(away):
                gather(chunk, lons - away, item, lax.rem(index, 2)).start()

        belt_peers(ready)
        fill_table(waves_ref, dft_ref, slots, owners, lon_count)
        legendre_range(0, EARLY)
        pl.semaphore_wait(ready, belts - 1)
        transform(0)
        legendre_range(EARLY, legendre_steps)
        transform(1)

        source = iota((2 * rows, 2 * rows), 0)
        target = iota((2 * rows, 2 * rows), 1)
        wanted = jnp.zeros((1, 2 * rows), jnp.int32)
        for index in range(levels):
            wanted = jnp.where(lax.rem(iota((1, 2 * rows), 1), levels) == index, order_ref[index], wanted)
        within = lax.rem(source, rows)
        level = lax.rem(within // 2, lons) * items + within // (2 * lons)
        match = (
            (level == wanted)
            & (lax.rem(within, 2) == lax.rem(target, rows) // levels)
            & (source // rows == target // rows)
        )
        order = jnp.where(match, 1.0, 0.0).T.astype(jnp.bfloat16)

        other_count = owners // 2
        for chunk in range(CHUNKS):
            exchanged(chunk, 1 - side, other_count).wait_recv()
            mirror_sums(chunk, 1 - side)
            if chunk < CHUNKS - 1:
                own_block(chunk).wait()
                exchanged(chunk, side, other_count - 1).wait_recv()
                mirror_sums(chunk, side)

        def keep(slot, parity, value):
            sum_ref[slot, parity] = value

        def finish(slot, parity, value):
            out_ref[slot, :, parity, :] = sum_ref[slot, parity] + value

        project(1 - side, order, keep)
        own_block(CHUNKS - 1).wait()
        exchanged(CHUNKS - 1, side, other_count - 1).wait_recv()
        mirror_sums(CHUNKS - 1, side)
        project(side, order, finish)

        for chunk in range(CHUNKS):
            gathered(chunk).wait_send()
            exchanged(chunk, side, owners - 1).wait_send()

    dma = pltpu.SemaphoreType.DMA
    return pl.pallas_call(
        body,
        name="analyse",
        in_specs=[
            pl.BlockSpec(memory_space=pl.ANY),
            pl.BlockSpec(memory_space=pltpu.VMEM),
            pl.BlockSpec(memory_space=pltpu.SMEM),
        ],
        out_specs=pl.BlockSpec(memory_space=pltpu.VMEM),
        out_shape=jax.ShapeDtypeStruct((slots, rows, 2, half_modes), jnp.float32),
        scratch_shapes=[
            pltpu.VMEM((owners * owner_rows, lon_count), jnp.bfloat16),
            pltpu.VMEM((slots, 2, half_modes, half), jnp.bfloat16),
            pltpu.VMEM((CHUNKS, lons, chunk_rows, lon_local), jnp.bfloat16),
            pltpu.VMEM((CHUNKS, blocks, group, owner_rows, chunk_rows), jnp.int16),
            pltpu.VMEM((CHUNKS, owners, owner_rows, chunk_rows), jnp.int16),
            pltpu.VMEM((2, belts // 2, items, 2 * lons * slots, lat_local), jnp.float32),
            pltpu.VMEM((slots, 2, rows, half_modes), jnp.float32),
            pltpu.VMEM((slots, half), jnp.float32),
            pltpu.VMEM((slots, half), jnp.float32),
            pltpu.VMEM((slots, half), jnp.float32),
            pltpu.VMEM((slots, LANES), jnp.float32),
            pltpu.VMEM((2, slots, half), jnp.float32),
            pltpu.VMEM((half // LANES, BLOCK * slots, LANES), jnp.float32),
            dma((CHUNKS,)),
            dma((CHUNKS,)),
            dma((CHUNKS, chunk_items)),
            dma((CHUNKS,)),
            dma((CHUNKS, 2)),
            dma((CHUNKS,)),
            pltpu.SemaphoreType.REGULAR,
        ],
        compiler_params=pltpu.CompilerParams(
            collective_id=0, has_side_effects=True, vmem_limit_bytes=60 << 20
        ),
    )(grid_fields, waves, field_order)


def on_device(grid_fields, field_order, wave_order):
    owners = lax.axis_size("belt") * lax.axis_size("lon")
    mode_count = wave_order.shape[0]
    slots = mode_count // owners
    levels = grid_fields.shape[0]
    waves = wave_order.astype(jnp.int32).reshape(mode_count // LANES, LANES)
    spectral = analyse(grid_fields, waves, field_order.astype(jnp.int32))
    return spectral.reshape(slots, 2, levels, 2, mode_count // 2)


def solution(mesh):
    return jax.shard_map(
        on_device,
        mesh=mesh,
        in_specs=(P(None, "belt", "lon"), P(), P()),
        out_specs=P(("belt", "lon"), None, None, None, None),
        check_vma=False,
    )
```

```python
import math

import jax
import jax.numpy as jnp
from jax import lax
from jax.experimental import pallas as pl
from jax.experimental.pallas import tpu as pltpu
from jax.sharding import PartitionSpec as P

LANES = 128
NT_DIMS = (((1,), (1,)), ((), ()))

CODE_STEPS = 1024.0
CODE_LOW = -20.0

CHUNKS = 2
BLOCK = 32
RENORM = 16
EARLY = 19


def encode(value):
    magnitude = jnp.abs(value)
    exponent = jnp.floor(jnp.log(jnp.maximum(magnitude, 2.0**CODE_LOW)) * (1.0 / math.log(2.0)))
    exponent = jnp.maximum(exponent, CODE_LOW)
    code = jnp.round(((exponent - CODE_LOW) + magnitude * jnp.exp2(-exponent)) * CODE_STEPS)
    return jnp.where(value < 0.0, -code, code).astype(jnp.int32).astype(jnp.int16)


def decode(code):
    level = code.astype(jnp.int32).astype(jnp.float32) * (1.0 / CODE_STEPS)
    magnitude = jnp.abs(level)
    octave = jnp.maximum(jnp.floor(magnitude), 1.0)
    value = (magnitude - octave + 1.0) * jnp.exp2(octave + (CODE_LOW - 1.0))
    return jnp.where(level < 0.0, -value, value)


def split(value):
    high = value.astype(jnp.bfloat16)
    return high, (value - high.astype(jnp.float32)).astype(jnp.bfloat16)


def iota(shape, dim):
    return lax.broadcasted_iota(jnp.int32, shape, dim)


def column_of(waves, owner, slots):
    waves = waves.astype(jnp.float32)
    per_row = LANES // slots
    row = jnp.sum(jnp.where(iota(waves.shape, 0) == owner // per_row, waves, 0.0), axis=0, keepdims=True)
    shape = (slots, LANES)
    mine = iota(shape, 1) == lax.rem(owner, per_row) * slots + iota(shape, 0)
    return jnp.sum(jnp.where(mine, jnp.broadcast_to(row, shape), 0.0), axis=1, keepdims=True)


def fill_table(waves_ref, table_ref, slots, owners, lon_count):
    quarter = lon_count // 4
    coarse_count = quarter // LANES
    lane = iota((slots, LANES), 1)
    steps = (lane, lax.rem(lane, coarse_count) * LANES)

    def one_owner(owner):
        wave = jnp.broadcast_to(column_of(waves_ref[...], owner, slots), (slots, LANES)).astype(jnp.int32)
        angles = [
            lax.rem(wave * step, lon_count).astype(jnp.float32) * (2.0 * math.pi / lon_count) for step in steps
        ]
        cos_fine, cos_coarse = [jnp.cos(angle) for angle in angles]
        sin_fine, sin_coarse = [jnp.sin(angle) for angle in angles]
        turn = lax.rem(wave, 4).astype(jnp.float32)
        turn = jnp.concatenate((turn, turn), axis=0)
        one = jnp.ones_like(turn)
        zero = jnp.zeros_like(turn)
        keep = jnp.where(turn == 0.0, one, jnp.where(turn == 2.0, -one, zero)).astype(jnp.bfloat16)
        swap = jnp.where(turn == 1.0, -one, jnp.where(turn == 3.0, one, zero)).astype(jnp.bfloat16)
        opposite = jnp.where((turn == 1.0) | (turn == 3.0), -one, one).astype(jnp.bfloat16)
        row = pl.multiple_of(owner * 2 * slots, 2 * slots)
        for a in range(coarse_count):
            ca = cos_coarse[:, a : a + 1]
            sa = sin_coarse[:, a : a + 1]
            cosine = ca * cos_fine - sa * sin_fine
            sine = sa * cos_fine + ca * sin_fine
            plain = jnp.concatenate((cosine, -sine), axis=0).astype(jnp.bfloat16)
            other = jnp.concatenate((sine, cosine), axis=0).astype(jnp.bfloat16)
            turned = plain * keep + other * swap
            for index, value in enumerate((plain, turned, plain * opposite, turned * opposite)):
                start = index * quarter + a * LANES
                table_ref[pl.ds(row, 2 * slots), start : start + LANES] = value

    @pl.loop(0, owners // 2)
    def _(pair):
        one_owner(2 * pair)
        one_owner(2 * pair + 1)


def start_legendre(wave, refs, mode_count, half):
    prev_ref, cur_ref, scale_ref, inv_ref, geo_ref, _ = refs
    lane = iota(wave.shape, 1).astype(jnp.float32)
    terms = None
    for a in range(mode_count // LANES):
        index = lane + (a * LANES + 1.0)
        term = jnp.where(index <= wave, jnp.log1p(0.5 / index), 0.0)
        terms = term if terms is None else terms + term
    start_sum = jnp.sum(terms, axis=1, keepdims=True)
    prev_ref[...] = jnp.zeros_like(prev_ref)
    cur_ref[...] = jnp.ones_like(cur_ref)
    inv_ref[...] = jnp.zeros_like(inv_ref)
    for a in range(half // LANES):
        lanes = slice(a * LANES, (a + 1) * LANES)
        colatitude = (math.pi / (2 * half + 0.5)) * (lane + (a * LANES + 0.75))
        sine = jnp.sin(colatitude)
        geo_ref[0, :, lanes] = jnp.cos(colatitude)
        geo_ref[1, :, lanes] = (math.pi / (2 * half + 0.5) * math.sqrt(half)) * sine
        scale_ref[:, lanes] = -0.5 * math.log(2.0) + 0.5 * start_sum + wave * jnp.log(sine)


def legendre_block(step, wave, refs, table_ref, mode_count, half):
    prev_ref, cur_ref, scale_ref, inv_ref, geo_ref, rows_ref = refs
    slots = wave.shape[0]
    first = (step * BLOCK).astype(jnp.float32)
    chunks = half // LANES
    lanes = [slice(a * LANES, (a + 1) * LANES) for a in range(chunks)]
    inverse = inv_ref[...]
    prev = [prev_ref[:, s] for s in lanes]
    cur = [cur_ref[:, s] for s in lanes]
    amp = [None] * chunks
    for row in range(BLOCK):
        if row % RENORM == 0:
            for a in range(chunks):
                total = jnp.maximum(jnp.abs(prev[a]) + jnp.abs(cur[a]), 1e-30)
                prev[a] = prev[a] / total
                cur[a] = cur[a] / total
                log_scale = scale_ref[:, lanes[a]] + jnp.log(total)
                scale_ref[:, lanes[a]] = log_scale
                amp[a] = jnp.exp(log_scale) * geo_ref[1, :, lanes[a]]
        for a in range(chunks):
            rows_ref[a, row * slots : (row + 1) * slots, :] = cur[a] * amp[a]
        offset = first + (row + 1.0)
        degree = wave + offset
        numer = 4.0 * degree * degree - 1.0
        denom = offset * (wave + degree)
        root = lax.rsqrt(numer * denom)
        factor = jnp.where(degree < mode_count, numer * root, 0.0)
        ratio = factor * inverse
        inverse = denom * root
        for a in range(chunks):
            following = (factor * geo_ref[0, :, lanes[a]]) * cur[a] - ratio * prev[a]
            prev[a] = cur[a]
            cur[a] = following
    inv_ref[...] = inverse
    for a in range(chunks):
        prev_ref[:, lanes[a]] = prev[a]
        cur_ref[:, lanes[a]] = cur[a]
    out_row = pl.multiple_of(step * (BLOCK // 2), BLOCK // 2)
    for slot in range(slots):
        for parity in range(2):
            for a in range(chunks):
                table_ref[slot, parity, pl.ds(out_row, BLOCK // 2), lanes[a]] = rows_ref[
                    a, pl.ds(parity * slots + slot, BLOCK // 2, stride=2 * slots), :
                ].astype(jnp.bfloat16)


def analyse(grid_fields, waves, field_order):
    belts = lax.axis_size("belt")
    lons = lax.axis_size("lon")
    levels, lat_local, lon_local = grid_fields.shape
    owners = belts * lons
    mode_count = waves.shape[0] * waves.shape[1]
    slots = mode_count // owners
    lat_count = lat_local * belts
    half = lat_count // 2
    lon_count = lon_local * lons
    half_modes = mode_count // 2
    items = levels // lons
    chunk_items = items // CHUNKS
    chunk_rows = chunk_items * lat_local
    group = 2 * lons
    blocks = owners // group
    owner_rows = 2 * slots
    block_rows = group * owner_rows
    rows = 2 * levels
    half_lons = lons // 2
    side_belts = belts // 4
    piece = lat_local // 2
    scale = 1.0 / math.sqrt(lon_count)
    mesh_id = pl.DeviceIdType.MESH
    legendre_steps = mode_count // BLOCK

    def body(
        fields_ref, waves_in_ref, order_in_ref, out_ref, waves_ref, order_ref, dft_ref, leg_ref, rows_in_ref, send_ref, recv_ref, wide_ref, sum_ref,
        prev_ref, cur_ref, scale_ref, inv_ref, geo_ref, step_rows_ref,
        in_send, in_recv, in_local, out_send, out_recv, out_local, small, ready,
    ):
        belt = lax.axis_index("belt")
        lon = lax.axis_index("lon")
        me = belt * lons + lon
        barrier = pltpu.get_barrier_semaphore()
        refs = (prev_ref, cur_ref, scale_ref, inv_ref, geo_ref, step_rows_ref)

        def lon_away(away):
            high = lax.rem(lon // half_lons + away // half_lons, 2)
            return high * half_lons + lax.rem(lax.rem(lon, half_lons) + lax.rem(away, half_lons), half_lons)

        side = lax.rem((belt // 4 + 1) // 2, 2)

        def place(step):
            turn = step // 2
            high = lax.rem(belt // 8 + lax.rem(turn + 1, 2), 2)
            low = lax.rem(lax.rem(belt // 4, 2) + lax.rem((turn + 1) // 2, 2), 2)
            return high * 4 + low * 2 + lax.rem(lax.rem(belt // 2, 2) + lax.rem(step + 1, 2), 2)

        def member(index):
            return lax.rem(lax.rem(belt, 2) + index // lons, 2), lon_away(lax.rem(index, lons))

        def gather(chunk, away, item, part):
            target = lon_away(away)
            return pltpu.make_async_remote_copy(
                fields_ref.at[target * items + chunk * chunk_items + item, pl.ds(part * piece, piece)],
                rows_in_ref.at[chunk, lon, pl.ds(item * lat_local + part * piece, piece)],
                in_send.at[chunk],
                in_recv.at[chunk],
                device_id=(belt, target),
                device_id_type=mesh_id,
            )

        def own_rows(chunk, item):
            return pltpu.make_async_copy(
                fields_ref.at[lon * items + chunk * chunk_items + item],
                rows_in_ref.at[chunk, lon, pl.ds(item * lat_local, lat_local)],
                in_local.at[chunk, item],
            )

        def send(chunk, step, index):
            core, target = member(index)
            return pltpu.make_async_remote_copy(
                send_ref.at[chunk, step, core * lons + target],
                recv_ref.at[chunk, me],
                out_send.at[chunk],
                out_recv.at[chunk, side],
                device_id=(place(step) * 2 + core, target),
                device_id_type=mesh_id,
            )

        def own_block(chunk):
            core, target = member(0)
            return pltpu.make_async_copy(
                send_ref.at[chunk, blocks - 1, core * lons + target], recv_ref.at[chunk, me], out_local.at[chunk]
            )

        def gathered(chunk):
            whole = rows_in_ref.at[chunk, pl.ds(0, lons - 1)]
            return pltpu.make_async_remote_copy(
                whole, whole, in_send.at[chunk], in_recv.at[chunk],
                device_id=(belt, lon_away(1)), device_id_type=mesh_id,
            )

        def exchanged(chunk, from_side, count):
            whole = recv_ref.at[chunk, pl.ds(0, count)]
            return pltpu.make_async_remote_copy(
                whole, whole, out_send.at[chunk], out_recv.at[chunk, from_side],
                device_id=(belt, lon_away(1)), device_id_type=mesh_id,
            )

        def legendre_range(start, stop):
            wave = jnp.broadcast_to(column_of(waves_ref[...], me, slots), (slots, LANES))

            @pl.loop(start, stop)
            def _(step):
                legendre_block(step, wave, refs, leg_ref, mode_count, half)

        def transform(chunk):
            for item in range(chunk_items):
                own_rows(chunk, item).wait()
            gathered(chunk).wait_recv()

            @pl.loop(0, blocks)
            def _(step):
                start = pl.multiple_of(place(step) * block_rows, block_rows)
                total = None
                for part in range(lons):
                    term = lax.dot_general(
                        dft_ref[pl.ds(start, block_rows), part * lon_local : (part + 1) * lon_local],
                        rows_in_ref[chunk, part],
                        NT_DIMS,
                        preferred_element_type=jnp.float32,
                    )
                    total = term if total is None else total + term
                send_ref[chunk, step] = encode(total * scale).reshape(group, owner_rows, chunk_rows)

                @pl.loop(0, group)
                def _(back):
                    index = group - 1 - back

                    @pl.when((step < blocks - 1) | (index > 0))
                    def _():
                        send(chunk, step, index).start()

            own_block(chunk).start()

        def mirror_sums(chunk, from_side):
            mirror = (iota((lat_local, lat_local), 0) + iota((lat_local, lat_local), 1)).astype(jnp.float32)
            mirror = jnp.where(mirror == lat_local - 1.0, 1.0, 0.0).astype(jnp.bfloat16)

            @pl.loop(0, side_belts, unroll=4)
            def _(index):
                near = from_side * side_belts + index
                far = belts - 1 - near
                for item in range(chunk_items):
                    lanes = slice(item * lat_local, (item + 1) * lat_local)
                    north = decode(recv_ref[chunk, pl.ds(near * lons, lons), :, lanes]).reshape(-1, lat_local)
                    south = decode(recv_ref[chunk, pl.ds(far * lons, lons), :, lanes]).reshape(-1, lat_local)
                    high, low = split(south)
                    south = jnp.dot(high, mirror, preferred_element_type=jnp.float32) + jnp.dot(
                        low, mirror, preferred_element_type=jnp.float32
                    )
                    wide_ref[0, near, chunk * chunk_items + item] = north + south
                    wide_ref[1, near, chunk * chunk_items + item] = north - south

        def project(from_side, order, emit):
            start = pl.multiple_of(from_side * side_belts * lat_local, LANES)

            @pl.loop(0, slots, unroll=4)
            def _(slot):
                for parity in range(2):
                    value = jnp.concatenate(
                        [
                            jnp.concatenate(
                                [
                                    wide_ref[
                                        parity, from_side * side_belts + near, item,
                                        pl.ds(slot, 2 * lons, stride=slots), :,
                                    ]
                                    for item in range(items)
                                ],
                                axis=0,
                            )
                            for near in range(side_belts)
                        ],
                        axis=1,
                    )
                    sums = jnp.dot(
                        order, jnp.concatenate(split(value), axis=0), preferred_element_type=jnp.float32
                    ).astype(jnp.bfloat16)
                    result = lax.dot_general(
                        sums,
                        leg_ref[slot, parity, :, pl.ds(start, side_belts * lat_local)],
                        NT_DIMS,
                        preferred_element_type=jnp.float32,
                    )
                    emit(slot, parity, result[:rows] + result[rows:])

        def belt_peers(semaphore):
            @pl.loop(1, belts)
            def _(away):
                peer = (lax.rem(belt + away, belts), lon)
                pl.semaphore_signal(semaphore, inc=1, device_id=peer, device_id_type=mesh_id)

        @pl.loop(1, lons)
        def _(away):
            pl.semaphore_signal(barrier, inc=1, device_id=(belt, lon_away(away)), device_id_type=mesh_id)

        belt_peers(barrier)
        waves_copy = pltpu.make_async_copy(waves_in_ref, waves_ref, small.at[0])
        order_copy = pltpu.make_async_copy(order_in_ref, order_ref, small.at[1])
        waves_copy.start()
        order_copy.start()

        for chunk in range(CHUNKS):
            for item in range(chunk_items):
                own_rows(chunk, item).start()
        pl.semaphore_wait(barrier, lons + belts - 2)

        @pl.loop(0, CHUNKS * chunk_items * 2)
        def _(index):
            chunk = index // (2 * chunk_items)
            item = lax.rem(index // 2, chunk_items)

            @pl.loop(1, lons)
            def _(away):
                gather(chunk, lons - away, item, lax.rem(index, 2)).start()

        belt_peers(ready)
        waves_copy.wait()
        order_copy.wait()
        start_legendre(
            jnp.broadcast_to(column_of(waves_ref[...], me, slots), (slots, LANES)), refs, mode_count, half
        )
        fill_table(waves_ref, dft_ref, slots, owners, lon_count)
        legendre_range(0, EARLY)
        pl.semaphore_wait(ready, belts - 1)
        transform(0)
        legendre_range(EARLY, legendre_steps)
        transform(1)

        source = iota((2 * rows, 2 * rows), 0)
        target = iota((2 * rows, 2 * rows), 1)
        wanted = jnp.zeros((1, 2 * rows), jnp.int32)
        for index in range(levels):
            wanted = jnp.where(lax.rem(iota((1, 2 * rows), 1), levels) == index, order_ref[index], wanted)
        within = lax.rem(source, rows)
        level = lax.rem(within // 2, lons) * items + within // (2 * lons)
        match = (
            (level == wanted)
            & (lax.rem(within, 2) == lax.rem(target, rows) // levels)
            & (source // rows == target // rows)
        )
        order = jnp.where(match, 1.0, 0.0).T.astype(jnp.bfloat16)

        other_count = owners // 2
        for chunk in range(CHUNKS):
            exchanged(chunk, 1 - side, other_count).wait_recv()
            mirror_sums(chunk, 1 - side)
            if chunk < CHUNKS - 1:
                own_block(chunk).wait()
                exchanged(chunk, side, other_count - 1).wait_recv()
                mirror_sums(chunk, side)

        def keep(slot, parity, value):
            sum_ref[slot, parity] = value

        def finish(slot, parity, value):
            out_ref[slot, :, parity, :] = sum_ref[slot, parity] + value

        project(1 - side, order, keep)
        own_block(CHUNKS - 1).wait()
        exchanged(CHUNKS - 1, side, other_count - 1).wait_recv()
        mirror_sums(CHUNKS - 1, side)
        project(side, order, finish)

        for chunk in range(CHUNKS):
            gathered(chunk).wait_send()
            exchanged(chunk, side, owners - 1).wait_send()

    dma = pltpu.SemaphoreType.DMA
    return pl.pallas_call(
        body,
        name="analyse",
        in_specs=[
            pl.BlockSpec(memory_space=pl.ANY),
            pl.BlockSpec(memory_space=pltpu.HBM),
            pl.BlockSpec(memory_space=pltpu.HBM),
        ],
        out_specs=pl.BlockSpec(memory_space=pltpu.VMEM),
        out_shape=jax.ShapeDtypeStruct((slots, rows, 2, half_modes), jnp.float32),
        scratch_shapes=[
            pltpu.VMEM(waves.shape, jnp.int32),
            pltpu.SMEM(field_order.shape, jnp.int32),
            pltpu.VMEM((owners * owner_rows, lon_count), jnp.bfloat16),
            pltpu.VMEM((slots, 2, half_modes, half), jnp.bfloat16),
            pltpu.VMEM((CHUNKS, lons, chunk_rows, lon_local), jnp.bfloat16),
            pltpu.VMEM((CHUNKS, blocks, group, owner_rows, chunk_rows), jnp.int16),
            pltpu.VMEM((CHUNKS, owners, owner_rows, chunk_rows), jnp.int16),
            pltpu.VMEM((2, belts // 2, items, 2 * lons * slots, lat_local), jnp.float32),
            pltpu.VMEM((slots, 2, rows, half_modes), jnp.float32),
            pltpu.VMEM((slots, half), jnp.float32),
            pltpu.VMEM((slots, half), jnp.float32),
            pltpu.VMEM((slots, half), jnp.float32),
            pltpu.VMEM((slots, LANES), jnp.float32),
            pltpu.VMEM((2, slots, half), jnp.float32),
            pltpu.VMEM((half // LANES, BLOCK * slots, LANES), jnp.float32),
            dma((CHUNKS,)),
            dma((CHUNKS,)),
            dma((CHUNKS, chunk_items)),
            dma((CHUNKS,)),
            dma((CHUNKS, 2)),
            dma((CHUNKS,)),
            dma((2,)),
            pltpu.SemaphoreType.REGULAR,
        ],
        compiler_params=pltpu.CompilerParams(
            collective_id=0, has_side_effects=True, vmem_limit_bytes=51 << 20
        ),
    )(grid_fields, waves, field_order)


def hand_on(value):
    def body(in_ref, out_ref, done):
        copy = pltpu.make_async_copy(in_ref, out_ref, done)
        copy.start()
        copy.wait()

    return pl.pallas_call(
        body,
        name="hand_on",
        in_specs=[pl.BlockSpec(memory_space=pltpu.VMEM)],
        out_specs=pl.BlockSpec(memory_space=pl.ANY),
        out_shape=jax.ShapeDtypeStruct(value.shape, value.dtype),
        scratch_shapes=[pltpu.SemaphoreType.DMA],
        compiler_params=pltpu.CompilerParams(vmem_limit_bytes=4 << 20),
    )(value)


def on_device(grid_fields, field_order, wave_order):
    owners = lax.axis_size("belt") * lax.axis_size("lon")
    mode_count = wave_order.shape[0]
    slots = mode_count // owners
    levels = grid_fields.shape[0]
    waves = wave_order.astype(jnp.int32).reshape(mode_count // LANES, LANES)
    waves = pltpu.with_memory_space_constraint(waves, pltpu.HBM)
    field_order = pltpu.with_memory_space_constraint(field_order.astype(jnp.int32), pltpu.HBM)
    spectral = analyse(grid_fields, waves, field_order)
    return hand_on(spectral).reshape(slots, 2, levels, 2, mode_count // 2)


def solution(mesh):
    return jax.shard_map(
        on_device,
        mesh=mesh,
        in_specs=(P(None, "belt", "lon"), P(), P()),
        out_specs=P(("belt", "lon"), None, None, None, None),
        check_vma=False,
    )
```

```python
import math

import jax
import jax.numpy as jnp
from jax import lax
from jax.experimental import pallas as pl
from jax.experimental.pallas import tpu as pltpu
from jax.sharding import PartitionSpec as P

LANES = 128
NT_DIMS = (((1,), (1,)), ((), ()))

CODE_STEPS = 1024.0
CODE_LOW = -20.0

CHUNKS = 2
PIECES = 4
BLOCK = 32
RENORM = 16
EARLY = 19


def encode(value):
    magnitude = jnp.abs(value)
    exponent = jnp.floor(jnp.log(jnp.maximum(magnitude, 2.0**CODE_LOW)) * (1.0 / math.log(2.0)))
    exponent = jnp.maximum(exponent, CODE_LOW)
    code = jnp.round(((exponent - CODE_LOW) + magnitude * jnp.exp2(-exponent)) * CODE_STEPS)
    return jnp.where(value < 0.0, -code, code).astype(jnp.int32).astype(jnp.int16)


def decode(code):
    level = code.astype(jnp.int32).astype(jnp.float32) * (1.0 / CODE_STEPS)
    magnitude = jnp.abs(level)
    octave = jnp.maximum(jnp.floor(magnitude), 1.0)
    value = (magnitude - octave + 1.0) * jnp.exp2(octave + (CODE_LOW - 1.0))
    return jnp.where(level < 0.0, -value, value)


def split(value):
    high = value.astype(jnp.bfloat16)
    return high, (value - high.astype(jnp.float32)).astype(jnp.bfloat16)


def iota(shape, dim):
    return lax.broadcasted_iota(jnp.int32, shape, dim)


def column_of(waves, owner, slots):
    waves = waves.astype(jnp.float32)
    per_row = LANES // slots
    row = jnp.sum(jnp.where(iota(waves.shape, 0) == owner // per_row, waves, 0.0), axis=0, keepdims=True)
    shape = (slots, LANES)
    mine = iota(shape, 1) == lax.rem(owner, per_row) * slots + iota(shape, 0)
    return jnp.sum(jnp.where(mine, jnp.broadcast_to(row, shape), 0.0), axis=1, keepdims=True)


def fill_table(waves_ref, table_ref, slots, owners, lon_count):
    quarter = lon_count // 4
    coarse_count = quarter // LANES
    lane = iota((slots, LANES), 1)
    steps = (lane, lax.rem(lane, coarse_count) * LANES)

    def one_owner(owner):
        wave = jnp.broadcast_to(column_of(waves_ref[...], owner, slots), (slots, LANES)).astype(jnp.int32)
        angles = [
            lax.rem(wave * step, lon_count).astype(jnp.float32) * (2.0 * math.pi / lon_count) for step in steps
        ]
        cos_fine, cos_coarse = [jnp.cos(angle) for angle in angles]
        sin_fine, sin_coarse = [jnp.sin(angle) for angle in angles]
        turn = lax.rem(wave, 4).astype(jnp.float32)
        turn = jnp.concatenate((turn, turn), axis=0)
        one = jnp.ones_like(turn)
        zero = jnp.zeros_like(turn)
        keep = jnp.where(turn == 0.0, one, jnp.where(turn == 2.0, -one, zero)).astype(jnp.bfloat16)
        swap = jnp.where(turn == 1.0, -one, jnp.where(turn == 3.0, one, zero)).astype(jnp.bfloat16)
        opposite = jnp.where((turn == 1.0) | (turn == 3.0), -one, one).astype(jnp.bfloat16)
        row = pl.multiple_of(owner * 2 * slots, 2 * slots)
        for a in range(coarse_count):
            ca = cos_coarse[:, a : a + 1]
            sa = sin_coarse[:, a : a + 1]
            cosine = ca * cos_fine - sa * sin_fine
            sine = sa * cos_fine + ca * sin_fine
            plain = jnp.concatenate((cosine, -sine), axis=0).astype(jnp.bfloat16)
            other = jnp.concatenate((sine, cosine), axis=0).astype(jnp.bfloat16)
            turned = plain * keep + other * swap
            for index, value in enumerate((plain, turned, plain * opposite, turned * opposite)):
                start = index * quarter + a * LANES
                table_ref[pl.ds(row, 2 * slots), start : start + LANES] = value

    @pl.loop(0, owners // 2)
    def _(pair):
        one_owner(2 * pair)
        one_owner(2 * pair + 1)


def start_legendre(wave, refs, mode_count, half):
    prev_ref, cur_ref, scale_ref, inv_ref, geo_ref, _ = refs
    lane = iota(wave.shape, 1).astype(jnp.float32)
    terms = None
    for a in range(mode_count // LANES):
        index = lane + (a * LANES + 1.0)
        term = jnp.where(index <= wave, jnp.log1p(0.5 / index), 0.0)
        terms = term if terms is None else terms + term
    start_sum = jnp.sum(terms, axis=1, keepdims=True)
    prev_ref[...] = jnp.zeros_like(prev_ref)
    cur_ref[...] = jnp.ones_like(cur_ref)
    inv_ref[...] = jnp.zeros_like(inv_ref)
    for a in range(half // LANES):
        lanes = slice(a * LANES, (a + 1) * LANES)
        colatitude = (math.pi / (2 * half + 0.5)) * (lane + (a * LANES + 0.75))
        sine = jnp.sin(colatitude)
        geo_ref[0, :, lanes] = jnp.cos(colatitude)
        geo_ref[1, :, lanes] = (math.pi / (2 * half + 0.5) * math.sqrt(half)) * sine
        scale_ref[:, lanes] = -0.5 * math.log(2.0) + 0.5 * start_sum + wave * jnp.log(sine)


def legendre_block(step, wave, refs, table_ref, mode_count, half):
    prev_ref, cur_ref, scale_ref, inv_ref, geo_ref, rows_ref = refs
    slots = wave.shape[0]
    first = (step * BLOCK).astype(jnp.float32)
    chunks = half // LANES
    lanes = [slice(a * LANES, (a + 1) * LANES) for a in range(chunks)]
    inverse = inv_ref[...]
    prev = [prev_ref[:, s] for s in lanes]
    cur = [cur_ref[:, s] for s in lanes]
    amp = [None] * chunks
    for row in range(BLOCK):
        if row % RENORM == 0:
            for a in range(chunks):
                total = jnp.maximum(jnp.abs(prev[a]) + jnp.abs(cur[a]), 1e-30)
                prev[a] = prev[a] / total
                cur[a] = cur[a] / total
                log_scale = scale_ref[:, lanes[a]] + jnp.log(total)
                scale_ref[:, lanes[a]] = log_scale
                amp[a] = jnp.exp(log_scale) * geo_ref[1, :, lanes[a]]
        for a in range(chunks):
            rows_ref[a, row * slots : (row + 1) * slots, :] = cur[a] * amp[a]
        offset = first + (row + 1.0)
        degree = wave + offset
        numer = 4.0 * degree * degree - 1.0
        denom = offset * (wave + degree)
        root = lax.rsqrt(numer * denom)
        factor = jnp.where(degree < mode_count, numer * root, 0.0)
        ratio = factor * inverse
        inverse = denom * root
        for a in range(chunks):
            following = (factor * geo_ref[0, :, lanes[a]]) * cur[a] - ratio * prev[a]
            prev[a] = cur[a]
            cur[a] = following
    inv_ref[...] = inverse
    for a in range(chunks):
        prev_ref[:, lanes[a]] = prev[a]
        cur_ref[:, lanes[a]] = cur[a]
    out_row = pl.multiple_of(step * (BLOCK // 2), BLOCK // 2)
    for slot in range(slots):
        for parity in range(2):
            for a in range(chunks):
                table_ref[slot, parity, pl.ds(out_row, BLOCK // 2), lanes[a]] = rows_ref[
                    a, pl.ds(parity * slots + slot, BLOCK // 2, stride=2 * slots), :
                ].astype(jnp.bfloat16)


def analyse(grid_fields, waves, field_order):
    belts = lax.axis_size("belt")
    lons = lax.axis_size("lon")
    levels, lat_local, lon_local = grid_fields.shape
    owners = belts * lons
    mode_count = waves.shape[0] * waves.shape[1]
    slots = mode_count // owners
    lat_count = lat_local * belts
    half = lat_count // 2
    lon_count = lon_local * lons
    half_modes = mode_count // 2
    items = levels // lons
    chunk_items = items // CHUNKS
    chunk_rows = chunk_items * lat_local
    group = 2 * lons
    blocks = owners // group
    owner_rows = 2 * slots
    block_rows = group * owner_rows
    rows = 2 * levels
    half_lons = lons // 2
    side_belts = belts // 4
    piece = lat_local // PIECES
    scale = 1.0 / math.sqrt(lon_count)
    mesh_id = pl.DeviceIdType.MESH
    legendre_steps = mode_count // BLOCK

    def body(
        fields_ref, waves_in_ref, order_in_ref, out_ref, waves_ref, order_ref, dft_ref, leg_ref, rows_in_ref, send_ref, recv_ref, wide_ref, sum_ref,
        prev_ref, cur_ref, scale_ref, inv_ref, geo_ref, step_rows_ref,
        in_send, in_recv, in_local, out_send, out_recv, out_local, small, ready,
    ):
        belt = lax.axis_index("belt")
        lon = lax.axis_index("lon")
        me = belt * lons + lon
        barrier = pltpu.get_barrier_semaphore()
        refs = (prev_ref, cur_ref, scale_ref, inv_ref, geo_ref, step_rows_ref)

        def lon_away(away):
            high = lax.rem(lon // half_lons + away // half_lons, 2)
            return high * half_lons + lax.rem(lax.rem(lon, half_lons) + lax.rem(away, half_lons), half_lons)

        side = lax.rem((belt // 4 + 1) // 2, 2)

        def place(step):
            turn = step // 2
            high = lax.rem(belt // 8 + lax.rem(turn + 1, 2), 2)
            low = lax.rem(lax.rem(belt // 4, 2) + lax.rem((turn + 1) // 2, 2), 2)
            return high * 4 + low * 2 + lax.rem(lax.rem(belt // 2, 2) + lax.rem(step + 1, 2), 2)

        def member(index):
            return lax.rem(lax.rem(belt, 2) + index // lons, 2), lon_away(lax.rem(index, lons))

        def gather(chunk, away, item, part):
            target = lon_away(away)
            return pltpu.make_async_remote_copy(
                fields_ref.at[target * items + chunk * chunk_items + item, pl.ds(part * piece, piece)],
                rows_in_ref.at[chunk, lon, pl.ds(item * lat_local + part * piece, piece)],
                in_send.at[chunk],
                in_recv.at[chunk],
                device_id=(belt, target),
                device_id_type=mesh_id,
            )

        def own_rows(chunk, item):
            return pltpu.make_async_copy(
                fields_ref.at[lon * items + chunk * chunk_items + item],
                rows_in_ref.at[chunk, lon, pl.ds(item * lat_local, lat_local)],
                in_local.at[chunk, item],
            )

        members = [member(index) for index in range(group)]

        def send(chunk, step, block, index):
            core, target = members[index]
            return pltpu.make_async_remote_copy(
                send_ref.at[chunk, step, core * lons + target],
                recv_ref.at[chunk, me],
                out_send.at[chunk],
                out_recv.at[chunk, side],
                device_id=(block * 2 + core, target),
                device_id_type=mesh_id,
            )

        def own_block(chunk):
            core, target = members[0]
            return pltpu.make_async_copy(
                send_ref.at[chunk, blocks - 1, core * lons + target], recv_ref.at[chunk, me], out_local.at[chunk]
            )

        def gathered(chunk):
            whole = rows_in_ref.at[chunk, pl.ds(0, lons - 1)]
            return pltpu.make_async_remote_copy(
                whole, whole, in_send.at[chunk], in_recv.at[chunk],
                device_id=(belt, lon_away(1)), device_id_type=mesh_id,
            )

        def exchanged(chunk, from_side, count):
            whole = recv_ref.at[chunk, pl.ds(0, count)]
            return pltpu.make_async_remote_copy(
                whole, whole, out_send.at[chunk], out_recv.at[chunk, from_side],
                device_id=(belt, lon_away(1)), device_id_type=mesh_id,
            )

        def legendre_range(start, stop):
            wave = jnp.broadcast_to(column_of(waves_ref[...], me, slots), (slots, LANES))

            @pl.loop(start, stop)
            def _(step):
                legendre_block(step, wave, refs, leg_ref, mode_count, half)

        def transform(chunk):
            for item in range(chunk_items):
                own_rows(chunk, item).wait()
            gathered(chunk).wait_recv()

            @pl.loop(0, blocks)
            def _(step):
                block = place(step)
                start = pl.multiple_of(block * block_rows, block_rows)
                total = None
                for part in range(lons):
                    term = lax.dot_general(
                        dft_ref[pl.ds(start, block_rows), part * lon_local : (part + 1) * lon_local],
                        rows_in_ref[chunk, part],
                        NT_DIMS,
                        preferred_element_type=jnp.float32,
                    )
                    total = term if total is None else total + term
                send_ref[chunk, step] = encode(total * scale).reshape(group, owner_rows, chunk_rows)

                for index in range(group - 1, 0, -1):
                    send(chunk, step, block, index).start()

                @pl.when(step < blocks - 1)
                def _():
                    send(chunk, step, block, 0).start()

            own_block(chunk).start()

        def mirror_sums(chunk, from_side):
            mirror = (iota((lat_local, lat_local), 0) + iota((lat_local, lat_local), 1)).astype(jnp.float32)
            mirror = jnp.where(mirror == lat_local - 1.0, 1.0, 0.0).astype(jnp.bfloat16)

            @pl.loop(0, side_belts, unroll=4)
            def _(index):
                near = from_side * side_belts + index
                far = belts - 1 - near
                for item in range(chunk_items):
                    lanes = slice(item * lat_local, (item + 1) * lat_local)
                    north = decode(recv_ref[chunk, pl.ds(near * lons, lons), :, lanes]).reshape(-1, lat_local)
                    south = decode(recv_ref[chunk, pl.ds(far * lons, lons), :, lanes]).reshape(-1, lat_local)
                    high, low = split(south)
                    south = jnp.dot(high, mirror, preferred_element_type=jnp.float32) + jnp.dot(
                        low, mirror, preferred_element_type=jnp.float32
                    )
                    wide_ref[0, near, chunk * chunk_items + item] = north + south
                    wide_ref[1, near, chunk * chunk_items + item] = north - south

        def project(from_side, order, emit):
            start = pl.multiple_of(from_side * side_belts * lat_local, LANES)

            @pl.loop(0, slots, unroll=8)
            def _(slot):
                for parity in range(2):
                    value = jnp.concatenate(
                        [
                            jnp.concatenate(
                                [
                                    wide_ref[
                                        parity, from_side * side_belts + near, item,
                                        pl.ds(slot, 2 * lons, stride=slots), :,
                                    ]
                                    for item in range(items)
                                ],
                                axis=0,
                            )
                            for near in range(side_belts)
                        ],
                        axis=1,
                    )
                    sums = jnp.dot(
                        order, jnp.concatenate(split(value), axis=0), preferred_element_type=jnp.float32
                    ).astype(jnp.bfloat16)
                    result = lax.dot_general(
                        sums,
                        leg_ref[slot, parity, :, pl.ds(start, side_belts * lat_local)],
                        NT_DIMS,
                        preferred_element_type=jnp.float32,
                    )
                    emit(slot, parity, result[:rows] + result[rows:])

        def belt_peers(semaphore):
            @pl.loop(1, belts)
            def _(away):
                peer = (lax.rem(belt + away, belts), lon)
                pl.semaphore_signal(semaphore, inc=1, device_id=peer, device_id_type=mesh_id)

        @pl.loop(1, lons)
        def _(away):
            pl.semaphore_signal(barrier, inc=1, device_id=(belt, lon_away(away)), device_id_type=mesh_id)

        belt_peers(barrier)
        waves_copy = pltpu.make_async_copy(waves_in_ref, waves_ref, small.at[0])
        order_copy = pltpu.make_async_copy(order_in_ref, order_ref, small.at[1])
        waves_copy.start()
        order_copy.start()

        for chunk in range(CHUNKS):
            for item in range(chunk_items):
                own_rows(chunk, item).start()
        pl.semaphore_wait(barrier, lons + belts - 2)

        @pl.loop(0, CHUNKS * chunk_items * PIECES)
        def _(index):
            chunk = index // (PIECES * chunk_items)
            item = lax.rem(index // PIECES, chunk_items)

            @pl.loop(1, lons)
            def _(away):
                gather(chunk, lons - away, item, lax.rem(index, PIECES)).start()

        belt_peers(ready)
        waves_copy.wait()
        order_copy.wait()
        start_legendre(
            jnp.broadcast_to(column_of(waves_ref[...], me, slots), (slots, LANES)), refs, mode_count, half
        )
        fill_table(waves_ref, dft_ref, slots, owners, lon_count)
        legendre_range(0, EARLY)
        pl.semaphore_wait(ready, belts - 1)
        transform(0)
        legendre_range(EARLY, legendre_steps)
        transform(1)

        source = iota((2 * rows, 2 * rows), 0)
        target = iota((2 * rows, 2 * rows), 1)
        wanted = jnp.zeros((1, 2 * rows), jnp.int32)
        for index in range(levels):
            wanted = jnp.where(lax.rem(iota((1, 2 * rows), 1), levels) == index, order_ref[index], wanted)
        within = lax.rem(source, rows)
        level = lax.rem(within // 2, lons) * items + within // (2 * lons)
        match = (
            (level == wanted)
            & (lax.rem(within, 2) == lax.rem(target, rows) // levels)
            & (source // rows == target // rows)
        )
        order = jnp.where(match, 1.0, 0.0).T.astype(jnp.bfloat16)

        other_count = owners // 2
        for chunk in range(CHUNKS):
            exchanged(chunk, 1 - side, other_count).wait_recv()
            mirror_sums(chunk, 1 - side)
            if chunk < CHUNKS - 1:
                own_block(chunk).wait()
                exchanged(chunk, side, other_count - 1).wait_recv()
                mirror_sums(chunk, side)

        def keep(slot, parity, value):
            sum_ref[slot, parity] = value

        def finish(slot, parity, value):
            out_ref[slot, :, parity, :] = sum_ref[slot, parity] + value

        project(1 - side, order, keep)
        own_block(CHUNKS - 1).wait()
        exchanged(CHUNKS - 1, side, other_count - 1).wait_recv()
        mirror_sums(CHUNKS - 1, side)
        project(side, order, finish)

        for chunk in range(CHUNKS):
            gathered(chunk).wait_send()
            exchanged(chunk, side, owners - 1).wait_send()

    dma = pltpu.SemaphoreType.DMA
    return pl.pallas_call(
        body,
        name="analyse",
        in_specs=[
            pl.BlockSpec(memory_space=pl.ANY),
            pl.BlockSpec(memory_space=pltpu.HBM),
            pl.BlockSpec(memory_space=pltpu.HBM),
        ],
        out_specs=pl.BlockSpec(memory_space=pltpu.VMEM),
        out_shape=jax.ShapeDtypeStruct((slots, rows, 2, half_modes), jnp.float32),
        scratch_shapes=[
            pltpu.VMEM(waves.shape, jnp.int32),
            pltpu.SMEM(field_order.shape, jnp.int32),
            pltpu.VMEM((owners * owner_rows, lon_count), jnp.bfloat16),
            pltpu.VMEM((slots, 2, half_modes, half), jnp.bfloat16),
            pltpu.VMEM((CHUNKS, lons, chunk_rows, lon_local), jnp.bfloat16),
            pltpu.VMEM((CHUNKS, blocks, group, owner_rows, chunk_rows), jnp.int16),
            pltpu.VMEM((CHUNKS, owners, owner_rows, chunk_rows), jnp.int16),
            pltpu.VMEM((2, belts // 2, items, 2 * lons * slots, lat_local), jnp.float32),
            pltpu.VMEM((slots, 2, rows, half_modes), jnp.float32),
            pltpu.VMEM((slots, half), jnp.float32),
            pltpu.VMEM((slots, half), jnp.float32),
            pltpu.VMEM((slots, half), jnp.float32),
            pltpu.VMEM((slots, LANES), jnp.float32),
            pltpu.VMEM((2, slots, half), jnp.float32),
            pltpu.VMEM((half // LANES, BLOCK * slots, LANES), jnp.float32),
            dma((CHUNKS,)),
            dma((CHUNKS,)),
            dma((CHUNKS, chunk_items)),
            dma((CHUNKS,)),
            dma((CHUNKS, 2)),
            dma((CHUNKS,)),
            dma((2,)),
            pltpu.SemaphoreType.REGULAR,
        ],
        compiler_params=pltpu.CompilerParams(
            collective_id=0, has_side_effects=True, vmem_limit_bytes=51 << 20
        ),
    )(grid_fields, waves, field_order)


def hand_on(value):
    def body(in_ref, out_ref, done):
        copy = pltpu.make_async_copy(in_ref, out_ref, done)
        copy.start()
        copy.wait()

    return pl.pallas_call(
        body,
        name="hand_on",
        in_specs=[pl.BlockSpec(memory_space=pltpu.VMEM)],
        out_specs=pl.BlockSpec(memory_space=pl.ANY),
        out_shape=jax.ShapeDtypeStruct(value.shape, value.dtype),
        scratch_shapes=[pltpu.SemaphoreType.DMA],
        compiler_params=pltpu.CompilerParams(vmem_limit_bytes=4 << 20),
    )(value)


def on_device(grid_fields, field_order, wave_order):
    owners = lax.axis_size("belt") * lax.axis_size("lon")
    mode_count = wave_order.shape[0]
    slots = mode_count // owners
    levels = grid_fields.shape[0]
    waves = wave_order.astype(jnp.int32).reshape(mode_count // LANES, LANES)
    waves = pltpu.with_memory_space_constraint(waves, pltpu.HBM)
    field_order = pltpu.with_memory_space_constraint(field_order.astype(jnp.int32), pltpu.HBM)
    spectral = analyse(grid_fields, waves, field_order)
    return hand_on(spectral).reshape(slots, 2, levels, 2, mode_count // 2)


def solution(mesh):
    return jax.shard_map(
        on_device,
        mesh=mesh,
        in_specs=(P(None, "belt", "lon"), P(), P()),
        out_specs=P(("belt", "lon"), None, None, None, None),
        check_vma=False,
    )
```

```python
import math

import jax
import jax.numpy as jnp
from jax import lax
from jax.experimental import pallas as pl
from jax.experimental.pallas import tpu as pltpu
from jax.sharding import PartitionSpec as P

LANES = 128
NT_DIMS = (((1,), (1,)), ((), ()))

CODE_STEPS = 1024.0
CODE_LOW = -20.0

CHUNKS = 2
PIECES = 4
BLOCK = 32
RENORM = 16
EARLY = 19


def encode(value):
    magnitude = jnp.abs(value)
    exponent = jnp.floor(jnp.log(jnp.maximum(magnitude, 2.0**CODE_LOW)) * (1.0 / math.log(2.0)))
    exponent = jnp.maximum(exponent, CODE_LOW)
    code = jnp.round(((exponent - CODE_LOW) + magnitude * jnp.exp2(-exponent)) * CODE_STEPS)
    return jnp.where(value < 0.0, -code, code).astype(jnp.int32).astype(jnp.int16)


def decode(code):
    level = code.astype(jnp.int32).astype(jnp.float32) * (1.0 / CODE_STEPS)
    magnitude = jnp.abs(level)
    octave = jnp.maximum(jnp.floor(magnitude), 1.0)
    value = (magnitude - octave + 1.0) * jnp.exp2(octave + (CODE_LOW - 1.0))
    return jnp.where(level < 0.0, -value, value)


def split(value):
    high = value.astype(jnp.bfloat16)
    return high, (value - high.astype(jnp.float32)).astype(jnp.bfloat16)


def iota(shape, dim):
    return lax.broadcasted_iota(jnp.int32, shape, dim)


def column_of(waves, owner, slots):
    waves = waves.astype(jnp.float32)
    per_row = LANES // slots
    row = jnp.sum(jnp.where(iota(waves.shape, 0) == owner // per_row, waves, 0.0), axis=0, keepdims=True)
    shape = (slots, LANES)
    mine = iota(shape, 1) == lax.rem(owner, per_row) * slots + iota(shape, 0)
    return jnp.sum(jnp.where(mine, jnp.broadcast_to(row, shape), 0.0), axis=1, keepdims=True)


def fill_table(waves_ref, table_ref, slots, owners, lon_count):
    quarter = lon_count // 4
    coarse_count = quarter // LANES
    lane = iota((slots, LANES), 1)
    steps = (lane, lax.rem(lane, coarse_count) * LANES)

    def one_owner(owner):
        wave = jnp.broadcast_to(column_of(waves_ref[...], owner, slots), (slots, LANES)).astype(jnp.int32)
        angles = [
            lax.rem(wave * step, lon_count).astype(jnp.float32) * (2.0 * math.pi / lon_count) for step in steps
        ]
        cos_fine, cos_coarse = [jnp.cos(angle) for angle in angles]
        sin_fine, sin_coarse = [jnp.sin(angle) for angle in angles]
        turn = lax.rem(wave, 4).astype(jnp.float32)
        turn = jnp.concatenate((turn, turn), axis=0)
        one = jnp.ones_like(turn)
        zero = jnp.zeros_like(turn)
        keep = jnp.where(turn == 0.0, one, jnp.where(turn == 2.0, -one, zero)).astype(jnp.bfloat16)
        swap = jnp.where(turn == 1.0, -one, jnp.where(turn == 3.0, one, zero)).astype(jnp.bfloat16)
        opposite = jnp.where((turn == 1.0) | (turn == 3.0), -one, one).astype(jnp.bfloat16)
        row = pl.multiple_of(owner * 2 * slots, 2 * slots)
        for a in range(coarse_count):
            ca = cos_coarse[:, a : a + 1]
            sa = sin_coarse[:, a : a + 1]
            cosine = ca * cos_fine - sa * sin_fine
            sine = sa * cos_fine + ca * sin_fine
            plain = jnp.concatenate((cosine, -sine), axis=0).astype(jnp.bfloat16)
            other = jnp.concatenate((sine, cosine), axis=0).astype(jnp.bfloat16)
            turned = plain * keep + other * swap
            for index, value in enumerate((plain, turned, plain * opposite, turned * opposite)):
                start = index * quarter + a * LANES
                table_ref[pl.ds(row, 2 * slots), start : start + LANES] = value

    @pl.loop(0, owners // 2)
    def _(pair):
        one_owner(2 * pair)
        one_owner(2 * pair + 1)


def start_legendre(wave, refs, mode_count, half):
    prev_ref, cur_ref, scale_ref, inv_ref, geo_ref, _ = refs
    lane = iota(wave.shape, 1).astype(jnp.float32)
    terms = None
    for a in range(mode_count // LANES):
        index = lane + (a * LANES + 1.0)
        term = jnp.where(index <= wave, jnp.log1p(0.5 / index), 0.0)
        terms = term if terms is None else terms + term
    start_sum = jnp.sum(terms, axis=1, keepdims=True)
    prev_ref[...] = jnp.zeros_like(prev_ref)
    cur_ref[...] = jnp.ones_like(cur_ref)
    inv_ref[...] = jnp.zeros_like(inv_ref)
    for a in range(half // LANES):
        lanes = slice(a * LANES, (a + 1) * LANES)
        colatitude = (math.pi / (2 * half + 0.5)) * (lane + (a * LANES + 0.75))
        sine = jnp.sin(colatitude)
        geo_ref[0, :, lanes] = jnp.cos(colatitude)
        geo_ref[1, :, lanes] = (math.pi / (2 * half + 0.5) * math.sqrt(half)) * sine
        scale_ref[:, lanes] = -0.5 * math.log(2.0) + 0.5 * start_sum + wave * jnp.log(sine)


def legendre_block(step, wave, refs, table_ref, mode_count, half):
    prev_ref, cur_ref, scale_ref, inv_ref, geo_ref, rows_ref = refs
    slots = wave.shape[0]
    first = (step * BLOCK).astype(jnp.float32)
    chunks = half // LANES
    lanes = [slice(a * LANES, (a + 1) * LANES) for a in range(chunks)]
    inverse = inv_ref[...]
    prev = [prev_ref[:, s] for s in lanes]
    cur = [cur_ref[:, s] for s in lanes]
    amp = [None] * chunks
    for row in range(BLOCK):
        if row % RENORM == 0:
            for a in range(chunks):
                total = jnp.maximum(jnp.abs(prev[a]) + jnp.abs(cur[a]), 1e-30)
                prev[a] = prev[a] / total
                cur[a] = cur[a] / total
                log_scale = scale_ref[:, lanes[a]] + jnp.log(total)
                scale_ref[:, lanes[a]] = log_scale
                amp[a] = jnp.exp(log_scale) * geo_ref[1, :, lanes[a]]
        for a in range(chunks):
            rows_ref[a, row * slots : (row + 1) * slots, :] = cur[a] * amp[a]
        offset = first + (row + 1.0)
        degree = wave + offset
        numer = 4.0 * degree * degree - 1.0
        denom = offset * (wave + degree)
        root = lax.rsqrt(numer * denom)
        factor = jnp.where(degree < mode_count, numer * root, 0.0)
        ratio = factor * inverse
        inverse = denom * root
        for a in range(chunks):
            following = (factor * geo_ref[0, :, lanes[a]]) * cur[a] - ratio * prev[a]
            prev[a] = cur[a]
            cur[a] = following
    inv_ref[...] = inverse
    for a in range(chunks):
        prev_ref[:, lanes[a]] = prev[a]
        cur_ref[:, lanes[a]] = cur[a]
    out_row = pl.multiple_of(step * (BLOCK // 2), BLOCK // 2)
    for slot in range(slots):
        for parity in range(2):
            for a in range(chunks):
                table_ref[slot, parity, pl.ds(out_row, BLOCK // 2), lanes[a]] = rows_ref[
                    a, pl.ds(parity * slots + slot, BLOCK // 2, stride=2 * slots), :
                ].astype(jnp.bfloat16)


def analyse(grid_fields, waves):
    belts = lax.axis_size("belt")
    lons = lax.axis_size("lon")
    levels, lat_local, lon_local = grid_fields.shape
    owners = belts * lons
    mode_count = waves.shape[0] * waves.shape[1]
    slots = mode_count // owners
    lat_count = lat_local * belts
    half = lat_count // 2
    lon_count = lon_local * lons
    half_modes = mode_count // 2
    items = levels // lons
    chunk_items = items // CHUNKS
    chunk_rows = chunk_items * lat_local
    group = 2 * lons
    blocks = owners // group
    owner_rows = 2 * slots
    block_rows = group * owner_rows
    rows = 2 * levels
    half_lons = lons // 2
    side_belts = belts // 4
    tiles = half_modes // LANES
    piece = lat_local // PIECES
    scale = 1.0 / math.sqrt(lon_count)
    mesh_id = pl.DeviceIdType.MESH
    legendre_steps = mode_count // BLOCK

    def body(
        fields_ref, waves_in_ref, out_ref, waves_ref, dft_ref, leg_ref, rows_in_ref, send_ref, recv_ref, wide_ref, sum_ref,
        prev_ref, cur_ref, scale_ref, inv_ref, geo_ref, step_rows_ref,
        in_send, in_recv, in_local, out_send, out_recv, out_local, small, ready,
    ):
        belt = lax.axis_index("belt")
        lon = lax.axis_index("lon")
        me = belt * lons + lon
        barrier = pltpu.get_barrier_semaphore()
        refs = (prev_ref, cur_ref, scale_ref, inv_ref, geo_ref, step_rows_ref)

        def lon_away(away):
            high = lax.rem(lon // half_lons + away // half_lons, 2)
            return high * half_lons + lax.rem(lax.rem(lon, half_lons) + lax.rem(away, half_lons), half_lons)

        side = lax.rem((belt // 4 + 1) // 2, 2)

        def place(step):
            turn = step // 2
            high = lax.rem(belt // 8 + lax.rem(turn + 1, 2), 2)
            low = lax.rem(lax.rem(belt // 4, 2) + lax.rem((turn + 1) // 2, 2), 2)
            return high * 4 + low * 2 + lax.rem(lax.rem(belt // 2, 2) + lax.rem(step + 1, 2), 2)

        def member(index):
            return lax.rem(lax.rem(belt, 2) + index // lons, 2), lon_away(lax.rem(index, lons))

        def gather(chunk, away, item, part):
            target = lon_away(away)
            return pltpu.make_async_remote_copy(
                fields_ref.at[target * items + chunk * chunk_items + item, pl.ds(part * piece, piece)],
                rows_in_ref.at[chunk, lon, pl.ds(item * lat_local + part * piece, piece)],
                in_send.at[chunk],
                in_recv.at[chunk],
                device_id=(belt, target),
                device_id_type=mesh_id,
            )

        def own_rows(chunk, item):
            return pltpu.make_async_copy(
                fields_ref.at[lon * items + chunk * chunk_items + item],
                rows_in_ref.at[chunk, lon, pl.ds(item * lat_local, lat_local)],
                in_local.at[chunk, item],
            )

        members = [member(index) for index in range(group)]

        def send(chunk, step, block, index):
            core, target = members[index]
            return pltpu.make_async_remote_copy(
                send_ref.at[chunk, step, core * lons + target],
                recv_ref.at[chunk, me],
                out_send.at[chunk],
                out_recv.at[chunk, side],
                device_id=(block * 2 + core, target),
                device_id_type=mesh_id,
            )

        def own_block(chunk):
            core, target = members[0]
            return pltpu.make_async_copy(
                send_ref.at[chunk, blocks - 1, core * lons + target], recv_ref.at[chunk, me], out_local.at[chunk]
            )

        def gathered(chunk):
            whole = rows_in_ref.at[chunk, pl.ds(0, lons - 1)]
            return pltpu.make_async_remote_copy(
                whole, whole, in_send.at[chunk], in_recv.at[chunk],
                device_id=(belt, lon_away(1)), device_id_type=mesh_id,
            )

        def exchanged(chunk, from_side, count):
            whole = recv_ref.at[chunk, pl.ds(0, count)]
            return pltpu.make_async_remote_copy(
                whole, whole, out_send.at[chunk], out_recv.at[chunk, from_side],
                device_id=(belt, lon_away(1)), device_id_type=mesh_id,
            )

        def legendre_range(start, stop):
            wave = jnp.broadcast_to(column_of(waves_ref[...], me, slots), (slots, LANES))

            @pl.loop(start, stop)
            def _(step):
                legendre_block(step, wave, refs, leg_ref, mode_count, half)

        def transform(chunk):
            for item in range(chunk_items):
                own_rows(chunk, item).wait()
            gathered(chunk).wait_recv()

            @pl.loop(0, blocks)
            def _(step):
                block = place(step)
                start = pl.multiple_of(block * block_rows, block_rows)
                total = None
                for part in range(lons):
                    term = lax.dot_general(
                        dft_ref[pl.ds(start, block_rows), part * lon_local : (part + 1) * lon_local],
                        rows_in_ref[chunk, part],
                        NT_DIMS,
                        preferred_element_type=jnp.float32,
                    )
                    total = term if total is None else total + term
                send_ref[chunk, step] = encode(total * scale).reshape(group, owner_rows, chunk_rows)

                for index in range(group - 1, 0, -1):
                    send(chunk, step, block, index).start()

                @pl.when(step < blocks - 1)
                def _():
                    send(chunk, step, block, 0).start()

            own_block(chunk).start()

        def mirror_sums(chunk, from_side):
            mirror = (iota((lat_local, lat_local), 0) + iota((lat_local, lat_local), 1)).astype(jnp.float32)
            mirror = jnp.where(mirror == lat_local - 1.0, 1.0, 0.0).astype(jnp.bfloat16)

            @pl.loop(0, side_belts, unroll=4)
            def _(index):
                near = from_side * side_belts + index
                far = belts - 1 - near
                for item in range(chunk_items):
                    lanes = slice(item * lat_local, (item + 1) * lat_local)
                    north = decode(recv_ref[chunk, pl.ds(near * lons, lons), :, lanes]).reshape(-1, lat_local)
                    south = decode(recv_ref[chunk, pl.ds(far * lons, lons), :, lanes]).reshape(-1, lat_local)
                    high, low = split(south)
                    south = jnp.dot(high, mirror, preferred_element_type=jnp.float32) + jnp.dot(
                        low, mirror, preferred_element_type=jnp.float32
                    )
                    wide_ref[0, near, chunk * chunk_items + item] = north + south
                    wide_ref[1, near, chunk * chunk_items + item] = north - south

        def project(from_side, emit):
            start = pl.multiple_of(from_side * side_belts * lat_local, LANES)

            @pl.loop(0, slots, unroll=8)
            def _(slot):
                for parity in range(2):
                    value = jnp.concatenate(
                        [
                            jnp.concatenate(
                                [
                                    wide_ref[
                                        parity, from_side * side_belts + near, item,
                                        pl.ds(slot, 2 * lons, stride=slots), :,
                                    ]
                                    for item in range(items)
                                ],
                                axis=0,
                            )
                            for near in range(side_belts)
                        ],
                        axis=1,
                    )
                    sums = jnp.concatenate(split(value), axis=0)
                    result = lax.dot_general(
                        sums,
                        leg_ref[slot, parity, :, pl.ds(start, side_belts * lat_local)],
                        NT_DIMS,
                        preferred_element_type=jnp.float32,
                    )
                    emit(slot, parity, result[:rows] + result[rows:])

        def belt_peers(semaphore):
            @pl.loop(1, belts)
            def _(away):
                peer = (lax.rem(belt + away, belts), lon)
                pl.semaphore_signal(semaphore, inc=1, device_id=peer, device_id_type=mesh_id)

        @pl.loop(1, lons)
        def _(away):
            pl.semaphore_signal(barrier, inc=1, device_id=(belt, lon_away(away)), device_id_type=mesh_id)

        belt_peers(barrier)
        waves_copy = pltpu.make_async_copy(waves_in_ref, waves_ref, small)
        waves_copy.start()

        for chunk in range(CHUNKS):
            for item in range(chunk_items):
                own_rows(chunk, item).start()
        pl.semaphore_wait(barrier, lons + belts - 2)

        @pl.loop(0, CHUNKS * chunk_items * PIECES)
        def _(index):
            chunk = index // (PIECES * chunk_items)
            item = lax.rem(index // PIECES, chunk_items)

            @pl.loop(1, lons)
            def _(away):
                gather(chunk, lons - away, item, lax.rem(index, PIECES)).start()

        belt_peers(ready)
        waves_copy.wait()
        start_legendre(
            jnp.broadcast_to(column_of(waves_ref[...], me, slots), (slots, LANES)), refs, mode_count, half
        )
        fill_table(waves_ref, dft_ref, slots, owners, lon_count)
        legendre_range(0, EARLY)
        pl.semaphore_wait(ready, belts - 1)
        transform(0)
        legendre_range(EARLY, legendre_steps)
        transform(1)

        other_count = owners // 2
        for chunk in range(CHUNKS):
            exchanged(chunk, 1 - side, other_count).wait_recv()
            mirror_sums(chunk, 1 - side)
            if chunk < CHUNKS - 1:
                own_block(chunk).wait()
                exchanged(chunk, side, other_count - 1).wait_recv()
                mirror_sums(chunk, side)

        def keep(slot, parity, value):
            sum_ref[slot, parity] = value

        def finish(slot, parity, value):
            value = sum_ref[slot, parity] + value
            for tile in range(tiles):
                start = slot * (rows * tiles * 2) + tile * 2 + parity
                out_ref[pl.ds(start, rows, stride=2 * tiles), :] = value[:, tile * LANES : (tile + 1) * LANES]

        project(1 - side, keep)
        own_block(CHUNKS - 1).wait()
        exchanged(CHUNKS - 1, side, other_count - 1).wait_recv()
        mirror_sums(CHUNKS - 1, side)
        project(side, finish)

        for chunk in range(CHUNKS):
            gathered(chunk).wait_send()
            exchanged(chunk, side, owners - 1).wait_send()

    dma = pltpu.SemaphoreType.DMA
    return pl.pallas_call(
        body,
        name="analyse",
        in_specs=[
            pl.BlockSpec(memory_space=pl.ANY),
            pl.BlockSpec(memory_space=pltpu.HBM),
        ],
        out_specs=pl.BlockSpec(memory_space=pltpu.VMEM),
        out_shape=jax.ShapeDtypeStruct((slots * rows * tiles * 2, LANES), jnp.float32),
        scratch_shapes=[
            pltpu.VMEM(waves.shape, jnp.int32),
            pltpu.VMEM((owners * owner_rows, lon_count), jnp.bfloat16),
            pltpu.VMEM((slots, 2, half_modes, half), jnp.bfloat16),
            pltpu.VMEM((CHUNKS, lons, chunk_rows, lon_local), jnp.bfloat16),
            pltpu.VMEM((CHUNKS, blocks, group, owner_rows, chunk_rows), jnp.int16),
            pltpu.VMEM((CHUNKS, owners, owner_rows, chunk_rows), jnp.int16),
            pltpu.VMEM((2, belts // 2, items, 2 * lons * slots, lat_local), jnp.float32),
            pltpu.VMEM((slots, 2, rows, half_modes), jnp.float32),
            pltpu.VMEM((slots, half), jnp.float32),
            pltpu.VMEM((slots, half), jnp.float32),
            pltpu.VMEM((slots, half), jnp.float32),
            pltpu.VMEM((slots, LANES), jnp.float32),
            pltpu.VMEM((2, slots, half), jnp.float32),
            pltpu.VMEM((half // LANES, BLOCK * slots, LANES), jnp.float32),
            dma((CHUNKS,)),
            dma((CHUNKS,)),
            dma((CHUNKS, chunk_items)),
            dma((CHUNKS,)),
            dma((CHUNKS, 2)),
            dma((CHUNKS,)),
            dma,
            pltpu.SemaphoreType.REGULAR,
        ],
        compiler_params=pltpu.CompilerParams(
            collective_id=0, has_side_effects=True, vmem_limit_bytes=51 << 20
        ),
    )(grid_fields, waves)


def hand_on(value, field_order, items, lons):
    levels = items * lons

    def body(order_ref, in_ref, out_ref, done):
        for place in range(levels):
            level = order_ref[place]
            for component in range(2):
                source = lax.rem(level, items) * (2 * lons) + lax.div(level, items) * 2 + component
                pltpu.make_async_copy(
                    in_ref.at[:, source], out_ref.at[:, component * levels + place], done
                ).start()
        pltpu.make_async_copy(in_ref, out_ref, done).wait()

    return pl.pallas_call(
        body,
        name="hand_on",
        in_specs=[pl.BlockSpec(memory_space=pltpu.SMEM), pl.BlockSpec(memory_space=pltpu.VMEM)],
        out_specs=pl.BlockSpec(memory_space=pl.ANY),
        out_shape=jax.ShapeDtypeStruct(value.shape, value.dtype),
        scratch_shapes=[pltpu.SemaphoreType.DMA],
        compiler_params=pltpu.CompilerParams(vmem_limit_bytes=4 << 20),
    )(field_order, value)


def on_device(grid_fields, field_order, wave_order):
    owners = lax.axis_size("belt") * lax.axis_size("lon")
    mode_count = wave_order.shape[0]
    slots = mode_count // owners
    levels = grid_fields.shape[0]
    waves = wave_order.astype(jnp.int32).reshape(mode_count // LANES, LANES)
    waves = pltpu.with_memory_space_constraint(waves, pltpu.HBM)
    spectral = analyse(grid_fields, waves).reshape(slots, 2 * levels, -1, LANES)
    lons = lax.axis_size("lon")
    spectral = hand_on(spectral, field_order.astype(jnp.int32), levels // lons, lons)
    spectral = spectral.reshape(slots, 2, levels, -1, 2, LANES)
    return jnp.swapaxes(spectral, 3, 4).reshape(slots, 2, levels, 2, mode_count // 2)


def solution(mesh):
    return jax.shard_map(
        on_device,
        mesh=mesh,
        in_specs=(P(None, "belt", "lon"), P(), P()),
        out_specs=P(("belt", "lon"), None, None, None, None),
        check_vma=False,
    )
```

```python
import math

import jax
import jax.numpy as jnp
from jax import lax
from jax.experimental import pallas as pl
from jax.experimental.pallas import tpu as pltpu
from jax.sharding import PartitionSpec as P

LANES = 128
NT_DIMS = (((1,), (1,)), ((), ()))

CODE_STEPS = 1024.0
CODE_LOW = -20.0

CHUNKS = 2
PIECES = 4
BLOCK = 32
RENORM = 16
EARLY = 19


def encode(value):
    magnitude = jnp.abs(value)
    exponent = jnp.floor(jnp.log(jnp.maximum(magnitude, 2.0**CODE_LOW)) * (1.0 / math.log(2.0)))
    exponent = jnp.maximum(exponent, CODE_LOW)
    code = jnp.round(((exponent - CODE_LOW) + magnitude * jnp.exp2(-exponent)) * CODE_STEPS)
    return jnp.where(value < 0.0, -code, code).astype(jnp.int32).astype(jnp.int16)


def decode(code):
    level = code.astype(jnp.int32).astype(jnp.float32) * (1.0 / CODE_STEPS)
    magnitude = jnp.abs(level)
    octave = jnp.maximum(jnp.floor(magnitude), 1.0)
    value = (magnitude - octave + 1.0) * jnp.exp2(octave + (CODE_LOW - 1.0))
    return jnp.where(level < 0.0, -value, value)


def split(value):
    high = value.astype(jnp.bfloat16)
    return high, (value - high.astype(jnp.float32)).astype(jnp.bfloat16)


def iota(shape, dim):
    return lax.broadcasted_iota(jnp.int32, shape, dim)


def column_of(waves, owner, slots):
    waves = waves.astype(jnp.float32)
    per_row = LANES // slots
    row = jnp.sum(jnp.where(iota(waves.shape, 0) == owner // per_row, waves, 0.0), axis=0, keepdims=True)
    shape = (slots, LANES)
    mine = iota(shape, 1) == lax.rem(owner, per_row) * slots + iota(shape, 0)
    return jnp.sum(jnp.where(mine, jnp.broadcast_to(row, shape), 0.0), axis=1, keepdims=True)


def fill_table(waves_ref, table_ref, slots, owners, lon_count):
    quarter = lon_count // 4
    coarse_count = quarter // LANES
    lane = iota((slots, LANES), 1)
    steps = (lane, lax.rem(lane, coarse_count) * LANES)

    def one_owner(owner):
        wave = jnp.broadcast_to(column_of(waves_ref[...], owner, slots), (slots, LANES)).astype(jnp.int32)
        angles = [
            lax.rem(wave * step, lon_count).astype(jnp.float32) * (2.0 * math.pi / lon_count) for step in steps
        ]
        cos_fine, cos_coarse = [jnp.cos(angle) for angle in angles]
        sin_fine, sin_coarse = [jnp.sin(angle) for angle in angles]
        turn = lax.rem(wave, 4).astype(jnp.float32)
        turn = jnp.concatenate((turn, turn), axis=0)
        one = jnp.ones_like(turn)
        zero = jnp.zeros_like(turn)
        keep = jnp.where(turn == 0.0, one, jnp.where(turn == 2.0, -one, zero)).astype(jnp.bfloat16)
        swap = jnp.where(turn == 1.0, -one, jnp.where(turn == 3.0, one, zero)).astype(jnp.bfloat16)
        opposite = jnp.where((turn == 1.0) | (turn == 3.0), -one, one).astype(jnp.bfloat16)
        row = pl.multiple_of(owner * 2 * slots, 2 * slots)
        for a in range(coarse_count):
            ca = cos_coarse[:, a : a + 1]
            sa = sin_coarse[:, a : a + 1]
            cosine = ca * cos_fine - sa * sin_fine
            sine = sa * cos_fine + ca * sin_fine
            plain = jnp.concatenate((cosine, -sine), axis=0).astype(jnp.bfloat16)
            other = jnp.concatenate((sine, cosine), axis=0).astype(jnp.bfloat16)
            turned = plain * keep + other * swap
            for index, value in enumerate((plain, turned, plain * opposite, turned * opposite)):
                start = index * quarter + a * LANES
                table_ref[pl.ds(row, 2 * slots), start : start + LANES] = value

    @pl.loop(0, owners // 2)
    def _(pair):
        one_owner(2 * pair)
        one_owner(2 * pair + 1)


def start_legendre(wave, refs, mode_count, half):
    prev_ref, cur_ref, scale_ref, inv_ref, geo_ref, _ = refs
    lane = iota(wave.shape, 1).astype(jnp.float32)
    terms = None
    for a in range(mode_count // LANES):
        index = lane + (a * LANES + 1.0)
        term = jnp.where(index <= wave, jnp.log1p(0.5 / index), 0.0)
        terms = term if terms is None else terms + term
    start_sum = jnp.sum(terms, axis=1, keepdims=True)
    prev_ref[...] = jnp.zeros_like(prev_ref)
    cur_ref[...] = jnp.ones_like(cur_ref)
    inv_ref[...] = jnp.zeros_like(inv_ref)
    for a in range(half // LANES):
        lanes = slice(a * LANES, (a + 1) * LANES)
        colatitude = (math.pi / (2 * half + 0.5)) * (lane + (a * LANES + 0.75))
        sine = jnp.sin(colatitude)
        geo_ref[0, :, lanes] = jnp.cos(colatitude)
        geo_ref[1, :, lanes] = (math.pi / (2 * half + 0.5) * math.sqrt(half)) * sine
        scale_ref[:, lanes] = -0.5 * math.log(2.0) + 0.5 * start_sum + wave * jnp.log(sine)


def legendre_block(step, wave, refs, table_ref, mode_count, half):
    prev_ref, cur_ref, scale_ref, inv_ref, geo_ref, rows_ref = refs
    slots = wave.shape[0]
    first = (step * BLOCK).astype(jnp.float32)
    chunks = half // LANES
    lanes = [slice(a * LANES, (a + 1) * LANES) for a in range(chunks)]
    inverse = inv_ref[...]
    prev = [prev_ref[:, s] for s in lanes]
    cur = [cur_ref[:, s] for s in lanes]
    amp = [None] * chunks
    for row in range(BLOCK):
        if row % RENORM == 0:
            for a in range(chunks):
                total = jnp.maximum(jnp.abs(prev[a]) + jnp.abs(cur[a]), 1e-30)
                prev[a] = prev[a] / total
                cur[a] = cur[a] / total
                log_scale = scale_ref[:, lanes[a]] + jnp.log(total)
                scale_ref[:, lanes[a]] = log_scale
                amp[a] = jnp.exp(log_scale) * geo_ref[1, :, lanes[a]]
        for a in range(chunks):
            rows_ref[a, row * slots : (row + 1) * slots, :] = cur[a] * amp[a]
        offset = first + (row + 1.0)
        degree = wave + offset
        numer = 4.0 * degree * degree - 1.0
        denom = offset * (wave + degree)
        root = lax.rsqrt(numer * denom)
        factor = jnp.where(degree < mode_count, numer * root, 0.0)
        ratio = factor * inverse
        inverse = denom * root
        for a in range(chunks):
            following = (factor * geo_ref[0, :, lanes[a]]) * cur[a] - ratio * prev[a]
            prev[a] = cur[a]
            cur[a] = following
    inv_ref[...] = inverse
    for a in range(chunks):
        prev_ref[:, lanes[a]] = prev[a]
        cur_ref[:, lanes[a]] = cur[a]
    out_row = pl.multiple_of(step * (BLOCK // 2), BLOCK // 2)
    for slot in range(slots):
        for parity in range(2):
            for a in range(chunks):
                table_ref[slot, parity, pl.ds(out_row, BLOCK // 2), lanes[a]] = rows_ref[
                    a, pl.ds(parity * slots + slot, BLOCK // 2, stride=2 * slots), :
                ].astype(jnp.bfloat16)


def analyse(grid_fields, waves):
    belts = lax.axis_size("belt")
    lons = lax.axis_size("lon")
    levels, lat_local, lon_local = grid_fields.shape
    owners = belts * lons
    mode_count = waves.shape[0] * waves.shape[1]
    slots = mode_count // owners
    lat_count = lat_local * belts
    half = lat_count // 2
    lon_count = lon_local * lons
    half_modes = mode_count // 2
    items = levels // lons
    chunk_items = items // CHUNKS
    chunk_rows = chunk_items * lat_local
    group = 2 * lons
    blocks = owners // group
    owner_rows = 2 * slots
    block_rows = group * owner_rows
    rows = 2 * levels
    half_lons = lons // 2
    side_belts = belts // 4
    tiles = half_modes // LANES
    piece = lat_local // PIECES
    scale = 1.0 / math.sqrt(lon_count)
    mesh_id = pl.DeviceIdType.MESH
    legendre_steps = mode_count // BLOCK

    def body(
        fields_ref, waves_in_ref, out_ref, waves_ref, dft_ref, leg_ref, rows_in_ref, send_ref, recv_ref, wide_ref, sum_ref,
        prev_ref, cur_ref, scale_ref, inv_ref, geo_ref, step_rows_ref,
        in_send, in_recv, in_local, out_send, out_recv, out_local, small, ready,
    ):
        belt = lax.axis_index("belt")
        lon = lax.axis_index("lon")
        me = belt * lons + lon
        barrier = pltpu.get_barrier_semaphore()
        refs = (prev_ref, cur_ref, scale_ref, inv_ref, geo_ref, step_rows_ref)

        def lon_away(away):
            high = lax.rem(lon // half_lons + away // half_lons, 2)
            return high * half_lons + lax.rem(lax.rem(lon, half_lons) + lax.rem(away, half_lons), half_lons)

        side = lax.rem((belt // 4 + 1) // 2, 2)

        def place(step):
            turn = step // 2
            high = lax.rem(belt // 8 + lax.rem(turn + 1, 2), 2)
            low = lax.rem(lax.rem(belt // 4, 2) + lax.rem((turn + 1) // 2, 2), 2)
            return high * 4 + low * 2 + lax.rem(lax.rem(belt // 2, 2) + lax.rem(step + 1, 2), 2)

        def member(index):
            return lax.rem(lax.rem(belt, 2) + index // lons, 2), lon_away(lax.rem(index, lons))

        def gather(chunk, away, item, part):
            target = lon_away(away)
            return pltpu.make_async_remote_copy(
                fields_ref.at[target * items + chunk * chunk_items + item, pl.ds(part * piece, piece)],
                rows_in_ref.at[chunk, lon, pl.ds(item * lat_local + part * piece, piece)],
                in_send.at[chunk],
                in_recv.at[chunk],
                device_id=(belt, target),
                device_id_type=mesh_id,
            )

        def own_rows(chunk, item):
            return pltpu.make_async_copy(
                fields_ref.at[lon * items + chunk * chunk_items + item],
                rows_in_ref.at[chunk, lon, pl.ds(item * lat_local, lat_local)],
                in_local.at[chunk, item],
            )

        members = [member(index) for index in range(group)]

        def send(chunk, step, block, index):
            core, target = members[index]
            return pltpu.make_async_remote_copy(
                send_ref.at[chunk, step, core * lons + target],
                recv_ref.at[chunk, me],
                out_send.at[chunk],
                out_recv.at[chunk, side],
                device_id=(block * 2 + core, target),
                device_id_type=mesh_id,
            )

        def own_block(chunk):
            core, target = members[0]
            return pltpu.make_async_copy(
                send_ref.at[chunk, blocks - 1, core * lons + target], recv_ref.at[chunk, me], out_local.at[chunk]
            )

        def gathered(chunk):
            whole = rows_in_ref.at[chunk, pl.ds(0, lons - 1)]
            return pltpu.make_async_remote_copy(
                whole, whole, in_send.at[chunk], in_recv.at[chunk],
                device_id=(belt, lon_away(1)), device_id_type=mesh_id,
            )

        def exchanged(chunk, from_side, count):
            whole = recv_ref.at[chunk, pl.ds(0, count)]
            return pltpu.make_async_remote_copy(
                whole, whole, out_send.at[chunk], out_recv.at[chunk, from_side],
                device_id=(belt, lon_away(1)), device_id_type=mesh_id,
            )

        def legendre_range(start, stop):
            wave = jnp.broadcast_to(column_of(waves_ref[...], me, slots), (slots, LANES))

            @pl.loop(start, stop)
            def _(step):
                legendre_block(step, wave, refs, leg_ref, mode_count, half)

        def transform(chunk):
            for item in range(chunk_items):
                own_rows(chunk, item).wait()
            gathered(chunk).wait_recv()

            @pl.loop(0, blocks)
            def _(step):
                block = place(step)
                start = pl.multiple_of(block * block_rows, block_rows)
                total = None
                for part in range(lons):
                    term = lax.dot_general(
                        dft_ref[pl.ds(start, block_rows), part * lon_local : (part + 1) * lon_local],
                        rows_in_ref[chunk, part],
                        NT_DIMS,
                        preferred_element_type=jnp.float32,
                    )
                    total = term if total is None else total + term
                send_ref[chunk, step] = encode(total * scale).reshape(group, owner_rows, chunk_rows)

                for index in range(group - 1, 0, -1):
                    send(chunk, step, block, index).start()

                @pl.when(step < blocks - 1)
                def _():
                    send(chunk, step, block, 0).start()

            own_block(chunk).start()

        def mirror_sums(chunk, from_side):
            mirror = (iota((lat_local, lat_local), 0) + iota((lat_local, lat_local), 1)).astype(jnp.float32)
            mirror = jnp.where(mirror == lat_local - 1.0, 1.0, 0.0).astype(jnp.bfloat16)

            @pl.loop(0, side_belts, unroll=4)
            def _(index):
                near = from_side * side_belts + index
                far = belts - 1 - near
                for item in range(chunk_items):
                    lanes = slice(item * lat_local, (item + 1) * lat_local)
                    north = decode(recv_ref[chunk, pl.ds(near * lons, lons), :, lanes]).reshape(-1, lat_local)
                    south = decode(recv_ref[chunk, pl.ds(far * lons, lons), :, lanes]).reshape(-1, lat_local)
                    high, low = split(south)
                    south = jnp.dot(high, mirror, preferred_element_type=jnp.float32) + jnp.dot(
                        low, mirror, preferred_element_type=jnp.float32
                    )
                    wide_ref[0, near, chunk * chunk_items + item] = north + south
                    wide_ref[1, near, chunk * chunk_items + item] = north - south

        def project(from_side, chosen, emit):
            start = pl.multiple_of(from_side * side_belts * lat_local, LANES)

            @pl.loop(0, slots, unroll=8)
            def _(slot):
                for parity in range(2):
                    value = jnp.concatenate(
                        [
                            jnp.concatenate(
                                [
                                    wide_ref[
                                        parity, from_side * side_belts + near, item,
                                        pl.ds(slot, 2 * lons, stride=slots), :,
                                    ]
                                    for item in chosen
                                ],
                                axis=0,
                            )
                            for near in range(side_belts)
                        ],
                        axis=1,
                    )
                    sums = jnp.concatenate(split(value), axis=0)
                    result = lax.dot_general(
                        sums,
                        leg_ref[slot, parity, :, pl.ds(start, side_belts * lat_local)],
                        NT_DIMS,
                        preferred_element_type=jnp.float32,
                    )
                    half_rows = result.shape[0] // 2
                    emit(slot, parity, result[:half_rows] + result[half_rows:])

        def belt_peers(semaphore):
            @pl.loop(1, belts)
            def _(away):
                peer = (lax.rem(belt + away, belts), lon)
                pl.semaphore_signal(semaphore, inc=1, device_id=peer, device_id_type=mesh_id)

        @pl.loop(1, lons)
        def _(away):
            pl.semaphore_signal(barrier, inc=1, device_id=(belt, lon_away(away)), device_id_type=mesh_id)

        belt_peers(barrier)
        waves_copy = pltpu.make_async_copy(waves_in_ref, waves_ref, small)
        waves_copy.start()

        for chunk in range(CHUNKS):
            for item in range(chunk_items):
                own_rows(chunk, item).start()
        pl.semaphore_wait(barrier, lons + belts - 2)

        @pl.loop(0, CHUNKS * chunk_items * PIECES)
        def _(index):
            chunk = index // (PIECES * chunk_items)
            item = lax.rem(index // PIECES, chunk_items)

            @pl.loop(1, lons)
            def _(away):
                gather(chunk, lons - away, item, lax.rem(index, PIECES)).start()

        belt_peers(ready)
        waves_copy.wait()
        start_legendre(
            jnp.broadcast_to(column_of(waves_ref[...], me, slots), (slots, LANES)), refs, mode_count, half
        )
        fill_table(waves_ref, dft_ref, slots, owners, lon_count)
        legendre_range(0, EARLY)
        pl.semaphore_wait(ready, belts - 1)
        transform(0)
        legendre_range(EARLY, legendre_steps)
        transform(1)

        other_count = owners // 2
        early = rows - chunk_items * 2 * lons

        def add(slot, parity, value):
            sum_ref[slot, parity, :early] += value[:early]
            sum_ref[slot, parity, early:] = value[early:]

        def keep_early(slot, parity, value):
            sum_ref[slot, parity, :early] = value

        def finish(slot, parity, value):
            value = jnp.concatenate((sum_ref[slot, parity, :early], sum_ref[slot, parity, early:] + value), axis=0)
            for tile in range(tiles):
                start = slot * (rows * tiles * 2) + tile * 2 + parity
                out_ref[pl.ds(start, rows, stride=2 * tiles), :] = value[:, tile * LANES : (tile + 1) * LANES]

        for chunk in range(CHUNKS):
            exchanged(chunk, 1 - side, other_count).wait_recv()
            mirror_sums(chunk, 1 - side)
            if chunk < CHUNKS - 1:
                own_block(chunk).wait()
                exchanged(chunk, side, other_count - 1).wait_recv()
                mirror_sums(chunk, side)

            if chunk == CHUNKS - 2:
                project(side, range(items - chunk_items), keep_early)

        project(1 - side, range(items), add)
        own_block(CHUNKS - 1).wait()
        exchanged(CHUNKS - 1, side, other_count - 1).wait_recv()
        mirror_sums(CHUNKS - 1, side)
        project(side, range(items - chunk_items, items), finish)

        for chunk in range(CHUNKS):
            gathered(chunk).wait_send()
            exchanged(chunk, side, owners - 1).wait_send()

    dma = pltpu.SemaphoreType.DMA
    return pl.pallas_call(
        body,
        name="analyse",
        in_specs=[
            pl.BlockSpec(memory_space=pl.ANY),
            pl.BlockSpec(memory_space=pltpu.HBM),
        ],
        out_specs=pl.BlockSpec(memory_space=pltpu.VMEM),
        out_shape=jax.ShapeDtypeStruct((slots * rows * tiles * 2, LANES), jnp.float32),
        scratch_shapes=[
            pltpu.VMEM(waves.shape, jnp.int32),
            pltpu.VMEM((owners * owner_rows, lon_count), jnp.bfloat16),
            pltpu.VMEM((slots, 2, half_modes, half), jnp.bfloat16),
            pltpu.VMEM((CHUNKS, lons, chunk_rows, lon_local), jnp.bfloat16),
            pltpu.VMEM((CHUNKS, blocks, group, owner_rows, chunk_rows), jnp.int16),
            pltpu.VMEM((CHUNKS, owners, owner_rows, chunk_rows), jnp.int16),
            pltpu.VMEM((2, belts // 2, items, 2 * lons * slots, lat_local), jnp.float32),
            pltpu.VMEM((slots, 2, rows, half_modes), jnp.float32),
            pltpu.VMEM((slots, half), jnp.float32),
            pltpu.VMEM((slots, half), jnp.float32),
            pltpu.VMEM((slots, half), jnp.float32),
            pltpu.VMEM((slots, LANES), jnp.float32),
            pltpu.VMEM((2, slots, half), jnp.float32),
            pltpu.VMEM((half // LANES, BLOCK * slots, LANES), jnp.float32),
            dma((CHUNKS,)),
            dma((CHUNKS,)),
            dma((CHUNKS, chunk_items)),
            dma((CHUNKS,)),
            dma((CHUNKS, 2)),
            dma((CHUNKS,)),
            dma,
            pltpu.SemaphoreType.REGULAR,
        ],
        compiler_params=pltpu.CompilerParams(
            collective_id=0, has_side_effects=True, vmem_limit_bytes=51 << 20
        ),
    )(grid_fields, waves)


def hand_on(value, field_order, items, lons):
    levels = items * lons

    def body(order_ref, in_ref, out_ref, done):
        for place in range(levels):
            level = order_ref[place]
            for component in range(2):
                source = lax.rem(level, items) * (2 * lons) + lax.div(level, items) * 2 + component
                pltpu.make_async_copy(
                    in_ref.at[:, source], out_ref.at[:, component * levels + place], done
                ).start()
        pltpu.make_async_copy(in_ref, out_ref, done).wait()

    return pl.pallas_call(
        body,
        name="hand_on",
        in_specs=[pl.BlockSpec(memory_space=pltpu.SMEM), pl.BlockSpec(memory_space=pltpu.VMEM)],
        out_specs=pl.BlockSpec(memory_space=pl.ANY),
        out_shape=jax.ShapeDtypeStruct(value.shape, value.dtype),
        scratch_shapes=[pltpu.SemaphoreType.DMA],
        compiler_params=pltpu.CompilerParams(vmem_limit_bytes=4 << 20),
    )(field_order, value)


def on_device(grid_fields, field_order, wave_order):
    owners = lax.axis_size("belt") * lax.axis_size("lon")
    mode_count = wave_order.shape[0]
    slots = mode_count // owners
    levels = grid_fields.shape[0]
    waves = wave_order.astype(jnp.int32).reshape(mode_count // LANES, LANES)
    waves = pltpu.with_memory_space_constraint(waves, pltpu.HBM)
    spectral = analyse(grid_fields, waves).reshape(slots, 2 * levels, -1, LANES)
    lons = lax.axis_size("lon")
    spectral = hand_on(spectral, field_order.astype(jnp.int32), levels // lons, lons)
    spectral = spectral.reshape(slots, 2, levels, -1, 2, LANES)
    return jnp.swapaxes(spectral, 3, 4).reshape(slots, 2, levels, 2, mode_count // 2)


def solution(mesh):
    return jax.shard_map(
        on_device,
        mesh=mesh,
        in_specs=(P(None, "belt", "lon"), P(), P()),
        out_specs=P(("belt", "lon"), None, None, None, None),
        check_vma=False,
    )
```
